32 devices in a mesh: fsdp: 4 (over x, core), context: 4 (over z), tensor: 2 (over y).
Axes of the slice: x: 2, y: 2, z: 4, core: 2. Of those that a mesh axis runs over, the one named last changes fastest.
Arguments:
- tokens: bfloat16 [4, 2048, 2048], P('fsdp', 'context'), may hold values from -6 to 6
- segments: int32 [4, 2048], P('fsdp'), may hold values from 0 to 7, never falling along the last dimension, each value on 1 to 1024 neighbouring positions
- query_weight: bfloat16 [2048, 2048], P(('fsdp', 'context'), 'tensor'), may hold values from -0.125 to 0.125
- key_weight: bfloat16 [2048, 2048], P(('fsdp', 'context'), 'tensor'), may hold values from -0.125 to 0.125
- value_weight: bfloat16 [2048, 2048], P(('fsdp', 'context'), 'tensor'), may hold values from -0.125 to 0.125
- out_weight: bfloat16 [2048, 2048], P(('fsdp', 'context'), 'tensor'), may hold values from -0.375 to 0.375
- up_weight: bfloat16 [2048, 8192], P(('fsdp', 'context'), 'tensor'), may hold values from -0.125 to 0.125
- down_weight: bfloat16 [2048, 8192], P(('fsdp', 'context'), 'tensor'), may hold values from -0.0625 to 0.0625
- attn_gain: bfloat16 [2048], P(('fsdp', 'context')), may hold values from 0.5 to 1.5
- attn_bias: bfloat16 [2048], P(('fsdp', 'context')), may hold values from -1 to 1
- mlp_gain: bfloat16 [2048], P(('fsdp', 'context')), may hold values from 0.5 to 1.5
- mlp_bias: bfloat16 [2048], P(('fsdp', 'context')), may hold values from -1 to 1
- cotangent: bfloat16 [4, 2048, 2048], P('fsdp', 'context'), may hold values from -6 to 6
Outputs:
- output: bfloat16 [4, 2048, 2048], P('fsdp', 'context')
- tokens_grad: bfloat16 [4, 2048, 2048], P('fsdp', 'context')
- query_grad: float32 [2048, 2048], P(('fsdp', 'context'), 'tensor')
- key_grad: float32 [2048, 2048], P(('fsdp', 'context'), 'tensor')
- value_grad: float32 [2048, 2048], P(('fsdp', 'context'), 'tensor')
- out_grad: float32 [2048, 2048], P(('fsdp', 'context'), 'tensor')
- up_grad: float32 [2048, 8192], P(('fsdp', 'context'), 'tensor')
- down_grad: float32 [2048, 8192], P(('fsdp', 'context'), 'tensor')
- attn_gain_grad: float32 [2048], P(('fsdp', 'context'))
- attn_bias_grad: float32 [2048], P(('fsdp', 'context'))
- mlp_gain_grad: float32 [2048], P(('fsdp', 'context'))
- mlp_bias_grad: float32 [2048], P(('fsdp', 'context'))
The draws below stay inside these ranges and needn't reach their ends.
Inputs may be any that keep to these rules, and one draw needn't show every extreme that they name: `segments`: in each sequence the document numbers run from 0 to 7 without falling; every document has 1 to 1024 tokens and one has exactly 1024.
All inputs are finite; a program needn't handle non-finite values.
Results may differ from the reference program's by a relative error of at most 0.017.
Values may be sent and summed in bfloat16 or wider, within the bound.
A program may use at most 320 MiB of HBM per device.

```python
import math
import jax
import jax.numpy as jnp
import numpy as np
from jax import lax

D = 2048
HEADS = 16
HEAD = 128
FF = 8192
LEN = 2048
SEQS = 4
DOCS = 8
DOC_MOST = 1024


def block_scale(key, dims, pieces, smallest, high):
    gain = 1.0
    for position, parts in pieces:
        steps = jax.random.uniform(jax.random.fold_in(jax.random.fold_in(key, 6), position), (parts,), jnp.float32, smallest / len(pieces), high / len(pieces))
        gain = gain * jnp.repeat(jnp.exp(steps), dims[position] // parts).reshape((-1,) + (1,) * (len(dims) - 1 - position))
    return gain


def profile(count, total, most, slope):
    loads = [(1 << 20) // math.isqrt(rank ** slope) + 1 for rank in range(2, count + 1)]
    surplus, counts = total - most - (count - 1), [1] * (count - 1)
    while surplus > 0:
        movable = [i for i in range(count - 1) if counts[i] < most]
        whole, budget = sum([loads[i] for i in movable]), surplus
        for i in movable:
            more = min(most - counts[i], max(1, budget * loads[i] // whole), surplus)
            counts[i] = counts[i] + more
            surplus = surplus - more
    return np.array([most] + counts)


def uneven_parts(stream_key, amount, total, limit, slope):
    if amount == 2:
        one = jax.random.randint(stream_key, (), max(1, total - limit), min(limit, total - 1) + 1)
        return jnp.stack([one, total - one])
    lengths = jnp.asarray(profile(amount, total, limit, slope), jnp.int32)
    couples = (amount - 1) // 2
    source_of, taker = lengths[1:1 + 2 * couples:2], lengths[2:2 + 2 * couples:2]
    room = jnp.minimum(source_of - 1, limit - taker)
    shifted = jax.random.randint(jax.random.fold_in(stream_key, 1), (couples,), 0, 1 << 20) % (room + 1)
    lengths = lengths.at[1:1 + 2 * couples:2].set(source_of - shifted).at[2:2 + 2 * couples:2].set(taker + shifted)
    return lengths[jax.random.permutation(jax.random.fold_in(stream_key, 2), amount)]


def noise(own_key, dims, width, bound, cuts=(), held_as=jnp.bfloat16):
    gain = block_scale(own_key, dims, cuts, -0.22, 0.18) if cuts else 1.0
    values = jax.random.normal(own_key, dims, jnp.float32) * width * gain
    return jnp.minimum(jnp.maximum(values, -bound), bound).astype(held_as)


def setup_inputs(seed: int = 0) -> dict:
    seeds = jax.random.split(jax.random.key(seed), 14)
    tokens = noise(seeds[0], (SEQS, LEN, D), 1.0, 6.0, ((0, 4), (1, 4)))
    segments = jax.vmap(lambda own: jnp.searchsorted(jnp.cumsum(uneven_parts(own, DOCS, LEN, DOC_MOST, 2)), jnp.arange(LEN), side="right"))(jax.random.split(seeds[1], SEQS)).reshape((SEQS, LEN)).astype(jnp.int32)
    query_weight = noise(seeds[2], (D, D), D ** -0.5, 0.125, ((0, 16), (1, 2)))
    key_weight = noise(seeds[3], (D, D), D ** -0.5, 0.125, ((0, 16), (1, 2)))
    value_weight = noise(seeds[4], (D, D), D ** -0.5, 0.125, ((0, 16), (1, 2)))
    out_weight = noise(seeds[5], (D, D), (D // 8) ** -0.5, 0.375, ((0, 16), (1, 2)))
    up_weight = noise(seeds[6], (D, FF), D ** -0.5, 0.125, ((0, 16), (1, 2)))
    down_weight = noise(seeds[7], (D, FF), FF ** -0.5, 0.0625, ((0, 16), (1, 2)))
    attn_gain = jnp.clip(1.0 + 0.1 * jax.random.normal(seeds[8], (D,), jnp.float32), 0.5, 1.5).astype(jnp.bfloat16)
    attn_bias = noise(seeds[9], (D,), 0.2, 1.0, ((0, 16),))
    mlp_gain = jnp.clip(1.0 + 0.1 * jax.random.normal(seeds[10], (D,), jnp.float32), 0.5, 1.5).astype(jnp.bfloat16)
    mlp_bias = noise(seeds[11], (D,), 0.2, 1.0, ((0, 16),))
    cotangent = noise(seeds[12], (SEQS, LEN, D), 1.0, 6.0, ((0, 4), (1, 4)))
    return dict(tokens=tokens, segments=segments, query_weight=query_weight, key_weight=key_weight, value_weight=value_weight, out_weight=out_weight, up_weight=up_weight, down_weight=down_weight, attn_gain=attn_gain, attn_bias=attn_bias, mlp_gain=mlp_gain, mlp_bias=mlp_bias, cotangent=cotangent)


@jax.custom_vjp
def low(v):
    return lax.optimization_barrier(v.astype(jnp.bfloat16)).astype(jnp.float32)

@jax.custom_vjp
def low_back(v):
    return v

def low_keep(v):
    return (low(v), None)

def low_pass(kept, grad):
    return (grad,)

def back_keep(v):
    return (v, None)

def back_low(kept, grad):
    return (low(grad),)
low.defvjp(low_keep, low_pass)
low_back.defvjp(back_keep, back_low)
highest = lax.Precision.HIGHEST
epsilon = 1e-05
big_negative = -1e+30

def product(left, right):
    return jnp.dot(left, right, precision=highest)

def layer_norm(row_vals, gain_vals, bias_vals):
    average = lax.optimization_barrier(jnp.mean(row_vals, axis=-1, keepdims=True))
    centered = row_vals - average
    variance = lax.optimization_barrier(jnp.mean(centered * centered, axis=-1, keepdims=True))
    return centered * lax.rsqrt(variance + epsilon) * gain_vals + bias_vals

def one_sequence(tok_seq, seg_seq, params):
    query_weight, key_weight, value_weight, out_weight, up_weight, down_weight, attn_gain, attn_bias, mlp_gain, mlp_bias = params
    normed_one = low(layer_norm(tok_seq, attn_gain, attn_bias))
    query_rows = low_back(low(product(normed_one, query_weight))).reshape(LEN, HEADS, HEAD)
    key_rows = low_back(low(product(normed_one, key_weight))).reshape(LEN, HEADS, HEAD)
    value_rows = low_back(low(product(normed_one, value_weight))).reshape(LEN, HEADS, HEAD)
    positions = jnp.arange(LEN, dtype=jnp.int32)
    block_len = min(512, LEN)

    def query_block(block_index):
        first_row = block_index * block_len
        block_query = lax.dynamic_slice_in_dim(query_rows, first_row, block_len, 0)
        block_seg = lax.dynamic_slice_in_dim(seg_seq, first_row, block_len, 0)
        block_pos = first_row + jnp.arange(block_len, dtype=jnp.int32)
        scores = low_back(jnp.einsum('qhd,khd->hqk', block_query, key_rows, precision=highest) * HEAD ** (-0.5))
        allowed = (block_seg[:, None] == seg_seq[None, :]) & (block_pos[:, None] >= positions[None, :])
        masked = jnp.where(allowed[None], scores, big_negative)
        row_peak = lax.optimization_barrier(jnp.max(masked, axis=-1, keepdims=True))
        exp_terms = jnp.where(allowed[None], jnp.exp(masked - row_peak), 0.0)
        prob_rows = exp_terms / lax.optimization_barrier(jnp.sum(exp_terms, axis=-1, keepdims=True))
        return jnp.einsum('hqk,khd->qhd', low(prob_rows), value_rows, precision=highest)
    attended = lax.map(jax.checkpoint(query_block), jnp.arange(LEN // block_len, dtype=jnp.int32)).reshape(LEN, D)
    attn_out = low_back(low(attended))
    branch = low_back(product(attn_out, out_weight.T))
    residual = tok_seq + branch
    normed_two = low(layer_norm(residual, mlp_gain, mlp_bias))
    pre_act = low_back(product(normed_two, up_weight))
    activated = low(jax.nn.gelu(pre_act, approximate=False))
    return residual + product(activated, down_weight.T)

def reference(tokens, segments, query_weight, key_weight, value_weight, out_weight, up_weight, down_weight, attn_gain, attn_bias, mlp_gain, mlp_bias, cotangent):
    params = tuple((array_in.astype(jnp.float32) for array_in in (query_weight, key_weight, value_weight, out_weight, up_weight, down_weight, attn_gain, attn_bias, mlp_gain, mlp_bias)))

    def forward(tok_all, *weights):

        def per_sequence(seq_pair):
            return one_sequence(seq_pair[0], seq_pair[1], weights)
        return lax.map(jax.checkpoint(per_sequence), (tok_all, segments))
    output, pullback = jax.vjp(forward, tokens.astype(jnp.float32), *params)
    gradients = pullback(cotangent.astype(jnp.float32))
    return (output.astype(jnp.bfloat16), gradients[0].astype(jnp.bfloat16), gradients[1], gradients[2], gradients[3], gradients[4], gradients[5], gradients[6], gradients[7], gradients[8], gradients[9], gradients[10])
```

```python
import functools

import jax
import jax.numpy as jnp
from jax import lax
from jax.experimental import pallas as pl
from jax.experimental.pallas import tpu as pltpu
from jax.sharding import PartitionSpec as P

HEAD = 128

epsilon = 1e-05
big_negative = -1e30
density = 0.3989422804014327
half_root = 0.7071067811865476
bf16 = jnp.bfloat16
f32 = jnp.float32


def contract(left, right, left_dim, right_dim):
    return lax.dot_general(
        left, right, (((left_dim,), (right_dim,)), ((), ())), preferred_element_type=f32
    )


def norm_stats(row_vals):
    average = jnp.mean(row_vals, axis=-1, keepdims=True)
    centered = row_vals - average
    variance = jnp.mean(centered * centered, axis=-1, keepdims=True)
    inv_std = lax.rsqrt(variance + epsilon)
    return (centered * inv_std, inv_std)


def norm_back(grad_out, normed_hat, inv_std, gain_vals):
    scaled = grad_out * gain_vals
    first_mean = jnp.mean(scaled, axis=-1, keepdims=True)
    second_mean = jnp.mean(scaled * normed_hat, axis=-1, keepdims=True)
    return inv_std * (scaled - first_mean - normed_hat * second_mean)


def attn_forward_kernel(reach, factor, flags, *refs):
    seg_row, seg_cols, query, own_key, own_value = refs[:5]
    far = refs[5 : 5 + 2 * reach]
    out, log_sum, run_max, run_sum, run_acc = refs[5 + 2 * reach :]
    rows = query.shape[0]

    def block(key_ref, value_ref, index, first):
        scores = contract(key_ref[...], query[...], 1, 1) * factor
        allowed = seg_cols[index] == seg_row[...]
        if first:
            key_pos = lax.broadcasted_iota(jnp.int32, (rows, rows), 0)
            query_pos = lax.broadcasted_iota(jnp.int32, (rows, rows), 1)
            allowed = allowed & (key_pos <= query_pos)
        scores = jnp.where(allowed, scores, big_negative)
        peak = jnp.max(scores, axis=0, keepdims=True)
        if not first:
            peak = jnp.maximum(peak, run_max[...])
        terms = jnp.where(allowed, jnp.exp(scores - peak), 0.0)
        total = jnp.sum(terms, axis=0, keepdims=True)
        value_sum = contract(value_ref[...], terms.astype(bf16), 0, 0)
        if first:
            run_sum[...] = total
            run_acc[...] = value_sum
        else:
            shrink = jnp.exp(run_max[...] - peak)
            run_sum[...] = run_sum[...] * shrink + total
            run_acc[...] = run_acc[...] * shrink + value_sum
        run_max[...] = peak

    block(own_key, own_value, 0, True)
    for step in range(reach):

        @pl.when(flags[step] > 0)
        def _(step=step):
            block(far[2 * step], far[2 * step + 1], step + 1, False)

    out[...] = (run_acc[...] / run_sum[...]).T.astype(bf16)
    log_sum[0] = run_max[...] + jnp.log(run_sum[...])


def attn_backward_kernel(reach, factor, flags, *refs):
    seg_row, seg_cols, query, own_key, own_value, grad_out, attn_out, log_sum = refs[:8]
    far = refs[8 : 8 + 2 * reach]
    outs = refs[8 + 2 * reach :]
    grad_query, own_key_grad, own_value_grad = outs[:3]
    far_grads = outs[3 : 3 + 2 * reach]
    acc = outs[3 + 2 * reach]
    rows = query.shape[0]
    delta = jnp.sum(
        (grad_out[...].astype(f32) * attn_out[...].astype(f32)).T, axis=0, keepdims=True
    )

    def block(key_ref, value_ref, key_grad, value_grad, index, first):
        scores = contract(key_ref[...], query[...], 1, 1) * factor
        allowed = seg_cols[index] == seg_row[...]
        if first:
            key_pos = lax.broadcasted_iota(jnp.int32, (rows, rows), 0)
            query_pos = lax.broadcasted_iota(jnp.int32, (rows, rows), 1)
            allowed = allowed & (key_pos <= query_pos)
        probs = jnp.where(
            allowed, jnp.exp(jnp.where(allowed, scores, big_negative) - log_sum[0]), 0.0
        )
        grad_probs = contract(value_ref[...], grad_out[...], 1, 1)
        grad_scores = (probs * (grad_probs - delta)).astype(bf16)
        key_grad[...] = (
            jnp.dot(grad_scores, query[...], preferred_element_type=f32) * factor
        ).astype(bf16)
        value_grad[...] = jnp.dot(
            probs.astype(bf16), grad_out[...], preferred_element_type=f32
        ).astype(bf16)
        update = contract(key_ref[...], grad_scores, 0, 0)
        if first:
            acc[...] = update
        else:
            acc[...] += update

    block(own_key, own_value, own_key_grad, own_value_grad, 0, True)
    for step in range(reach):

        @pl.when(flags[step] > 0)
        def _(step=step):
            block(
                far[2 * step],
                far[2 * step + 1],
                far_grads[2 * step],
                far_grads[2 * step + 1],
                step + 1,
                False,
            )

        @pl.when(flags[step] == 0)
        def _(step=step):
            far_grads[2 * step][...] = jnp.zeros_like(far_grads[2 * step])
            far_grads[2 * step + 1][...] = jnp.zeros_like(far_grads[2 * step + 1])

    grad_query[...] = (acc[...] * factor).T.astype(bf16)


def head_spec(rows, first):
    return pl.BlockSpec((rows, HEAD), lambda h, flags, first=first: (0, first + h))


def attention_forward(flags, seg_row, seg_cols, qkv, far, heads):
    rows = qkv.shape[0]
    reach = len(far)
    in_specs = [
        pl.BlockSpec((1, rows), lambda h, flags: (0, 0)),
        pl.BlockSpec(seg_cols.shape, lambda h, flags: (0, 0, 0)),
        head_spec(rows, 0),
        head_spec(rows, heads),
        head_spec(rows, 2 * heads),
    ]
    operands = [seg_row, seg_cols, qkv, qkv, qkv]
    for piece in far:
        in_specs += [head_spec(rows, 0), head_spec(rows, heads)]
        operands += [piece, piece]
    pairs = heads * rows * rows * (reach + 1)
    return pl.pallas_call(
        functools.partial(attn_forward_kernel, reach, HEAD ** (-0.5)),
        out_shape=(
            jax.ShapeDtypeStruct((rows, heads * HEAD), bf16),
            jax.ShapeDtypeStruct((heads, 1, rows), f32),
        ),
        grid_spec=pltpu.PrefetchScalarGridSpec(
            num_scalar_prefetch=1,
            grid=(heads,),
            in_specs=in_specs,
            out_specs=(
                head_spec(rows, 0),
                pl.BlockSpec((1, 1, rows), lambda h, flags: (h, 0, 0)),
            ),
            scratch_shapes=[
                pltpu.VMEM((1, rows), f32),
                pltpu.VMEM((1, rows), f32),
                pltpu.VMEM((HEAD, rows), f32),
            ],
        ),
        cost_estimate=pl.CostEstimate(
            flops=4 * HEAD * pairs, transcendentals=pairs, bytes_accessed=16 * rows * heads * HEAD
        ),
        name="attention_forward",
    )(flags, *operands)


def attention_backward(flags, seg_row, seg_cols, qkv, far, grad_out, attn_out, log_sum, heads):
    rows = qkv.shape[0]
    reach = len(far)
    in_specs = [
        pl.BlockSpec((1, rows), lambda h, flags: (0, 0)),
        pl.BlockSpec(seg_cols.shape, lambda h, flags: (0, 0, 0)),
        head_spec(rows, 0),
        head_spec(rows, heads),
        head_spec(rows, 2 * heads),
        head_spec(rows, 0),
        head_spec(rows, 0),
        pl.BlockSpec((1, 1, rows), lambda h, flags: (h, 0, 0)),
    ]
    operands = [seg_row, seg_cols, qkv, qkv, qkv, grad_out, attn_out, log_sum]
    for piece in far:
        in_specs += [head_spec(rows, 0), head_spec(rows, heads)]
        operands += [piece, piece]
    pairs = heads * rows * rows * (reach + 1)
    out = jax.ShapeDtypeStruct((rows, heads * HEAD), bf16)
    return pl.pallas_call(
        functools.partial(attn_backward_kernel, reach, HEAD ** (-0.5)),
        out_shape=(out,) * (3 + 2 * reach),
        grid_spec=pltpu.PrefetchScalarGridSpec(
            num_scalar_prefetch=1,
            grid=(heads,),
            in_specs=in_specs,
            out_specs=(head_spec(rows, 0),) * (3 + 2 * reach),
            scratch_shapes=[pltpu.VMEM((HEAD, rows), f32)],
        ),
        cost_estimate=pl.CostEstimate(
            flops=10 * HEAD * pairs, transcendentals=pairs, bytes_accessed=32 * rows * heads * HEAD
        ),
        name="attention_backward",
    )(flags, *operands)


def swap(array, axis, size):
    return lax.ppermute(array, axis, [(i, i ^ 1) for i in range(size)])


def line_move(array, axis, size, step):
    moves = [(i, i + step) for i in range(size) if 0 <= i + step < size]
    return lax.ppermute(array, axis, moves)


def direct_sum(own, axis, size, me):
    total = own(me)
    for step in range(1, size):
        target = lax.rem(me + step, size)
        moves = [(i, (i + step) % size) for i in range(size)]
        total = total + lax.ppermute(own(target).astype(bf16), axis, moves).astype(f32)
    return total


def tensor_sum(part, size):
    part = part.astype(bf16)
    if size == 2:
        return part.astype(f32) + swap(part, "tensor", 2).astype(f32)
    return lax.psum(part, "tensor").astype(f32)


def grad_scatter(part, sizes):
    fsdp, context = sizes["fsdp"], sizes["context"]
    chips = fsdp // 2
    mine = lax.axis_index("fsdp")
    core, chip = lax.rem(mine, 2), lax.div(mine, 2)
    place = lax.axis_index("context")

    def both_cores(target):
        sent = part(2 * target + 1 - core).astype(bf16)
        return part(2 * target + core) + swap(sent, "fsdp", fsdp).astype(f32)

    rows = both_cores(chip)
    for step in range(1, chips):
        sent = both_cores(lax.rem(chip + step, chips)).astype(bf16)
        moves = [(i, (i + 2 * step) % fsdp) for i in range(fsdp)]
        rows = rows + lax.ppermute(sent, "fsdp", moves).astype(f32)
    rows = rows.astype(bf16)
    count = rows.shape[0] // context
    return direct_sum(
        lambda t: lax.dynamic_slice_in_dim(rows, t * count, count, 0).astype(f32),
        "context",
        context,
        place,
    )


def product_scatter(left, right, sizes):
    block = left.shape[1] // sizes["fsdp"]

    def part(index):
        return contract(lax.dynamic_slice_in_dim(left, index * block, block, 1), right, 0, 0)

    return grad_scatter(part, sizes)


def vector_scatter(rows, sizes):
    fsdp, context = sizes["fsdp"], sizes["context"]
    if sizes["tensor"] == 2:
        rows = rows + swap(rows, "tensor", 2)
    else:
        rows = lax.psum(rows, "tensor")
    count = rows.shape[1] // (fsdp * context)
    mine, place = lax.axis_index("fsdp"), lax.axis_index("context")
    width = context * count

    def shift_sum(total, axis, size, me, width):
        own = lambda t: lax.dynamic_slice_in_dim(total, t * width, width, 1)
        result = own(me)
        for step in range(1, size):
            moves = [(i, (i + step) % size) for i in range(size)]
            result = result + lax.ppermute(own(lax.rem(me + step, size)), axis, moves)
        return result

    rows = shift_sum(rows, "fsdp", fsdp, mine, width)
    return shift_sum(rows, "context", context, place, count)


def per_device(
    sizes,
    tokens,
    segments,
    query_weight,
    key_weight,
    value_weight,
    out_weight,
    up_weight,
    down_weight,
    attn_gain,
    attn_bias,
    mlp_gain,
    mlp_bias,
    cotangent,
):
    seq_dev, group_len, model_width = tokens.shape
    assert seq_dev == 1
    shard_rows, local_width = query_weight.shape
    hidden_local = up_weight.shape[1]
    heads = local_width // HEAD
    seq_len = segments.shape[1]
    context, tensor = sizes["context"], sizes["tensor"]
    place = lax.axis_index("context")
    weight_axes = ("fsdp", "context")

    vectors = jnp.stack([attn_gain, attn_bias, mlp_gain, mlp_bias], axis=1)
    vectors = jnp.pad(vectors, ((0, 0), (0, HEAD - 4)))
    attn_full = lax.all_gather(
        jnp.concatenate([query_weight, key_weight, value_weight, out_weight, vectors], axis=1),
        weight_axes,
        axis=0,
        tiled=True,
    )
    mlp_full = lax.all_gather(
        jnp.concatenate([up_weight, down_weight], axis=1), weight_axes, axis=0, tiled=True
    )
    full_qkv = attn_full[:, : 3 * local_width]
    full_out = attn_full[:, 3 * local_width : 4 * local_width]
    vecs = attn_full[:, 4 * local_width : 4 * local_width + 4].T.astype(f32)
    gain_one, bias_one, gain_two, bias_two = vecs[0], vecs[1], vecs[2], vecs[3]
    full_up = mlp_full[:, :hidden_local]
    full_down = mlp_full[:, hidden_local:]

    rows_in = tokens.reshape(group_len, model_width).astype(f32)
    hat_one, inv_one = norm_stats(rows_in)
    normed_one = (hat_one * gain_one + bias_one).astype(bf16)
    qkv = jnp.dot(normed_one, full_qkv, preferred_element_type=f32).astype(bf16)

    reach = min(context - 1, -(-(seq_len // 2 - 1) // group_len))
    far = []
    piece = qkv[:, local_width:]
    for _ in range(reach):
        piece = line_move(piece, "context", context, 1)
        far.append(piece)
    first = place * group_len
    seg_row = lax.dynamic_slice_in_dim(segments, first, group_len, 1)
    seg_cols = [seg_row]
    for back in range(1, reach + 1):
        start = jnp.maximum(first - back * group_len, 0)
        block = lax.dynamic_slice_in_dim(segments, start, group_len, 1)
        seg_cols.append(jnp.where(place >= back, block, -1))
    flags = jnp.stack([(cols[0, -1] == seg_row[0, 0]).astype(jnp.int32) for cols in seg_cols[1:]])
    seg_cols = jnp.concatenate(seg_cols, axis=0)[:, :, None]

    attn, log_sum = attention_forward(flags, seg_row, seg_cols, qkv, far, heads)
    residual = rows_in + tensor_sum(contract(attn, full_out, 1, 1), tensor)

    hat_two, inv_two = norm_stats(residual)
    normed_two = (hat_two * gain_two + bias_two).astype(bf16)
    pre_act = jnp.dot(normed_two, full_up, preferred_element_type=f32)
    normal_cdf = 0.5 * (1.0 + lax.erf(pre_act * half_root))
    activated = (pre_act * normal_cdf).astype(bf16)
    slope = normal_cdf + pre_act * density * jnp.exp(-0.5 * pre_act * pre_act)
    grad_rows = cotangent.reshape(group_len, model_width)
    grad_act = jnp.dot(grad_rows, full_down, preferred_element_type=f32)
    grad_pre = (grad_act * slope).astype(bf16)
    norm_two_part = contract(grad_pre, full_up, 1, 1).astype(bf16)
    grad_norm_two = tensor_sum(norm_two_part, tensor)

    down_grad = product_scatter(grad_rows, activated, sizes)
    up_grad = product_scatter(normed_two, grad_pre, sizes)
    mlp_out = tensor_sum(contract(activated, full_down, 1, 1), tensor)
    output = (residual + mlp_out).astype(bf16).reshape(tokens.shape)

    grad_resid = grad_rows.astype(f32) + norm_back(grad_norm_two, hat_two, inv_two, gain_two)
    grad_branch = grad_resid.astype(bf16)
    grad_attn = jnp.dot(grad_branch, full_out, preferred_element_type=f32).astype(bf16)
    out_grad = product_scatter(grad_branch, attn, sizes)

    results = attention_backward(
        flags, seg_row, seg_cols, qkv, far, grad_attn, attn, log_sum, heads
    )
    query_bf = results[0]
    query_grad = product_scatter(normed_one, query_bf, sizes)
    carry = None
    for back in range(reach, -1, -1):
        term = jnp.concatenate(results[1 + 2 * back : 3 + 2 * back], axis=1)
        if carry is not None:
            term = (term.astype(f32) + carry.astype(f32)).astype(bf16)
        if back > 0:
            carry = line_move(term, "context", context, -1)
    pair_bf = term
    pair_grad = product_scatter(normed_one, pair_bf, sizes)
    input_part = contract(query_bf, full_qkv[:, :local_width], 1, 1) + contract(
        pair_bf, full_qkv[:, local_width:], 1, 1
    )
    norm_one_part = input_part.astype(bf16)
    grad_norm_one = tensor_sum(norm_one_part, tensor)
    tokens_grad = (
        (grad_resid + norm_back(grad_norm_one, hat_one, inv_one, gain_one))
        .astype(bf16)
        .reshape(tokens.shape)
    )
    one_f, two_f = norm_one_part.astype(f32), norm_two_part.astype(f32)
    vector_sums = jnp.stack(
        [
            jnp.sum(one_f * hat_one, axis=0),
            jnp.sum(one_f, axis=0),
            jnp.sum(two_f * hat_two, axis=0),
            jnp.sum(two_f, axis=0),
        ],
        axis=0,
    )
    vector_grads = vector_scatter(vector_sums, sizes)
    return (
        output,
        tokens_grad,
        query_grad,
        pair_grad[:, :local_width],
        pair_grad[:, local_width:],
        out_grad,
        up_grad,
        down_grad,
        vector_grads[0],
        vector_grads[1],
        vector_grads[2],
        vector_grads[3],
    )


def solution(mesh):
    weight = P(("fsdp", "context"), "tensor")
    vector = P(("fsdp", "context"))
    rows = P("fsdp", "context", None)
    return jax.shard_map(
        functools.partial(per_device, dict(mesh.shape)),
        mesh=mesh,
        in_specs=(rows, P("fsdp", None)) + (weight,) * 6 + (vector,) * 4 + (rows,),
        out_specs=(rows, rows) + (weight,) * 6 + (vector,) * 4,
        check_vma=False,
    )
```

```python
import functools

import jax
import jax.numpy as jnp
from jax import lax
from jax.experimental import pallas as pl
from jax.experimental.pallas import tpu as pltpu
from jax.sharding import PartitionSpec as P

HEAD = 128

epsilon = 1e-05
big_negative = -1e30
density = 0.3989422804014327
half_root = 0.7071067811865476
bf16 = jnp.bfloat16
f32 = jnp.float32
MESH = pl.DeviceIdType.MESH
WIDTH = 256


def contract(left, right, left_dim, right_dim):
    return lax.dot_general(
        left, right, (((left_dim,), (right_dim,)), ((), ())), preferred_element_type=f32
    )


def norm_stats(row_vals):
    average = jnp.mean(row_vals, axis=-1, keepdims=True)
    centered = row_vals - average
    variance = jnp.mean(centered * centered, axis=-1, keepdims=True)
    inv_std = lax.rsqrt(variance + epsilon)
    return (centered * inv_std, inv_std)


def norm_back(grad_out, normed_hat, inv_std, gain_vals):
    scaled = grad_out * gain_vals
    first_mean = jnp.mean(scaled, axis=-1, keepdims=True)
    second_mean = jnp.mean(scaled * normed_hat, axis=-1, keepdims=True)
    return inv_std * (scaled - first_mean - normed_hat * second_mean)


def attn_forward_kernel(reach, factor, flags, *refs):
    seg_row, seg_cols, query, own_key, own_value = refs[:5]
    far = refs[5 : 5 + 2 * reach]
    out, log_sum, run_max, run_sum, run_acc = refs[5 + 2 * reach :]
    rows = query.shape[0]

    def block(key_ref, value_ref, index, first):
        scores = contract(key_ref[...], query[...], 1, 1) * factor
        allowed = seg_cols[index] == seg_row[...]
        if first:
            key_pos = lax.broadcasted_iota(jnp.int32, (rows, rows), 0)
            query_pos = lax.broadcasted_iota(jnp.int32, (rows, rows), 1)
            allowed = allowed & (key_pos <= query_pos)
        scores = jnp.where(allowed, scores, big_negative)
        peak = jnp.max(scores, axis=0, keepdims=True)
        if not first:
            peak = jnp.maximum(peak, run_max[...])
        terms = jnp.where(allowed, jnp.exp(scores - peak), 0.0)
        total = jnp.sum(terms, axis=0, keepdims=True)
        value_sum = contract(value_ref[...], terms.astype(bf16), 0, 0)
        if first:
            run_sum[...] = total
            run_acc[...] = value_sum
        else:
            shrink = jnp.exp(run_max[...] - peak)
            run_sum[...] = run_sum[...] * shrink + total
            run_acc[...] = run_acc[...] * shrink + value_sum
        run_max[...] = peak

    block(own_key, own_value, 0, True)
    for step in range(reach):

        @pl.when(flags[step] > 0)
        def _(step=step):
            block(far[2 * step], far[2 * step + 1], step + 1, False)

    out[...] = (run_acc[...] / run_sum[...]).T.astype(bf16)
    log_sum[0] = run_max[...] + jnp.log(run_sum[...])


def attn_backward_kernel(reach, factor, flags, *refs):
    seg_row, seg_cols, query, own_key, own_value, grad_out, attn_out, log_sum = refs[:8]
    far = refs[8 : 8 + 2 * reach]
    outs = refs[8 + 2 * reach :]
    grad_query, own_key_grad, own_value_grad = outs[:3]
    far_grads = outs[3 : 3 + 2 * reach]
    acc = outs[3 + 2 * reach]
    rows = query.shape[0]
    delta = jnp.sum(
        (grad_out[...].astype(f32) * attn_out[...].astype(f32)).T, axis=0, keepdims=True
    )

    def block(key_ref, value_ref, key_grad, value_grad, index, first):
        scores = contract(key_ref[...], query[...], 1, 1) * factor
        allowed = seg_cols[index] == seg_row[...]
        if first:
            key_pos = lax.broadcasted_iota(jnp.int32, (rows, rows), 0)
            query_pos = lax.broadcasted_iota(jnp.int32, (rows, rows), 1)
            allowed = allowed & (key_pos <= query_pos)
        probs = jnp.where(
            allowed, jnp.exp(jnp.where(allowed, scores, big_negative) - log_sum[0]), 0.0
        )
        grad_probs = contract(value_ref[...], grad_out[...], 1, 1)
        grad_scores = (probs * (grad_probs - delta)).astype(bf16)
        key_grad[...] = (
            jnp.dot(grad_scores, query[...], preferred_element_type=f32) * factor
        ).astype(bf16)
        value_grad[...] = jnp.dot(
            probs.astype(bf16), grad_out[...], preferred_element_type=f32
        ).astype(bf16)
        update = contract(key_ref[...], grad_scores, 0, 0)
        if first:
            acc[...] = update
        else:
            acc[...] += update

    block(own_key, own_value, own_key_grad, own_value_grad, 0, True)
    for step in range(reach):

        @pl.when(flags[step] > 0)
        def _(step=step):
            block(
                far[2 * step],
                far[2 * step + 1],
                far_grads[2 * step],
                far_grads[2 * step + 1],
                step + 1,
                False,
            )

        @pl.when(flags[step] == 0)
        def _(step=step):
            far_grads[2 * step][...] = jnp.zeros_like(far_grads[2 * step])
            far_grads[2 * step + 1][...] = jnp.zeros_like(far_grads[2 * step + 1])

    grad_query[...] = (acc[...] * factor).T.astype(bf16)


def head_spec(rows, first):
    return pl.BlockSpec((rows, HEAD), lambda h, flags, first=first: (0, first + h))


def attention_forward(flags, seg_row, seg_cols, qkv, far, heads):
    rows = qkv.shape[0]
    reach = len(far)
    in_specs = [
        pl.BlockSpec((1, rows), lambda h, flags: (0, 0)),
        pl.BlockSpec(seg_cols.shape, lambda h, flags: (0, 0, 0)),
        head_spec(rows, 0),
        head_spec(rows, heads),
        head_spec(rows, 2 * heads),
    ]
    operands = [seg_row, seg_cols, qkv, qkv, qkv]
    for piece in far:
        in_specs += [head_spec(rows, 0), head_spec(rows, heads)]
        operands += [piece, piece]
    pairs = heads * rows * rows * (reach + 1)
    return pl.pallas_call(
        functools.partial(attn_forward_kernel, reach, HEAD ** (-0.5)),
        out_shape=(
            jax.ShapeDtypeStruct((rows, heads * HEAD), bf16),
            jax.ShapeDtypeStruct((heads, 1, rows), f32),
        ),
        grid_spec=pltpu.PrefetchScalarGridSpec(
            num_scalar_prefetch=1,
            grid=(heads,),
            in_specs=in_specs,
            out_specs=(
                head_spec(rows, 0),
                pl.BlockSpec((1, 1, rows), lambda h, flags: (h, 0, 0)),
            ),
            scratch_shapes=[
                pltpu.VMEM((1, rows), f32),
                pltpu.VMEM((1, rows), f32),
                pltpu.VMEM((HEAD, rows), f32),
            ],
        ),
        cost_estimate=pl.CostEstimate(
            flops=4 * HEAD * pairs, transcendentals=pairs, bytes_accessed=16 * rows * heads * HEAD
        ),
        name="attention_forward",
    )(flags, *operands)


def attention_backward(flags, seg_row, seg_cols, qkv, far, grad_out, attn_out, log_sum, heads):
    rows = qkv.shape[0]
    reach = len(far)
    in_specs = [
        pl.BlockSpec((1, rows), lambda h, flags: (0, 0)),
        pl.BlockSpec(seg_cols.shape, lambda h, flags: (0, 0, 0)),
        head_spec(rows, 0),
        head_spec(rows, heads),
        head_spec(rows, 2 * heads),
        head_spec(rows, 0),
        head_spec(rows, 0),
        pl.BlockSpec((1, 1, rows), lambda h, flags: (h, 0, 0)),
    ]
    operands = [seg_row, seg_cols, qkv, qkv, qkv, grad_out, attn_out, log_sum]
    for piece in far:
        in_specs += [head_spec(rows, 0), head_spec(rows, heads)]
        operands += [piece, piece]
    pairs = heads * rows * rows * (reach + 1)
    out = jax.ShapeDtypeStruct((rows, heads * HEAD), bf16)
    return pl.pallas_call(
        functools.partial(attn_backward_kernel, reach, HEAD ** (-0.5)),
        out_shape=(out,) * (3 + 2 * reach),
        grid_spec=pltpu.PrefetchScalarGridSpec(
            num_scalar_prefetch=1,
            grid=(heads,),
            in_specs=in_specs,
            out_specs=(head_spec(rows, 0),) * (3 + 2 * reach),
            scratch_shapes=[pltpu.VMEM((HEAD, rows), f32)],
        ),
        cost_estimate=pl.CostEstimate(
            flops=10 * HEAD * pairs, transcendentals=pairs, bytes_accessed=32 * rows * heads * HEAD
        ),
        name="attention_backward",
    )(flags, *operands)


def swap(array, axis, size):
    return lax.ppermute(array, axis, [(i, i ^ 1) for i in range(size)])


def line_move(array, axis, size, step):
    moves = [(i, i + step) for i in range(size) if 0 <= i + step < size]
    return lax.ppermute(array, axis, moves)


def tensor_other(part, size):
    if size == 2:
        return swap(part, "tensor", 2)
    return lax.psum(part, "tensor") - part


def after(value, *others):
    return lax.optimization_barrier((value,) + others)[0]


def reduce_kernel(sizes, width, pairs, left_count, right_count, *refs):
    lefts, refs = refs[:left_count], refs[left_count:]
    rights, refs = refs[:right_count], refs[right_count:]
    outs, refs = refs[: len(pairs)], refs[len(pairs) :]
    (core_send, core_recv, chip_send, chip_recv, line_send, line_recv, own, keep) = refs[:8]
    (core_sems, chip_sems, line_sems, core_free, chip_free, line_free) = refs[8:]
    fsdp, context = sizes["fsdp"], sizes["context"]
    chips = fsdp // 2
    mine, place = lax.axis_index("fsdp"), lax.axis_index("context")
    core, chip = lax.rem(mine, 2), lax.div(mine, 2)
    rows = lefts[0].shape[0] // fsdp
    piece = rows // context
    starts, total = [], 0
    for pair in pairs:
        starts.append(total)
        total += pair[3]

    sibling = {"fsdp": mine + 1 - 2 * core}
    chip_to = [{"fsdp": lax.rem(mine + 2 * k, fsdp)} for k in range(chips)]
    chip_from = [{"fsdp": lax.rem(mine + fsdp - 2 * k, fsdp)} for k in range(chips)]
    line_to = [{"context": lax.rem(place + k, context)} for k in range(context)]
    line_from = [{"context": lax.rem(place + context - k, context)} for k in range(context)]

    barrier = pltpu.get_barrier_semaphore()
    for peer in [sibling] + chip_to[1:] + line_to[1:]:
        pl.semaphore_signal(barrier, inc=1, device_id=peer, device_id_type=MESH)
    pl.semaphore_wait(barrier, 1 + (chips - 1) + (context - 1))

    def remote(source, target, sems, peer):
        return pltpu.make_async_remote_copy(
            src_ref=source,
            dst_ref=target,
            send_sem=sems[0],
            recv_sem=sems[1],
            device_id=peer,
            device_id_type=MESH,
        )

    def core_copy(t):
        slot = lax.rem(t, 2)
        sems = (core_sems.at[0, slot], core_sems.at[1, slot])
        return remote(core_send.at[slot], core_recv.at[slot], sems, sibling)

    def chip_copy(t, k):
        slot = lax.rem(t, 2)
        sems = (chip_sems.at[0, slot, k - 1], chip_sems.at[1, slot, k - 1])
        return remote(
            chip_send.at[slot, k - 1], chip_recv.at[slot, k - 1], sems, chip_to[k]
        )

    def line_copy(t, k):
        slot = lax.rem(t, 3)
        sems = (line_sems.at[0, slot, k - 1], line_sems.at[1, slot, k - 1])
        target = lax.rem(place + k, context)
        return remote(line_send.at[slot, target], line_recv.at[slot, k - 1], sems, line_to[k])

    def give(sem, peer):
        pl.semaphore_signal(sem, inc=1, device_id=peer, device_id_type=MESH)

    def each_pair(t, body):
        for index, (left, right, first, count) in enumerate(pairs):

            @pl.when((t >= starts[index]) & (t < starts[index] + count))
            def _(index=index, left=left, right=right, first=first):
                column = pl.multiple_of((first + t - starts[index]) * width, width)

                def part(block):
                    start = pl.multiple_of(block * rows, rows)
                    if left < 0:
                        return rights[right][pl.ds(start, rows), pl.ds(column, width)]
                    return jnp.dot(
                        lefts[left][pl.ds(start, rows), :],
                        rights[right][:, pl.ds(column, width)],
                        preferred_element_type=f32,
                    )

                body(part)

    def first_stage(t):
        slot = lax.rem(t, 2)

        @pl.when(t >= 2)
        def _():
            core_copy(t - 2).wait_send()

        def body(part):
            for j in range(chips):
                core_send[slot, j] = part(2 * j + 1 - core).astype(bf16)

        each_pair(t, body)

        @pl.when(t >= 2)
        def _():
            pl.semaphore_wait(core_free, 1)

        core_copy(t).start()

    def second_stage(t):
        slot = lax.rem(t, 2)
        core_copy(t).wait_recv()

        @pl.when(t >= 2)
        def _():
            for k in range(1, chips):
                chip_copy(t - 2, k).wait_send()

        def body(part):
            for k in list(range(1, chips)) + [0]:
                target = lax.rem(chip + k, chips)
                both = part(2 * target + core) + core_recv[slot, target].astype(f32)
                if k:
                    chip_send[slot, k - 1] = both.astype(bf16)
                else:
                    own[slot] = both

        each_pair(t, body)

        @pl.when(t <= total - 3)
        def _():
            give(core_free, sibling)

        for k in range(1, chips):

            @pl.when(t >= 2)
            def _(k=k):
                pl.semaphore_wait(chip_free.at[k - 1], 1)

            chip_copy(t, k).start()

    def third_stage(t):
        slot, place_slot = lax.rem(t, 2), lax.rem(t, 3)
        value = own[slot]
        for k in range(1, chips):
            chip_copy(t, k).wait_recv()
            value = value + chip_recv[slot, k - 1].astype(f32)

        @pl.when(t >= 3)
        def _():
            for k in range(1, context):
                line_copy(t - 3, k).wait_send()

        for p in range(context):
            line_send[place_slot, p] = value[p * piece : (p + 1) * piece].astype(bf16)

            @pl.when(place == p)
            def _(p=p):
                keep[place_slot] = value[p * piece : (p + 1) * piece]

        @pl.when(t <= total - 3)
        def _():
            for k in range(1, chips):
                give(chip_free.at[k - 1], chip_from[k])

        for k in range(1, context):

            @pl.when(t >= 3)
            def _(k=k):
                pl.semaphore_wait(line_free.at[k - 1], 1)

            line_copy(t, k).start()

    def last_stage(t):
        slot = lax.rem(t, 3)
        value = keep[slot]
        for k in range(1, context):
            line_copy(t, k).wait_recv()
            value = value + line_recv[slot, k - 1].astype(f32)

        @pl.when(t <= total - 4)
        def _():
            for k in range(1, context):
                give(line_free.at[k - 1], line_from[k])

        for index, pair in enumerate(pairs):

            @pl.when((t >= starts[index]) & (t < starts[index] + pair[3]))
            def _(index=index):
                column = pl.multiple_of((t - starts[index]) * width, width)
                outs[index][:, pl.ds(column, width)] = value

    def step(s, carry):
        for lag, stage in ((0, first_stage), (1, second_stage), (2, third_stage), (4, last_stage)):

            @pl.when((s >= lag) & (s < total + lag))
            def _(lag=lag, stage=stage):
                stage(s - lag)

        return carry

    lax.fori_loop(0, total + 4, step, 0)
    for t in range(total - 2, total):
        core_copy(t).wait_send()
        for k in range(1, chips):
            chip_copy(t, k).wait_send()
    for t in range(total - 3, total):
        for k in range(1, context):
            line_copy(t, k).wait_send()


def reduce_products(lefts, rights, pairs, sizes, width, number):
    fsdp, context = sizes["fsdp"], sizes["context"]
    chips = fsdp // 2
    depth, count = lefts[0].shape
    rows = depth // fsdp
    piece = rows // context
    chunks = tuple((a, b, first // width, n // width) for a, b, first, n in pairs)
    columns = sum(pair[3] for pair in pairs)
    vmem = pl.BlockSpec(memory_space=pltpu.VMEM)
    dma, regular = pltpu.SemaphoreType.DMA, pltpu.SemaphoreType.REGULAR
    return pl.pallas_call(
        functools.partial(reduce_kernel, sizes, width, chunks, len(lefts), len(rights)),
        out_shape=tuple(jax.ShapeDtypeStruct((piece, pair[3]), f32) for pair in pairs),
        in_specs=[vmem] * (len(lefts) + len(rights)),
        out_specs=(vmem,) * len(pairs),
        scratch_shapes=[
            pltpu.VMEM((2, chips, rows, width), bf16),
            pltpu.VMEM((2, chips, rows, width), bf16),
            pltpu.VMEM((2, chips - 1, rows, width), bf16),
            pltpu.VMEM((2, chips - 1, rows, width), bf16),
            pltpu.VMEM((3, context, piece, width), bf16),
            pltpu.VMEM((3, context - 1, piece, width), bf16),
            pltpu.VMEM((2, rows, width), f32),
            pltpu.VMEM((3, piece, width), f32),
            dma((2, 2)),
            dma((2, 2, chips - 1)),
            dma((2, 3, context - 1)),
            regular,
            regular((chips - 1,)),
            regular((context - 1,)),
        ],
        compiler_params=pltpu.CompilerParams(collective_id=number, has_side_effects=True),
        cost_estimate=pl.CostEstimate(
            flops=2 * depth * count * columns * 4,
            transcendentals=0,
            bytes_accessed=2 * (depth * len(lefts) + columns) * count + 4 * piece * columns,
        ),
        name=f"reduce_products_{number}",
    )(*lefts, *rights)


def per_device(
    sizes,
    tokens,
    segments,
    query_weight,
    key_weight,
    value_weight,
    out_weight,
    up_weight,
    down_weight,
    attn_gain,
    attn_bias,
    mlp_gain,
    mlp_bias,
    cotangent,
):
    seq_dev, group_len, model_width = tokens.shape
    assert seq_dev == 1
    shard_rows, local_width = query_weight.shape
    hidden_local = up_weight.shape[1]
    heads = local_width // HEAD
    seq_len = segments.shape[1]
    context, tensor = sizes["context"], sizes["tensor"]
    place = lax.axis_index("context")
    weight_axes = ("fsdp", "context")

    vectors = jnp.stack([attn_gain, attn_bias, mlp_gain, mlp_bias], axis=1)
    vectors = jnp.pad(vectors, ((0, 0), (0, HEAD - 4)))
    attn_full = lax.all_gather(
        jnp.concatenate([query_weight, key_weight, value_weight, out_weight, vectors], axis=1),
        weight_axes,
        axis=0,
        tiled=True,
    )
    mlp_full = lax.all_gather(
        jnp.concatenate([up_weight, down_weight], axis=1), weight_axes, axis=0, tiled=True
    )
    full_qkv = attn_full[:, : 3 * local_width]
    full_out = attn_full[:, 3 * local_width : 4 * local_width]
    vecs = attn_full[:, 4 * local_width : 4 * local_width + 4].T.astype(f32)
    gain_one, bias_one, gain_two, bias_two = vecs[0], vecs[1], vecs[2], vecs[3]
    full_up = mlp_full[:, :hidden_local]
    full_down = mlp_full[:, hidden_local:]

    rows_in = tokens.reshape(group_len, model_width).astype(f32)
    hat_one, inv_one = norm_stats(rows_in)
    normed_one = (hat_one * gain_one + bias_one).astype(bf16)
    qkv = jnp.dot(normed_one, full_qkv, preferred_element_type=f32).astype(bf16)

    reach = min(context - 1, -(-(seq_len // 2 - 1) // group_len))
    far = []
    piece = qkv[:, local_width:]
    for _ in range(reach):
        piece = line_move(piece, "context", context, 1)
        far.append(piece)
    first = place * group_len
    seg_row = lax.dynamic_slice_in_dim(segments, first, group_len, 1)
    seg_cols = [seg_row]
    for back in range(1, reach + 1):
        start = jnp.maximum(first - back * group_len, 0)
        block = lax.dynamic_slice_in_dim(segments, start, group_len, 1)
        seg_cols.append(jnp.where(place >= back, block, -1))
    flags = jnp.stack([(cols[0, -1] == seg_row[0, 0]).astype(jnp.int32) for cols in seg_cols[1:]])
    seg_cols = jnp.concatenate(seg_cols, axis=0)[:, :, None]

    attn, log_sum = attention_forward(flags, seg_row, seg_cols, qkv, far, heads)
    branch = contract(attn, full_out, 1, 1).astype(bf16)
    residual = rows_in + (branch.astype(f32) + tensor_other(branch, tensor).astype(f32))

    hat_two, inv_two = norm_stats(residual)
    normed_two = (hat_two * gain_two + bias_two).astype(bf16)
    pre_act = jnp.dot(normed_two, full_up, preferred_element_type=f32)
    normal_cdf = 0.5 * (1.0 + lax.erf(pre_act * half_root))
    activated = (pre_act * normal_cdf).astype(bf16)
    slope = normal_cdf + pre_act * density * jnp.exp(-0.5 * pre_act * pre_act)
    grad_rows = cotangent.reshape(group_len, model_width)
    grad_act = jnp.dot(grad_rows, full_down, preferred_element_type=f32)
    grad_pre = (grad_act * slope).astype(bf16)
    norm_two_part = contract(grad_pre, full_up, 1, 1).astype(bf16)
    norm_two_other = tensor_other(norm_two_part, tensor)
    mlp_part = contract(after(activated, norm_two_part), full_down, 1, 1).astype(bf16)
    mlp_other = tensor_other(mlp_part, tensor)

    (down_grad,) = reduce_products(
        (grad_rows.T,),
        (after(activated, mlp_part, norm_two_part),),
        ((0, 0, 0, hidden_local),),
        sizes,
        WIDTH,
        1,
    )
    norm_two_other = after(norm_two_other, down_grad)
    mlp_other = after(mlp_other, down_grad)
    mlp_out = mlp_part.astype(f32) + mlp_other.astype(f32)
    output = (residual + mlp_out).astype(bf16).reshape(tokens.shape)

    grad_norm_two = norm_two_part.astype(f32) + norm_two_other.astype(f32)
    grad_resid = grad_rows.astype(f32) + norm_back(grad_norm_two, hat_two, inv_two, gain_two)
    grad_branch = grad_resid.astype(bf16)
    grad_attn = jnp.dot(grad_branch, full_out, preferred_element_type=f32).astype(bf16)
    results = attention_backward(
        flags, seg_row, seg_cols, qkv, far, grad_attn, attn, log_sum, heads
    )
    query_bf = results[0]

    half = hidden_local // 2
    up_left, out_left = normed_two.T, grad_branch.T

    def first_work(tied):
        return reduce_products(
            (up_left,), (after(grad_pre, tied),), ((0, 0, 0, half),), sizes, WIDTH, 2
        )

    def second_work(tied):
        return reduce_products(
            (up_left, out_left),
            (after(grad_pre, tied), attn),
            ((0, 0, half, half), (1, 1, 0, local_width)),
            sizes,
            WIDTH,
            3,
        )

    works, done = [first_work, second_work], []
    carry = None
    for back in range(reach, -1, -1):
        term = jnp.concatenate(results[1 + 2 * back : 3 + 2 * back], axis=1)
        if carry is not None:
            term = (term.astype(f32) + carry.astype(f32)).astype(bf16)
        if back > 0:
            carry = line_move(term, "context", context, -1)
            if works:
                done.append(works.pop(0)(term))
                carry = after(carry, done[-1][0])
    pair_bf = term
    for work in works:
        done.append(work(pair_bf))
    up_grad = jnp.concatenate([done[0][0], done[1][0]], axis=1)
    out_grad = done[1][1]

    input_part = contract(query_bf, full_qkv[:, :local_width], 1, 1) + contract(
        pair_bf, full_qkv[:, local_width:], 1, 1
    )
    norm_one_part = input_part.astype(bf16)
    norm_one_other = tensor_other(norm_one_part, tensor)
    one_f, two_f = norm_one_part.astype(f32), norm_two_part.astype(f32)
    vector_sums = jnp.stack(
        [
            jnp.sum(one_f * hat_one, axis=0),
            jnp.sum(one_f, axis=0),
            jnp.sum(two_f * hat_two, axis=0),
            jnp.sum(two_f, axis=0),
        ],
        axis=0,
    )
    vector_sums = jnp.pad(vector_sums, ((0, WIDTH - 4), (0, 0))).T
    query_grad, key_grad, value_grad, vector_part = reduce_products(
        (normed_one.T,),
        (query_bf, pair_bf, vector_sums),
        (
            (0, 0, 0, local_width),
            (0, 1, 0, local_width),
            (0, 1, local_width, local_width),
            (-1, 2, 0, WIDTH),
        ),
        sizes,
        WIDTH,
        4,
    )
    norm_one_other = after(norm_one_other, query_grad)
    grad_norm_one = norm_one_part.astype(f32) + norm_one_other.astype(f32)
    tokens_grad = (
        (grad_resid + norm_back(grad_norm_one, hat_one, inv_one, gain_one))
        .astype(bf16)
        .reshape(tokens.shape)
    )
    vector_part = vector_part[:, :8]
    vector_grads = (vector_part + tensor_other(vector_part, tensor)).T
    return (
        output,
        tokens_grad,
        query_grad,
        key_grad,
        value_grad,
        out_grad,
        up_grad,
        down_grad,
        vector_grads[0],
        vector_grads[1],
        vector_grads[2],
        vector_grads[3],
    )


def solution(mesh):
    weight = P(("fsdp", "context"), "tensor")
    vector = P(("fsdp", "context"))
    rows = P("fsdp", "context", None)
    return jax.shard_map(
        functools.partial(per_device, dict(mesh.shape)),
        mesh=mesh,
        in_specs=(rows, P("fsdp", None)) + (weight,) * 6 + (vector,) * 4 + (rows,),
        out_specs=(rows, rows) + (weight,) * 6 + (vector,) * 4,
        check_vma=False,
    )
```

```python
import functools

import jax
import jax.numpy as jnp
from jax import lax
from jax.experimental import pallas as pl
from jax.experimental.pallas import tpu as pltpu
from jax.sharding import PartitionSpec as P

HEAD = 128

epsilon = 1e-05
big_negative = -1e30
density = 0.3989422804014327
half_root = 0.7071067811865476
bf16 = jnp.bfloat16
f32 = jnp.float32
MESH = pl.DeviceIdType.MESH
WIDTH = 256


def contract(left, right, left_dim, right_dim):
    return lax.dot_general(
        left, right, (((left_dim,), (right_dim,)), ((), ())), preferred_element_type=f32
    )


def norm_stats(row_vals):
    average = jnp.mean(row_vals, axis=-1, keepdims=True)
    centered = row_vals - average
    variance = jnp.mean(centered * centered, axis=-1, keepdims=True)
    inv_std = lax.rsqrt(variance + epsilon)
    return (centered * inv_std, inv_std)


def norm_back(grad_out, normed_hat, inv_std, gain_vals):
    scaled = grad_out * gain_vals
    first_mean = jnp.mean(scaled, axis=-1, keepdims=True)
    second_mean = jnp.mean(scaled * normed_hat, axis=-1, keepdims=True)
    return inv_std * (scaled - first_mean - normed_hat * second_mean)


def attn_forward_kernel(reach, factor, flags, *refs):
    seg_row, seg_cols, query, own_key, own_value = refs[:5]
    far = refs[5 : 5 + 2 * reach]
    out, log_sum, run_max, run_sum, run_acc = refs[5 + 2 * reach :]
    rows = query.shape[0]

    def block(key_ref, value_ref, index, first):
        scores = contract(key_ref[...], query[...], 1, 1) * factor
        allowed = seg_cols[index] == seg_row[...]
        if first:
            key_pos = lax.broadcasted_iota(jnp.int32, (rows, rows), 0)
            query_pos = lax.broadcasted_iota(jnp.int32, (rows, rows), 1)
            allowed = allowed & (key_pos <= query_pos)
        scores = jnp.where(allowed, scores, big_negative)
        peak = jnp.max(scores, axis=0, keepdims=True)
        if not first:
            peak = jnp.maximum(peak, run_max[...])
        terms = jnp.where(allowed, jnp.exp(scores - peak), 0.0)
        total = jnp.sum(terms, axis=0, keepdims=True)
        value_sum = contract(value_ref[...], terms.astype(bf16), 0, 0)
        if first:
            run_sum[...] = total
            run_acc[...] = value_sum
        else:
            shrink = jnp.exp(run_max[...] - peak)
            run_sum[...] = run_sum[...] * shrink + total
            run_acc[...] = run_acc[...] * shrink + value_sum
        run_max[...] = peak

    block(own_key, own_value, 0, True)
    for step in range(reach):

        @pl.when(flags[step] > 0)
        def _(step=step):
            block(far[2 * step], far[2 * step + 1], step + 1, False)

    out[...] = (run_acc[...] / run_sum[...]).T.astype(bf16)
    log_sum[0] = run_max[...] + jnp.log(run_sum[...])


def attn_backward_kernel(reach, factor, flags, *refs):
    seg_row, seg_cols, query, own_key, own_value, grad_out, attn_out, log_sum = refs[:8]
    far = refs[8 : 8 + 2 * reach]
    outs = refs[8 + 2 * reach :]
    grad_query, own_pair_grad = outs[:2]
    far_grads = outs[2 : 2 + reach]
    acc = outs[2 + reach]
    rows = query.shape[0]
    delta = jnp.sum(
        (grad_out[...].astype(f32) * attn_out[...].astype(f32)).T, axis=0, keepdims=True
    )

    def block(key_ref, value_ref, pair_grad, index, first):
        scores = contract(key_ref[...], query[...], 1, 1) * factor
        allowed = seg_cols[index] == seg_row[...]
        if first:
            key_pos = lax.broadcasted_iota(jnp.int32, (rows, rows), 0)
            query_pos = lax.broadcasted_iota(jnp.int32, (rows, rows), 1)
            allowed = allowed & (key_pos <= query_pos)
        probs = jnp.where(
            allowed, jnp.exp(jnp.where(allowed, scores, big_negative) - log_sum[0]), 0.0
        )
        grad_probs = contract(value_ref[...], grad_out[...], 1, 1)
        grad_scores = (probs * (grad_probs - delta)).astype(bf16)
        pair_grad[:, :HEAD] = (
            jnp.dot(grad_scores, query[...], preferred_element_type=f32) * factor
        ).astype(bf16)
        pair_grad[:, HEAD:] = jnp.dot(
            probs.astype(bf16), grad_out[...], preferred_element_type=f32
        ).astype(bf16)
        update = contract(key_ref[...], grad_scores, 0, 0)
        if first:
            acc[...] = update
        else:
            acc[...] += update

    block(own_key, own_value, own_pair_grad, 0, True)
    for step in range(reach):

        @pl.when(flags[step] > 0)
        def _(step=step):
            block(far[2 * step], far[2 * step + 1], far_grads[step], step + 1, False)

        @pl.when(flags[step] == 0)
        def _(step=step):
            far_grads[step][...] = jnp.zeros_like(far_grads[step])

    grad_query[...] = (acc[...] * factor).T.astype(bf16)


def head_spec(rows, first, stride=1):
    return pl.BlockSpec((rows, HEAD), lambda h, flags: (0, first + stride * h))


def attention_forward(flags, seg_row, seg_cols, qkv, far, heads):
    rows = qkv.shape[0]
    reach = len(far)
    in_specs = [
        pl.BlockSpec((1, rows), lambda h, flags: (0, 0)),
        pl.BlockSpec(seg_cols.shape, lambda h, flags: (0, 0, 0)),
        head_spec(rows, 0),
        head_spec(rows, heads, 2),
        head_spec(rows, heads + 1, 2),
    ]
    operands = [seg_row, seg_cols, qkv, qkv, qkv]
    for piece in far:
        in_specs += [head_spec(rows, 0, 2), head_spec(rows, 1, 2)]
        operands += [piece, piece]
    pairs = heads * rows * rows * (reach + 1)
    return pl.pallas_call(
        functools.partial(attn_forward_kernel, reach, HEAD ** (-0.5)),
        out_shape=(
            jax.ShapeDtypeStruct((rows, heads * HEAD), bf16),
            jax.ShapeDtypeStruct((heads, 1, rows), f32),
        ),
        grid_spec=pltpu.PrefetchScalarGridSpec(
            num_scalar_prefetch=1,
            grid=(heads,),
            in_specs=in_specs,
            out_specs=(
                head_spec(rows, 0),
                pl.BlockSpec((1, 1, rows), lambda h, flags: (h, 0, 0)),
            ),
            scratch_shapes=[
                pltpu.VMEM((1, rows), f32),
                pltpu.VMEM((1, rows), f32),
                pltpu.VMEM((HEAD, rows), f32),
            ],
        ),
        cost_estimate=pl.CostEstimate(
            flops=4 * HEAD * pairs, transcendentals=pairs, bytes_accessed=16 * rows * heads * HEAD
        ),
        name="attention_forward",
    )(flags, *operands)


def attention_backward(flags, seg_row, seg_cols, qkv, far, grad_out, attn_out, log_sum, heads):
    rows = qkv.shape[0]
    reach = len(far)
    in_specs = [
        pl.BlockSpec((1, rows), lambda h, flags: (0, 0)),
        pl.BlockSpec(seg_cols.shape, lambda h, flags: (0, 0, 0)),
        head_spec(rows, 0),
        head_spec(rows, heads, 2),
        head_spec(rows, heads + 1, 2),
        head_spec(rows, 0),
        head_spec(rows, 0),
        pl.BlockSpec((1, 1, rows), lambda h, flags: (h, 0, 0)),
    ]
    operands = [seg_row, seg_cols, qkv, qkv, qkv, grad_out, attn_out, log_sum]
    for piece in far:
        in_specs += [head_spec(rows, 0, 2), head_spec(rows, 1, 2)]
        operands += [piece, piece]
    pairs = heads * rows * rows * (reach + 1)
    pair_spec = pl.BlockSpec((rows, 2 * HEAD), lambda h, flags: (0, h))
    pair_out = jax.ShapeDtypeStruct((rows, 2 * heads * HEAD), bf16)
    return pl.pallas_call(
        functools.partial(attn_backward_kernel, reach, HEAD ** (-0.5)),
        out_shape=(jax.ShapeDtypeStruct((rows, heads * HEAD), bf16),) + (pair_out,) * (1 + reach),
        grid_spec=pltpu.PrefetchScalarGridSpec(
            num_scalar_prefetch=1,
            grid=(heads,),
            in_specs=in_specs,
            out_specs=(head_spec(rows, 0),) + (pair_spec,) * (1 + reach),
            scratch_shapes=[pltpu.VMEM((HEAD, rows), f32)],
        ),
        cost_estimate=pl.CostEstimate(
            flops=10 * HEAD * pairs, transcendentals=pairs, bytes_accessed=32 * rows * heads * HEAD
        ),
        name="attention_backward",
    )(flags, *operands)


def swap(array, axis, size):
    return lax.ppermute(array, axis, [(i, i ^ 1) for i in range(size)])


def line_move(array, axis, size, step):
    moves = [(i, i + step) for i in range(size) if 0 <= i + step < size]
    return lax.ppermute(array, axis, moves)


def tensor_other(part, size):
    if size == 2:
        return swap(part, "tensor", 2)
    return lax.psum(part, "tensor") - part


def after(value, *others):
    return lax.optimization_barrier((value,) + others)[0]


def remote(source, target, sems, peer):
    return pltpu.make_async_remote_copy(
        src_ref=source,
        dst_ref=target,
        send_sem=sems[0],
        recv_sem=sems[1],
        device_id=peer,
        device_id_type=MESH,
    )


def give(sem, peer):
    pl.semaphore_signal(sem, inc=1, device_id=peer, device_id_type=MESH)


def reduce_loop(sizes, width, depth, pairs, outs, scratch, others=(), extra=None):
    fsdp, context = sizes["fsdp"], sizes["context"]
    levels = context.bit_length() - 1
    (core_send, core_recv, chip_send, chip_recv, own) = scratch[:5]
    (core_sems, chip_sems, line_sems, core_free, chip_free, line_free) = scratch[5:11]
    line_send = scratch[11 : 11 + levels]
    line_recv = scratch[11 + levels : 11 + 2 * levels]
    line_keep = scratch[11 + 2 * levels : 11 + 3 * levels]
    chips = fsdp // 2
    mine, place = lax.axis_index("fsdp"), lax.axis_index("context")
    core, chip = lax.rem(mine, 2), lax.div(mine, 2)
    rows = depth // fsdp
    piece = rows // context
    starts, total = [], 0
    for pair in pairs:
        starts.append(total)
        total += pair[1]

    sibling = {"fsdp": mine + 1 - 2 * core}
    chip_to = [{"fsdp": lax.rem(mine + 2 * k, fsdp)} for k in range(chips)]
    chip_from = [{"fsdp": lax.rem(mine + fsdp - 2 * k, fsdp)} for k in range(chips)]
    bits = [lax.rem(lax.div(place, 1 << level), 2) for level in range(levels)]
    partners = [
        {"context": place + (1 - 2 * bits[level]) * (1 << level)} for level in range(levels)
    ]

    barrier = pltpu.get_barrier_semaphore()
    peers = [sibling] + chip_to[1:] + partners + list(others)
    for peer in peers:
        pl.semaphore_signal(barrier, inc=1, device_id=peer, device_id_type=MESH)
    pl.semaphore_wait(barrier, len(peers))

    def core_copy(t):
        slot = lax.rem(t, 2)
        sems = (core_sems.at[0, slot], core_sems.at[1, slot])
        return remote(core_send.at[slot], core_recv.at[slot], sems, sibling)

    def chip_copy(t, k):
        slot = lax.rem(t, 2)
        sems = (chip_sems.at[0, slot, k - 1], chip_sems.at[1, slot, k - 1])
        return remote(chip_send.at[slot, k - 1], chip_recv.at[slot, k - 1], sems, chip_to[k])

    def line_copy(t, level):
        slot = lax.rem(t, 3)
        sems = (line_sems.at[0, slot, level], line_sems.at[1, slot, level])
        source = line_send[level].at[slot, 1 - bits[level]]
        return remote(source, line_recv[level].at[slot], sems, partners[level])

    def line_out(t, level, value):
        slot = lax.rem(t, 3)

        @pl.when(t >= 3)
        def _():
            line_copy(t - 3, level).wait_send()

        for i in range(context >> level):
            line_send[level][slot, i % 2, i // 2] = value(i).astype(bf16)

            @pl.when(bits[level] == i % 2)
            def _(i=i):
                line_keep[level][slot, i // 2] = value(i)

        @pl.when(t >= 3)
        def _():
            pl.semaphore_wait(line_free.at[level], 1)

        line_copy(t, level).start()

    def each_pair(t, body):
        for start, (part, count, _) in zip(starts, pairs):

            @pl.when((t >= start) & (t < start + count))
            def _(start=start, part=part):
                body(lambda block: part(t - start, pl.multiple_of(block * rows, rows), rows))

    def first_stage(t):
        slot = lax.rem(t, 2)

        @pl.when(t >= 2)
        def _():
            core_copy(t - 2).wait_send()

        def body(part):
            for j in range(chips):
                core_send[slot, j] = part(2 * j + 1 - core).astype(bf16)

        each_pair(t, body)

        @pl.when(t >= 2)
        def _():
            pl.semaphore_wait(core_free, 1)

        core_copy(t).start()

    def second_stage(t):
        slot = lax.rem(t, 2)
        core_copy(t).wait_recv()

        @pl.when(t >= 2)
        def _():
            for k in range(1, chips):
                chip_copy(t - 2, k).wait_send()

        def body(part):
            for k in list(range(1, chips)) + [0]:
                target = lax.rem(chip + k, chips)
                both = part(2 * target + core) + core_recv[slot, target].astype(f32)
                if k:
                    chip_send[slot, k - 1] = both.astype(bf16)
                else:
                    own[slot] = both

        each_pair(t, body)

        @pl.when(t <= total - 3)
        def _():
            give(core_free, sibling)

        for k in range(1, chips):

            @pl.when(t >= 2)
            def _(k=k):
                pl.semaphore_wait(chip_free.at[k - 1], 1)

            chip_copy(t, k).start()

    def third_stage(t):
        slot = lax.rem(t, 2)
        value = own[slot]
        for k in range(1, chips):
            chip_copy(t, k).wait_recv()
            value = value + chip_recv[slot, k - 1].astype(f32)
        line_out(t, 0, lambda i: value[i * piece : (i + 1) * piece])

        @pl.when(t <= total - 3)
        def _():
            for k in range(1, chips):
                give(chip_free.at[k - 1], chip_from[k])

    def line_stage(t, level):
        slot = lax.rem(t, 3)
        line_copy(t, level).wait_recv()

        def value(i):
            return line_keep[level][slot, i] + line_recv[level][slot, i].astype(f32)

        if level + 1 < levels:
            line_out(t, level + 1, value)
        else:
            result = value(0)
            for start, (_, count, numbers) in zip(starts, pairs):

                @pl.when((t >= start) & (t < start + count))
                def _(start=start, numbers=numbers):
                    span = width // len(numbers)
                    column = pl.multiple_of((t - start) * span, span)
                    for index, number in enumerate(numbers):
                        outs[number][:, pl.ds(column, span)] = result[
                            :, index * span : (index + 1) * span
                        ]

        @pl.when(t <= total - 4)
        def _():
            give(line_free.at[level], partners[level])

    stages = [(0, first_stage), (1, second_stage), (2, third_stage)] + [
        (4 + 2 * level, functools.partial(line_stage, level=level)) for level in range(levels)
    ]

    def step(s, carry):
        for lag, stage in stages:

            @pl.when((s >= lag) & (s < total + lag))
            def _(lag=lag, stage=stage):
                stage(s - lag)

        if extra is not None:
            extra(s)
        return carry

    lax.fori_loop(0, total + 2 + 2 * levels, step, 0)
    for t in range(total - 2, total):
        core_copy(t).wait_send()
        for k in range(1, chips):
            chip_copy(t, k).wait_send()
    for t in range(total - 3, total):
        for level in range(levels):
            line_copy(t, level).wait_send()


def reduce_scratch(sizes, width, depth):
    fsdp, context = sizes["fsdp"], sizes["context"]
    chips = fsdp // 2
    rows = depth // fsdp
    piece = rows // context
    levels = context.bit_length() - 1
    assert context == 1 << levels
    dma, regular = pltpu.SemaphoreType.DMA, pltpu.SemaphoreType.REGULAR
    halves = [context >> (level + 1) for level in range(levels)]
    return (
        [
            pltpu.VMEM((2, chips, rows, width), bf16),
            pltpu.VMEM((2, chips, rows, width), bf16),
            pltpu.VMEM((2, chips - 1, rows, width), bf16),
            pltpu.VMEM((2, chips - 1, rows, width), bf16),
            pltpu.VMEM((2, rows, width), f32),
            dma((2, 2)),
            dma((2, 2, chips - 1)),
            dma((2, 3, levels)),
            regular,
            regular((chips - 1,)),
            regular((levels,)),
        ]
        + [pltpu.VMEM((3, 2, n, piece, width), bf16) for n in halves]
        + [pltpu.VMEM((3, n, piece, width), bf16) for n in halves]
        + [pltpu.VMEM((3, n, piece, width), f32) for n in halves]
    )


def product_part(left, right, first, width):
    def part(chunk, row, rows):
        column = pl.multiple_of((first + chunk) * width, width)
        return jnp.dot(
            left[pl.ds(row, rows), :], right[:, pl.ds(column, width)], preferred_element_type=f32
        )

    return part


def column_sums(first, second, row, width):
    first = jnp.sum(first, axis=0, keepdims=True)
    second = jnp.sum(second, axis=0, keepdims=True)
    line = lax.broadcasted_iota(jnp.int32, (128, width), 0)
    return jnp.where(line == row, first, jnp.where(line == row + 1, second, 0.0)).T


def middle_kernel(sizes, width, *refs):
    row_left, act, grad_pre, resid, rows, average, inverse, gain, weights, attn_full = refs[:10]
    down_grad, output, grad_resid, out_left, vec_two, grad_attn = refs[10:16]
    held, held_out, part_send, part_recv, means, acc = refs[16:22]
    held_sems, out_sem, part_sems = refs[22:25]
    scratch = refs[25:]
    depth, count = row_left.shape
    hidden = act.shape[1]
    local_width = grad_attn.shape[1]
    blocks = depth // width
    other = {"tensor": 1 - lax.axis_index("tensor")}
    pairs = [(product_part(row_left, act, 0, width), hidden // width, (0,))]
    total = hidden // width

    def held_copy(b):
        row = pl.multiple_of(lax.rem(b, blocks) * width, width)
        column = pl.multiple_of(lax.div(b, blocks) * hidden, hidden)
        slot = lax.rem(b, 2)
        return pltpu.make_async_copy(
            weights.at[pl.ds(row, width), pl.ds(column, hidden)], held.at[slot], held_sems.at[slot]
        )

    def out_copy():
        source = attn_full.at[:, pl.ds(3 * local_width, local_width)]
        return pltpu.make_async_copy(source, held_out, out_sem)

    def part_copy(b):
        sems = (part_sems.at[0, b], part_sems.at[1, b])
        return remote(part_send.at[b], part_recv.at[b], sems, other)

    def at(b):
        return pl.ds(pl.multiple_of(b * width, width), width)

    def normed_hat(b):
        return (resid[:, at(b)] - average[...]) * inverse[...]

    def send_block(b, left):
        held_copy(b).wait()
        rounded = contract(left[...], held[lax.rem(b, 2)], 1, 1).astype(bf16)
        part_send[b] = rounded
        part_copy(b).start()

        @pl.when(b + 2 < 2 * blocks)
        def _():
            held_copy(b + 2).start()

        return rounded.astype(f32)

    def norm_block(b):
        rounded = send_block(b, grad_pre)
        vec_two[at(b), :] = column_sums(rounded * normed_hat(b), rounded, 2, width)

    def both(b):
        return part_send[b].astype(f32) + part_recv[b].astype(f32)

    def norm_means():
        def add(b, sums):
            part_copy(b).wait_recv()
            scaled = both(b) * gain[:, at(b)]
            first = jnp.sum(scaled, axis=1, keepdims=True)
            second = jnp.sum(scaled * normed_hat(b), axis=1, keepdims=True)
            return (sums[0] + first, sums[1] + second)

        zero = jnp.zeros((count, 1), f32)
        first, second = lax.fori_loop(0, blocks, add, (zero, zero))
        means[0] = first * (1.0 / depth)
        means[1] = second * (1.0 / depth)

    def norm_result(b):
        back = both(b) * gain[:, at(b)] - means[0] - normed_hat(b) * means[1]
        result = rows[:, at(b)].astype(f32) + inverse[...] * back
        grad_resid[:, at(b)] = result
        out_left[at(b), :] = result.T.astype(bf16)
        update = jnp.dot(result.astype(bf16), held_out[at(b), :], preferred_element_type=f32)

        @pl.when(b == 0)
        def _():
            acc[...] = update

        @pl.when(b > 0)
        def _():
            acc[...] += update

        @pl.when(b == blocks - 1)
        def _():
            grad_attn[...] = acc[...].astype(bf16)

    def output_block(b):
        part_copy(blocks + b).wait_recv()
        output[:, at(b)] = (resid[:, at(b)] + both(blocks + b)).astype(bf16)

    def during(s, first, body):
        @pl.when((s >= first) & (s < first + blocks))
        def _():
            body(s - first)

    def extra(s):
        @pl.when(s == 0)
        def _():
            held_copy(0).start()
            held_copy(1).start()
            out_copy().start()

        during(s, 1, norm_block)
        during(s, 1 + blocks, lambda b: send_block(blocks + b, act))

        @pl.when(s == blocks + 3)
        def _():
            norm_means()
            out_copy().wait()

        during(s, blocks + 4, norm_result)
        during(s, blocks + 5, output_block)

    assert 2 * blocks <= total
    reduce_loop(sizes, width, depth, pairs, [down_grad], scratch, (other,), extra)
    for b in range(2 * blocks):
        part_copy(b).wait_send()


def backward_middle(left, act, grad_pre, resid, rows, norm, weights, attn_full, sizes, width, number):
    depth, count = left.shape
    hidden = act.shape[1]
    local_width = attn_full.shape[1] // HEAD // 4 * HEAD
    piece = depth // (sizes["fsdp"] * sizes["context"])
    blocks = depth // width
    vmem = pl.BlockSpec(memory_space=pltpu.VMEM)
    far = pl.BlockSpec(memory_space=pl.ANY)
    dma = pltpu.SemaphoreType.DMA
    return pl.pallas_call(
        functools.partial(middle_kernel, sizes, width),
        out_shape=(
            jax.ShapeDtypeStruct((piece, hidden), f32),
            jax.ShapeDtypeStruct((count, depth), bf16),
            jax.ShapeDtypeStruct((count, depth), f32),
            jax.ShapeDtypeStruct((depth, count), bf16),
            jax.ShapeDtypeStruct((depth, 128), f32),
            jax.ShapeDtypeStruct((count, local_width), bf16),
        ),
        in_specs=[vmem] * 8 + [far] * 2,
        out_specs=(vmem,) * 6,
        scratch_shapes=[
            pltpu.VMEM((2, width, hidden), bf16),
            pltpu.VMEM((depth, local_width), bf16),
            pltpu.VMEM((2 * blocks, count, width), bf16),
            pltpu.VMEM((2 * blocks, count, width), bf16),
            pltpu.VMEM((2, count, 1), f32),
            pltpu.VMEM((count, local_width), f32),
            dma((2,)),
            dma,
            dma((2, 2 * blocks)),
        ]
        + reduce_scratch(sizes, width, depth),
        compiler_params=pltpu.CompilerParams(
            collective_id=number, has_side_effects=True, vmem_limit_bytes=62 * 1024 * 1024
        ),
        cost_estimate=pl.CostEstimate(
            flops=12 * depth * count * hidden,
            transcendentals=0,
            bytes_accessed=4 * depth * hidden,
        ),
        name="backward_middle",
    )(left, act, grad_pre, resid, rows, *norm, weights, attn_full)


def tail_kernel(sizes, width, reach, *refs):
    up_left, out_left, one_left, grad_pre, attn, query, weights = refs[:7]
    tokens, average, inverse, gain, grad_resid, vec_two = refs[7:13]
    terms = refs[13 : 14 + reach]
    refs = refs[14 + reach :]
    outs, tokens_grad = refs[:6], refs[6]
    pair, hop_recv, carry, held, part_send, part_recv, vec_one, means = refs[7:15]
    hop_sems, hop_free, held_sems, part_sems = refs[15:19]
    scratch = refs[19:]
    context = sizes["context"]
    place = lax.axis_index("context")
    depth, count = up_left.shape
    local_width = query.shape[1]
    blocks = depth // width
    lower = {"context": lax.rem(place + context - 1, context)}
    upper = {"context": lax.rem(place + 1, context)}
    other = {"tensor": 1 - lax.axis_index("tensor")}

    def vec_part(chunk, row, rows):
        both = vec_one[pl.ds(row, rows), :] + vec_two[pl.ds(row, rows), :]
        return jnp.concatenate([both] * (width // both.shape[1]), axis=1)

    pairs = [
        (product_part(up_left, grad_pre, 0, width), grad_pre.shape[1] // width, (0,)),
        (product_part(out_left, attn, 0, width), local_width // width, (1,)),
        (product_part(one_left, query, 0, width), local_width // width, (2,)),
        (product_part(one_left, pair, 0, width), 2 * local_width // width, (3, 4)),
        (vec_part, 1, (5,)),
    ]
    total = sum(p[1] for p in pairs)
    begin = sum(p[1] for p in pairs[:3])
    hop_steps = [h * (begin - 2) // max(reach, 1) for h in range(reach + 1)]

    def hop_copy(h):
        source = terms[reach] if h == 0 else carry.at[h % carry.shape[0]]
        sems = (hop_sems.at[0, h], hop_sems.at[1, h])
        return remote(source, hop_recv.at[h % 2], sems, lower)

    def hop(h):
        term = terms[reach - h]
        target = pair if h == reach else carry.at[h % carry.shape[0]]
        if h > carry.shape[0] and h < reach:

            @pl.when(place > 0)
            def _():
                hop_copy(h - carry.shape[0]).wait_send()

        if h > 0:

            @pl.when(place < context - 1)
            def _():
                hop_copy(h - 1).wait_recv()

                def add(i, c):
                    at = pl.ds(pl.multiple_of(i * 64, 64), 64)
                    got = hop_recv[(h - 1) % 2, at, :].astype(f32)
                    target[at, :] = (term[at, :].astype(f32) + got).astype(bf16)
                    return c

                lax.fori_loop(0, count // 64, add, 0)
                if h + 1 < reach:
                    give(hop_free, upper)

            @pl.when(place == context - 1)
            def _():
                target[...] = term[...]

        elif reach == 0:
            pair[...] = term[...]
        if h < reach:

            @pl.when(place > 0)
            def _():
                if h >= 2:
                    pl.semaphore_wait(hop_free, 1)
                hop_copy(h).start()

    def held_copy(b):
        slot = lax.rem(b, 2)
        row = pl.multiple_of(b * width, width)
        return pltpu.make_async_copy(
            weights.at[pl.ds(row, width), pl.ds(0, 3 * local_width)],
            held.at[slot],
            held_sems.at[slot],
        )

    def part_copy(b):
        sems = (part_sems.at[0, b], part_sems.at[1, b])
        return remote(part_send.at[b], part_recv.at[b], sems, other)

    def normed_hat(b):
        columns = pl.ds(pl.multiple_of(b * width, width), width)
        return (tokens[:, columns].astype(f32) - average[...]) * inverse[...]

    def input_block(b):
        slot = lax.rem(b, 2)
        held_copy(b).wait()
        value = contract(query[...], held[slot, :, :local_width], 1, 1)
        value = value + contract(pair[...], held[slot, :, local_width:], 1, 1)
        rounded = value.astype(bf16)
        part_send[b] = rounded
        part_copy(b).start()

        @pl.when(b + 2 < blocks)
        def _():
            held_copy(b + 2).start()

        rounded = rounded.astype(f32)
        vec_one[pl.ds(pl.multiple_of(b * width, width), width), :] = column_sums(
            rounded * normed_hat(b), rounded, 0, width
        )

    def scaled_block(b):
        columns = pl.ds(pl.multiple_of(b * width, width), width)
        value = part_send[b].astype(f32) + part_recv[b].astype(f32)
        return value * gain[:, columns]

    def norm_means():
        def add(b, sums):
            part_copy(b).wait_recv()
            scaled = scaled_block(b)
            first = jnp.sum(scaled, axis=1, keepdims=True)
            second = jnp.sum(scaled * normed_hat(b), axis=1, keepdims=True)
            return (sums[0] + first, sums[1] + second)

        zero = jnp.zeros((count, 1), f32)
        first, second = lax.fori_loop(0, blocks, add, (zero, zero))
        means[0] = first * (1.0 / depth)
        means[1] = second * (1.0 / depth)

    def norm_result():
        def write(b, c):
            columns = pl.ds(pl.multiple_of(b * width, width), width)
            back = scaled_block(b) - means[0] - normed_hat(b) * means[1]
            tokens_grad[:, columns] = (
                grad_resid[:, columns] + inverse[...] * back
            ).astype(bf16)
            return c

        lax.fori_loop(0, blocks, write, 0)

    def extra(s):
        for h in range(reach + 1):

            @pl.when(s == hop_steps[h])
            def _(h=h):
                hop(h)

        @pl.when(s == begin - 2)
        def _():
            held_copy(0).start()
            held_copy(1).start()

        @pl.when((s >= begin) & (s < begin + blocks))
        def _():
            input_block(s - begin)

        @pl.when(s == total + 1)
        def _():
            norm_means()

        @pl.when(s == total + 2)
        def _():
            norm_result()

    assert begin + blocks < total
    reduce_loop(sizes, width, depth, pairs, outs, scratch, (other, lower, upper), extra)

    @pl.when(place > 0)
    def _():
        for h in range(reach):
            if h == 0 or h >= reach - carry.shape[0]:
                hop_copy(h).wait_send()

    for b in range(blocks):
        part_copy(b).wait_send()


def backward_tail(
    lefts, grad_pre, attn, query, weights, norm, grad_resid, vec_two, terms, sizes, width, number
):
    depth, count = lefts[0].shape
    local_width = query.shape[1]
    hidden = grad_pre.shape[1]
    reach = len(terms) - 1
    piece = depth // (sizes["fsdp"] * sizes["context"])
    blocks = depth // width
    vmem = pl.BlockSpec(memory_space=pltpu.VMEM)
    dma = pltpu.SemaphoreType.DMA
    columns = (hidden, local_width, local_width, local_width, local_width, width)
    operands = [*lefts, grad_pre, attn, query, weights, *norm, grad_resid, vec_two, *terms]
    in_specs = [vmem] * len(operands)
    in_specs[6] = pl.BlockSpec(memory_space=pl.ANY)
    slots = max(1, min(2, reach - 1))
    hops = max(reach, 1)
    return pl.pallas_call(
        functools.partial(tail_kernel, sizes, width, reach),
        out_shape=tuple(jax.ShapeDtypeStruct((piece, n), f32) for n in columns)
        + (jax.ShapeDtypeStruct((count, depth), bf16),),
        in_specs=in_specs,
        out_specs=(vmem,) * 7,
        scratch_shapes=[
            pltpu.VMEM((count, 2 * local_width), bf16),
            pltpu.VMEM((min(2, hops), count, 2 * local_width), bf16),
            pltpu.VMEM((slots, count, 2 * local_width), bf16),
            pltpu.VMEM((2, width, 3 * local_width), bf16),
            pltpu.VMEM((blocks, count, width), bf16),
            pltpu.VMEM((blocks, count, width), bf16),
            pltpu.VMEM((depth, 128), f32),
            pltpu.VMEM((2, count, 1), f32),
            dma((2, hops)),
            pltpu.SemaphoreType.REGULAR,
            dma((2,)),
            dma((2, blocks)),
        ]
        + reduce_scratch(sizes, width, depth),
        compiler_params=pltpu.CompilerParams(
            collective_id=number, has_side_effects=True, vmem_limit_bytes=62 * 1024 * 1024
        ),
        cost_estimate=pl.CostEstimate(
            flops=8 * depth * count * (hidden + 4 * local_width),
            transcendentals=0,
            bytes_accessed=16 * depth * count,
        ),
        name="backward_tail",
    )(*operands)


def per_device(
    sizes,
    tokens,
    segments,
    query_weight,
    key_weight,
    value_weight,
    out_weight,
    up_weight,
    down_weight,
    attn_gain,
    attn_bias,
    mlp_gain,
    mlp_bias,
    cotangent,
):
    seq_dev, group_len, model_width = tokens.shape
    assert seq_dev == 1
    shard_rows, local_width = query_weight.shape
    hidden_local = up_weight.shape[1]
    heads = local_width // HEAD
    seq_len = segments.shape[1]
    context, tensor = sizes["context"], sizes["tensor"]
    place = lax.axis_index("context")
    weight_axes = ("fsdp", "context")

    vectors = jnp.stack([attn_gain, attn_bias, mlp_gain, mlp_bias], axis=1)
    vectors = jnp.pad(vectors, ((0, 0), (0, HEAD - 4)))
    pair_weight = jnp.stack(
        [w.reshape(shard_rows, heads, HEAD) for w in (key_weight, value_weight)], axis=2
    ).reshape(shard_rows, 2 * local_width)
    attn_full = lax.all_gather(
        jnp.concatenate([query_weight, pair_weight, out_weight, vectors], axis=1),
        weight_axes,
        axis=0,
        tiled=True,
    )
    mlp_full = lax.all_gather(
        jnp.concatenate([up_weight, down_weight], axis=1), weight_axes, axis=0, tiled=True
    )
    full_qkv = attn_full[:, : 3 * local_width]
    full_out = attn_full[:, 3 * local_width : 4 * local_width]
    vecs = attn_full[:, 4 * local_width : 4 * local_width + 4].T.astype(f32)
    gain_one, bias_one, gain_two, bias_two = vecs[0], vecs[1], vecs[2], vecs[3]
    full_up = mlp_full[:, :hidden_local]
    full_down = mlp_full[:, hidden_local:]

    rows_in = tokens.reshape(group_len, model_width).astype(f32)
    hat_one, inv_one = norm_stats(rows_in)
    mean_one = jnp.mean(rows_in, axis=-1, keepdims=True)
    normed_one = (hat_one * gain_one + bias_one).astype(bf16)
    qkv = jnp.dot(normed_one, full_qkv, preferred_element_type=f32).astype(bf16)

    reach = min(context - 1, -(-(seq_len // 2 - 1) // group_len))
    far = []
    piece = qkv[:, local_width:]
    for _ in range(reach):
        piece = line_move(piece, "context", context, 1)
        far.append(piece)
    first = place * group_len
    seg_row = lax.dynamic_slice_in_dim(segments, first, group_len, 1)
    seg_cols = [seg_row]
    for back in range(1, reach + 1):
        start = jnp.maximum(first - back * group_len, 0)
        block = lax.dynamic_slice_in_dim(segments, start, group_len, 1)
        seg_cols.append(jnp.where(place >= back, block, -1))
    flags = jnp.stack([(cols[0, -1] == seg_row[0, 0]).astype(jnp.int32) for cols in seg_cols[1:]])
    seg_cols = jnp.concatenate(seg_cols, axis=0)[:, :, None]

    attn, log_sum = attention_forward(flags, seg_row, seg_cols, qkv, far, heads)
    branch = contract(attn, full_out, 1, 1).astype(bf16)
    residual = rows_in + (branch.astype(f32) + tensor_other(branch, tensor).astype(f32))

    hat_two, inv_two = norm_stats(residual)
    normed_two = (hat_two * gain_two + bias_two).astype(bf16)
    row_left, up_left, one_left = lax.optimization_barrier(
        (cotangent.reshape(group_len, model_width).T, normed_two.T, normed_one.T)
    )
    pre_act = jnp.dot(
        after(normed_two, row_left, up_left, one_left), full_up, preferred_element_type=f32
    )
    normal_cdf = 0.5 * (1.0 + lax.erf(pre_act * half_root))
    activated = (pre_act * normal_cdf).astype(bf16)
    slope = normal_cdf + pre_act * density * jnp.exp(-0.5 * pre_act * pre_act)
    grad_rows = cotangent.reshape(group_len, model_width)
    grad_act = jnp.dot(grad_rows, full_down, preferred_element_type=f32)
    grad_pre = (grad_act * slope).astype(bf16)
    mean_two = jnp.mean(residual, axis=-1, keepdims=True)
    down_grad, output, grad_resid, out_left, vec_two, grad_attn = backward_middle(
        row_left,
        activated,
        grad_pre,
        residual,
        grad_rows,
        (mean_two, inv_two, gain_two[None]),
        mlp_full,
        attn_full,
        sizes,
        WIDTH,
        1,
    )
    output = output.reshape(tokens.shape)
    results = attention_backward(
        flags, seg_row, seg_cols, qkv, far, grad_attn, attn, log_sum, heads
    )
    up_grad, out_grad, query_grad, key_grad, value_grad, vector_part, tokens_grad = backward_tail(
        (up_left, out_left, one_left),
        grad_pre,
        attn,
        results[0],
        attn_full,
        (tokens.reshape(group_len, model_width), mean_one, inv_one, gain_one[None]),
        grad_resid,
        vec_two,
        results[1:],
        sizes,
        WIDTH,
        2,
    )
    tokens_grad = tokens_grad.reshape(tokens.shape)
    vector_part = vector_part[:, :8]
    vector_grads = (vector_part + tensor_other(vector_part, tensor)).T
    return (
        output,
        tokens_grad,
        query_grad,
        key_grad,
        value_grad,
        out_grad,
        up_grad,
        down_grad,
        vector_grads[0],
        vector_grads[1],
        vector_grads[2],
        vector_grads[3],
    )


def solution(mesh):
    weight = P(("fsdp", "context"), "tensor")
    vector = P(("fsdp", "context"))
    rows = P("fsdp", "context", None)
    return jax.shard_map(
        functools.partial(per_device, dict(mesh.shape)),
        mesh=mesh,
        in_specs=(rows, P("fsdp", None)) + (weight,) * 6 + (vector,) * 4 + (rows,),
        out_specs=(rows, rows) + (weight,) * 6 + (vector,) * 4,
        check_vma=False,
    )
```

```python
import functools

import jax
import jax.numpy as jnp
from jax import lax
from jax.experimental import pallas as pl
from jax.experimental.pallas import tpu as pltpu
from jax.sharding import PartitionSpec as P

HEAD = 128

epsilon = 1e-05
big_negative = -1e30
density = 0.3989422804014327
half_root = 0.7071067811865476
bf16 = jnp.bfloat16
f32 = jnp.float32
MESH = pl.DeviceIdType.MESH
WIDTH = 256


def contract(left, right, left_dim, right_dim):
    return lax.dot_general(
        left, right, (((left_dim,), (right_dim,)), ((), ())), preferred_element_type=f32
    )


def norm_stats(row_vals):
    average = jnp.mean(row_vals, axis=-1, keepdims=True)
    centered = row_vals - average
    variance = jnp.mean(centered * centered, axis=-1, keepdims=True)
    inv_std = lax.rsqrt(variance + epsilon)
    return (centered * inv_std, inv_std)


def norm_back(grad_out, normed_hat, inv_std, gain_vals):
    scaled = grad_out * gain_vals
    first_mean = jnp.mean(scaled, axis=-1, keepdims=True)
    second_mean = jnp.mean(scaled * normed_hat, axis=-1, keepdims=True)
    return inv_std * (scaled - first_mean - normed_hat * second_mean)


def attn_forward_kernel(reach, factor, flags, *refs):
    seg_row, seg_cols, query, own_key, own_value = refs[:5]
    far = refs[5 : 5 + 2 * reach]
    out, log_sum, run_max, run_sum, run_acc = refs[5 + 2 * reach :]
    rows = query.shape[0]

    def block(key_ref, value_ref, index, first):
        scores = contract(key_ref[...], query[...], 1, 1) * factor
        allowed = seg_cols[index] == seg_row[...]
        if first:
            key_pos = lax.broadcasted_iota(jnp.int32, (rows, rows), 0)
            query_pos = lax.broadcasted_iota(jnp.int32, (rows, rows), 1)
            allowed = allowed & (key_pos <= query_pos)
        scores = jnp.where(allowed, scores, big_negative)
        peak = jnp.max(scores, axis=0, keepdims=True)
        if not first:
            peak = jnp.maximum(peak, run_max[...])
        terms = jnp.where(allowed, jnp.exp(scores - peak), 0.0)
        total = jnp.sum(terms, axis=0, keepdims=True)
        value_sum = contract(value_ref[...], terms.astype(bf16), 0, 0)
        if first:
            run_sum[...] = total
            run_acc[...] = value_sum
        else:
            shrink = jnp.exp(run_max[...] - peak)
            run_sum[...] = run_sum[...] * shrink + total
            run_acc[...] = run_acc[...] * shrink + value_sum
        run_max[...] = peak

    block(own_key, own_value, 0, True)
    for step in range(reach):

        @pl.when(flags[step] > 0)
        def _(step=step):
            block(far[2 * step], far[2 * step + 1], step + 1, False)

    out[...] = (run_acc[...] / run_sum[...]).T.astype(bf16)
    log_sum[0] = run_max[...] + jnp.log(run_sum[...])


def head_spec(rows, first, stride=1):
    return pl.BlockSpec((rows, HEAD), lambda h, flags: (0, first + stride * h))


def attention_forward(flags, seg_row, seg_cols, qkv, far, heads):
    rows = qkv.shape[0]
    reach = len(far)
    in_specs = [
        pl.BlockSpec((1, rows), lambda h, flags: (0, 0)),
        pl.BlockSpec(seg_cols.shape, lambda h, flags: (0, 0, 0)),
        head_spec(rows, 0),
        head_spec(rows, heads, 2),
        head_spec(rows, heads + 1, 2),
    ]
    operands = [seg_row, seg_cols, qkv, qkv, qkv]
    for piece in far:
        in_specs += [head_spec(rows, 0, 2), head_spec(rows, 1, 2)]
        operands += [piece, piece]
    pairs = heads * rows * rows * (reach + 1)
    return pl.pallas_call(
        functools.partial(attn_forward_kernel, reach, HEAD ** (-0.5)),
        out_shape=(
            jax.ShapeDtypeStruct((rows, heads * HEAD), bf16),
            jax.ShapeDtypeStruct((heads, 1, rows), f32),
        ),
        grid_spec=pltpu.PrefetchScalarGridSpec(
            num_scalar_prefetch=1,
            grid=(heads,),
            in_specs=in_specs,
            out_specs=(
                head_spec(rows, 0),
                pl.BlockSpec((1, 1, rows), lambda h, flags: (h, 0, 0)),
            ),
            scratch_shapes=[
                pltpu.VMEM((1, rows), f32),
                pltpu.VMEM((1, rows), f32),
                pltpu.VMEM((HEAD, rows), f32),
            ],
        ),
        cost_estimate=pl.CostEstimate(
            flops=4 * HEAD * pairs, transcendentals=pairs, bytes_accessed=16 * rows * heads * HEAD
        ),
        name="attention_forward",
    )(flags, *operands)


def swap(array, axis, size):
    return lax.ppermute(array, axis, [(i, i ^ 1) for i in range(size)])


def line_move(array, axis, size, step):
    moves = [(i, i + step) for i in range(size) if 0 <= i + step < size]
    return lax.ppermute(array, axis, moves)


def tensor_other(part, size):
    if size == 2:
        return swap(part, "tensor", 2)
    return lax.psum(part, "tensor") - part


def after(value, *others):
    return lax.optimization_barrier((value,) + others)[0]


def remote(source, target, sems, peer):
    return pltpu.make_async_remote_copy(
        src_ref=source,
        dst_ref=target,
        send_sem=sems[0],
        recv_sem=sems[1],
        device_id=peer,
        device_id_type=MESH,
    )


def give(sem, peer):
    pl.semaphore_signal(sem, inc=1, device_id=peer, device_id_type=MESH)


def reduce_loop(sizes, width, depth, pairs, outs, scratch, others=(), extra=None):
    fsdp, context = sizes["fsdp"], sizes["context"]
    levels = context.bit_length() - 1
    (core_send, core_recv, chip_send, chip_recv, own) = scratch[:5]
    (core_sems, chip_sems, line_sems, core_free, chip_free, line_free) = scratch[5:11]
    line_send = scratch[11 : 11 + levels]
    line_recv = scratch[11 + levels : 11 + 2 * levels]
    line_keep = scratch[11 + 2 * levels : 11 + 3 * levels]
    chips = fsdp // 2
    mine, place = lax.axis_index("fsdp"), lax.axis_index("context")
    core, chip = lax.rem(mine, 2), lax.div(mine, 2)
    rows = depth // fsdp
    piece = rows // context
    starts, total = [], 0
    for pair in pairs:
        starts.append(total)
        total += pair[1]

    sibling = {"fsdp": mine + 1 - 2 * core}
    chip_to = [{"fsdp": lax.rem(mine + 2 * k, fsdp)} for k in range(chips)]
    chip_from = [{"fsdp": lax.rem(mine + fsdp - 2 * k, fsdp)} for k in range(chips)]
    bits = [lax.rem(lax.div(place, 1 << level), 2) for level in range(levels)]
    partners = [
        {"context": place + (1 - 2 * bits[level]) * (1 << level)} for level in range(levels)
    ]

    barrier = pltpu.get_barrier_semaphore()
    peers = [sibling] + chip_to[1:] + partners + list(others)
    for peer in peers:
        pl.semaphore_signal(barrier, inc=1, device_id=peer, device_id_type=MESH)
    pl.semaphore_wait(barrier, len(peers))

    def core_copy(t):
        slot = lax.rem(t, 2)
        sems = (core_sems.at[0, slot], core_sems.at[1, slot])
        return remote(core_send.at[slot], core_recv.at[slot], sems, sibling)

    def chip_copy(t, k):
        slot = lax.rem(t, 2)
        sems = (chip_sems.at[0, slot, k - 1], chip_sems.at[1, slot, k - 1])
        return remote(chip_send.at[slot, k - 1], chip_recv.at[slot, k - 1], sems, chip_to[k])

    def line_copy(t, level):
        slot = lax.rem(t, 3)
        sems = (line_sems.at[0, slot, level], line_sems.at[1, slot, level])
        source = line_send[level].at[slot, 1 - bits[level]]
        return remote(source, line_recv[level].at[slot], sems, partners[level])

    def line_out(t, level, value):
        slot = lax.rem(t, 3)

        @pl.when(t >= 3)
        def _():
            line_copy(t - 3, level).wait_send()

        for i in range(context >> level):
            line_send[level][slot, i % 2, i // 2] = value(i).astype(bf16)

            @pl.when(bits[level] == i % 2)
            def _(i=i):
                line_keep[level][slot, i // 2] = value(i)

        @pl.when(t >= 3)
        def _():
            pl.semaphore_wait(line_free.at[level], 1)

        line_copy(t, level).start()

    def each_pair(t, body):
        for start, (part, count, _) in zip(starts, pairs):

            @pl.when((t >= start) & (t < start + count))
            def _(start=start, part=part):
                body(lambda block: part(t - start, pl.multiple_of(block * rows, rows), rows))

    def first_stage(t):
        slot = lax.rem(t, 2)

        @pl.when(t >= 2)
        def _():
            core_copy(t - 2).wait_send()

        def body(part):
            for j in range(chips):
                core_send[slot, j] = part(2 * j + 1 - core).astype(bf16)

        each_pair(t, body)

        @pl.when(t >= 2)
        def _():
            pl.semaphore_wait(core_free, 1)

        core_copy(t).start()

    def second_stage(t):
        slot = lax.rem(t, 2)
        core_copy(t).wait_recv()

        @pl.when(t >= 2)
        def _():
            for k in range(1, chips):
                chip_copy(t - 2, k).wait_send()

        def body(part):
            for k in list(range(1, chips)) + [0]:
                target = lax.rem(chip + k, chips)
                both = part(2 * target + core) + core_recv[slot, target].astype(f32)
                if k:
                    chip_send[slot, k - 1] = both.astype(bf16)
                else:
                    own[slot] = both

        each_pair(t, body)

        @pl.when(t <= total - 3)
        def _():
            give(core_free, sibling)

        for k in range(1, chips):

            @pl.when(t >= 2)
            def _(k=k):
                pl.semaphore_wait(chip_free.at[k - 1], 1)

            chip_copy(t, k).start()

    def third_stage(t):
        slot = lax.rem(t, 2)
        value = own[slot]
        for k in range(1, chips):
            chip_copy(t, k).wait_recv()
            value = value + chip_recv[slot, k - 1].astype(f32)
        line_out(t, 0, lambda i: value[i * piece : (i + 1) * piece])

        @pl.when(t <= total - 3)
        def _():
            for k in range(1, chips):
                give(chip_free.at[k - 1], chip_from[k])

    def line_stage(t, level):
        slot = lax.rem(t, 3)
        line_copy(t, level).wait_recv()

        def value(i):
            return line_keep[level][slot, i] + line_recv[level][slot, i].astype(f32)

        if level + 1 < levels:
            line_out(t, level + 1, value)
        else:
            result = value(0)
            for start, (_, count, numbers) in zip(starts, pairs):

                @pl.when((t >= start) & (t < start + count))
                def _(start=start, numbers=numbers):
                    span = width // len(numbers)
                    column = pl.multiple_of((t - start) * span, span)
                    for index, number in enumerate(numbers):
                        outs[number][:, pl.ds(column, span)] = result[
                            :, index * span : (index + 1) * span
                        ]

        @pl.when(t <= total - 4)
        def _():
            give(line_free.at[level], partners[level])

    stages = [(0, first_stage), (1, second_stage), (2, third_stage)] + [
        (4 + 2 * level, functools.partial(line_stage, level=level)) for level in range(levels)
    ]

    def step(s, carry):
        for lag, stage in stages:

            @pl.when((s >= lag) & (s < total + lag))
            def _(lag=lag, stage=stage):
                stage(s - lag)

        if extra is not None:
            extra(s)
        return carry

    lax.fori_loop(0, total + 2 + 2 * levels, step, 0)
    for t in range(total - 2, total):
        core_copy(t).wait_send()
        for k in range(1, chips):
            chip_copy(t, k).wait_send()
    for t in range(total - 3, total):
        for level in range(levels):
            line_copy(t, level).wait_send()


def reduce_scratch(sizes, width, depth):
    fsdp, context = sizes["fsdp"], sizes["context"]
    chips = fsdp // 2
    rows = depth // fsdp
    piece = rows // context
    levels = context.bit_length() - 1
    assert context == 1 << levels
    dma, regular = pltpu.SemaphoreType.DMA, pltpu.SemaphoreType.REGULAR
    halves = [context >> (level + 1) for level in range(levels)]
    return (
        [
            pltpu.VMEM((2, chips, rows, width), bf16),
            pltpu.VMEM((2, chips, rows, width), bf16),
            pltpu.VMEM((2, chips - 1, rows, width), bf16),
            pltpu.VMEM((2, chips - 1, rows, width), bf16),
            pltpu.VMEM((2, rows, width), f32),
            dma((2, 2)),
            dma((2, 2, chips - 1)),
            dma((2, 3, levels)),
            regular,
            regular((chips - 1,)),
            regular((levels,)),
        ]
        + [pltpu.VMEM((3, 2, n, piece, width), bf16) for n in halves]
        + [pltpu.VMEM((3, n, piece, width), bf16) for n in halves]
        + [pltpu.VMEM((3, n, piece, width), f32) for n in halves]
    )


def product_part(left, right, first, width):
    def part(chunk, row, rows):
        column = pl.multiple_of((first + chunk) * width, width)
        return jnp.dot(
            left[pl.ds(row, rows), :], right[:, pl.ds(column, width)], preferred_element_type=f32
        )

    return part


def column_sums(first, second, row, width):
    first = jnp.sum(first, axis=0, keepdims=True)
    second = jnp.sum(second, axis=0, keepdims=True)
    line = lax.broadcasted_iota(jnp.int32, (128, width), 0)
    return jnp.where(line == row, first, jnp.where(line == row + 1, second, 0.0)).T


def middle_kernel(sizes, width, *refs):
    row_left, act, grad_pre, resid, rows, average, inverse, gain, weights, attn_full = refs[:10]
    down_grad, output, grad_resid, out_left, vec_two, grad_attn = refs[10:16]
    held, held_out, part_send, part_recv, means, acc = refs[16:22]
    held_sems, out_sem, part_sems = refs[22:25]
    scratch = refs[25:]
    depth, count = row_left.shape
    hidden = act.shape[1]
    local_width = grad_attn.shape[1]
    blocks = depth // width
    other = {"tensor": 1 - lax.axis_index("tensor")}
    pairs = [(product_part(row_left, act, 0, width), hidden // width, (0,))]
    total = hidden // width

    def held_copy(b):
        row = pl.multiple_of(lax.rem(b, blocks) * width, width)
        column = pl.multiple_of(lax.div(b, blocks) * hidden, hidden)
        slot = lax.rem(b, 2)
        return pltpu.make_async_copy(
            weights.at[pl.ds(row, width), pl.ds(column, hidden)], held.at[slot], held_sems.at[slot]
        )

    def out_copy():
        source = attn_full.at[:, pl.ds(3 * local_width, local_width)]
        return pltpu.make_async_copy(source, held_out, out_sem)

    def part_copy(b):
        sems = (part_sems.at[0, b], part_sems.at[1, b])
        return remote(part_send.at[b], part_recv.at[b], sems, other)

    def at(b):
        return pl.ds(pl.multiple_of(b * width, width), width)

    def normed_hat(b):
        return (resid[:, at(b)] - average[...]) * inverse[...]

    def send_block(b, left):
        held_copy(b).wait()
        rounded = contract(left[...], held[lax.rem(b, 2)], 1, 1).astype(bf16)
        part_send[b] = rounded
        part_copy(b).start()

        @pl.when(b + 2 < 2 * blocks)
        def _():
            held_copy(b + 2).start()

        return rounded.astype(f32)

    def norm_block(b):
        rounded = send_block(b, grad_pre)
        vec_two[at(b), :] = column_sums(rounded * normed_hat(b), rounded, 2, width)

    def both(b):
        return part_send[b].astype(f32) + part_recv[b].astype(f32)

    def norm_means():
        def add(b, sums):
            part_copy(b).wait_recv()
            scaled = both(b) * gain[:, at(b)]
            first = jnp.sum(scaled, axis=1, keepdims=True)
            second = jnp.sum(scaled * normed_hat(b), axis=1, keepdims=True)
            return (sums[0] + first, sums[1] + second)

        zero = jnp.zeros((count, 1), f32)
        first, second = lax.fori_loop(0, blocks, add, (zero, zero))
        means[0] = first * (1.0 / depth)
        means[1] = second * (1.0 / depth)

    def norm_result(b):
        back = both(b) * gain[:, at(b)] - means[0] - normed_hat(b) * means[1]
        result = rows[:, at(b)].astype(f32) + inverse[...] * back
        grad_resid[:, at(b)] = result
        out_left[at(b), :] = result.T.astype(bf16)
        update = jnp.dot(result.astype(bf16), held_out[at(b), :], preferred_element_type=f32)

        @pl.when(b == 0)
        def _():
            acc[...] = update

        @pl.when(b > 0)
        def _():
            acc[...] += update

        @pl.when(b == blocks - 1)
        def _():
            grad_attn[...] = acc[...].astype(bf16)

    def output_block(b):
        part_copy(blocks + b).wait_recv()
        output[:, at(b)] = (resid[:, at(b)] + both(blocks + b)).astype(bf16)

    def during(s, first, body):
        @pl.when((s >= first) & (s < first + blocks))
        def _():
            body(s - first)

    def extra(s):
        @pl.when(s == 0)
        def _():
            held_copy(0).start()
            held_copy(1).start()
            out_copy().start()

        during(s, 1, norm_block)
        during(s, 1 + blocks, lambda b: send_block(blocks + b, act))

        @pl.when(s == blocks + 3)
        def _():
            norm_means()
            out_copy().wait()

        during(s, blocks + 4, norm_result)
        during(s, blocks + 5, output_block)

    assert 2 * blocks <= total
    reduce_loop(sizes, width, depth, pairs, [down_grad], scratch, (other,), extra)
    for b in range(2 * blocks):
        part_copy(b).wait_send()


def backward_middle(left, act, grad_pre, resid, rows, norm, weights, attn_full, sizes, width, number):
    depth, count = left.shape
    hidden = act.shape[1]
    local_width = attn_full.shape[1] // HEAD // 4 * HEAD
    piece = depth // (sizes["fsdp"] * sizes["context"])
    blocks = depth // width
    vmem = pl.BlockSpec(memory_space=pltpu.VMEM)
    far = pl.BlockSpec(memory_space=pl.ANY)
    dma = pltpu.SemaphoreType.DMA
    return pl.pallas_call(
        functools.partial(middle_kernel, sizes, width),
        out_shape=(
            jax.ShapeDtypeStruct((piece, hidden), f32),
            jax.ShapeDtypeStruct((count, depth), bf16),
            jax.ShapeDtypeStruct((count, depth), f32),
            jax.ShapeDtypeStruct((depth, count), bf16),
            jax.ShapeDtypeStruct((depth, 128), f32),
            jax.ShapeDtypeStruct((count, local_width), bf16),
        ),
        in_specs=[vmem] * 8 + [far] * 2,
        out_specs=(vmem,) * 6,
        scratch_shapes=[
            pltpu.VMEM((2, width, hidden), bf16),
            pltpu.VMEM((depth, local_width), bf16),
            pltpu.VMEM((2 * blocks, count, width), bf16),
            pltpu.VMEM((2 * blocks, count, width), bf16),
            pltpu.VMEM((2, count, 1), f32),
            pltpu.VMEM((count, local_width), f32),
            dma((2,)),
            dma,
            dma((2, 2 * blocks)),
        ]
        + reduce_scratch(sizes, width, depth),
        compiler_params=pltpu.CompilerParams(
            collective_id=number, has_side_effects=True, vmem_limit_bytes=62 * 1024 * 1024
        ),
        cost_estimate=pl.CostEstimate(
            flops=12 * depth * count * hidden,
            transcendentals=0,
            bytes_accessed=4 * depth * hidden,
        ),
        name="backward_middle",
    )(left, act, grad_pre, resid, rows, *norm, weights, attn_full)


def tail_kernel(sizes, width, reach, *refs):
    up_left, out_left, one_left, grad_pre, attn = refs[:5]
    tokens, average, inverse, gain, grad_resid, vec_two = refs[5:11]
    seg_row, seg_cols, log_sum, weights, grad_attn, qkv = refs[11:17]
    far = refs[17 : 17 + reach]
    refs = refs[17 + reach :]
    outs, tokens_grad = refs[:6], refs[6]
    query, terms, hop_recv, queries, grads, kept, held, part_send, part_recv = refs[7:16]
    vec_one, means, hop_sems, head_sems, held_sems, part_sems = refs[16:22]
    scratch = refs[22:]
    context = sizes["context"]
    place = lax.axis_index("context")
    depth, count = up_left.shape
    local_width = query.shape[1]
    heads = local_width // HEAD
    factor = HEAD ** (-0.5)
    blocks = depth // width
    lower = {"context": lax.rem(place + context - 1, context)}
    upper = {"context": lax.rem(place + 1, context)}
    other = {"tensor": 1 - lax.axis_index("tensor")}

    def vec_part(chunk, row, rows):
        both = vec_one[pl.ds(row, rows), :] + vec_two[pl.ds(row, rows), :]
        return jnp.concatenate([both] * (width // both.shape[1]), axis=1)

    def pair_part(chunk, row, rows):
        return jnp.dot(one_left[pl.ds(row, rows), :], terms[0, chunk], preferred_element_type=f32)

    pairs = [
        (product_part(up_left, grad_pre, 0, width), grad_pre.shape[1] // width, (0,)),
        (product_part(out_left, attn, 0, width), local_width // width, (1,)),
        (product_part(one_left, query, 0, width), local_width // width, (2,)),
        (pair_part, heads, (3, 4)),
        (vec_part, 1, (5,)),
    ]
    total = sum(p[1] for p in pairs)
    begin = sum(p[1] for p in pairs[:3])
    gap = (begin - 1 - heads) // reach

    def head_copies(h):
        slot = lax.rem(h, 2)
        one = pl.ds(pl.multiple_of(h * HEAD, HEAD), HEAD)
        near = pl.ds(pl.multiple_of(local_width + 2 * h * HEAD, HEAD), 2 * HEAD)
        two = pl.ds(pl.multiple_of(2 * h * HEAD, HEAD), 2 * HEAD)
        sources = [(qkv.at[:, one], queries.at[slot]), (grad_attn.at[:, one], grads.at[slot])]
        sources.append((qkv.at[:, near], kept.at[slot, 0]))
        sources += [(far[i].at[:, two], kept.at[slot, i + 1]) for i in range(reach)]
        return [
            pltpu.make_async_copy(source, target, head_sems.at[slot, i])
            for i, (source, target) in enumerate(sources)
        ]

    def head_block(h):
        slot = lax.rem(h, 2)
        one = pl.ds(pl.multiple_of(h * HEAD, HEAD), HEAD)
        for copy in head_copies(h):
            copy.wait()
        own_query, own_grad = queries[slot], grads[slot]
        delta = own_grad.astype(f32) * attn[:, one].astype(f32)
        delta = jnp.sum(delta.T, axis=0, keepdims=True)
        update = None
        for index in range(reach + 1):
            key, value = kept[slot, index, :, :HEAD], kept[slot, index, :, HEAD:]
            scores = contract(key, own_query, 1, 1) * factor
            allowed = seg_cols[index] == seg_row[...]
            if index == 0:
                key_pos = lax.broadcasted_iota(jnp.int32, (count, count), 0)
                query_pos = lax.broadcasted_iota(jnp.int32, (count, count), 1)
                allowed = allowed & (key_pos <= query_pos)
            scores = jnp.where(allowed, scores, big_negative)
            probs = jnp.where(allowed, jnp.exp(scores - log_sum[h]), 0.0)
            grad_probs = contract(value, own_grad, 1, 1)
            grad_scores = (probs * (grad_probs - delta)).astype(bf16)
            key_grad = jnp.dot(grad_scores, own_query, preferred_element_type=f32) * factor
            value_grad = jnp.dot(probs.astype(bf16), own_grad, preferred_element_type=f32)
            terms[index, h, :, :HEAD] = key_grad.astype(bf16)
            terms[index, h, :, HEAD:] = value_grad.astype(bf16)
            change = contract(key, grad_scores, 0, 0)
            update = change if update is None else update + change
        query[:, one] = (update * factor).T.astype(bf16)

        @pl.when(h + 2 < heads)
        def _():
            for copy in head_copies(h + 2):
                copy.start()

    def hop_copy(j, h):
        sems = (hop_sems.at[0, j, h], hop_sems.at[1, j, h])
        return remote(terms.at[reach - j, h], hop_recv.at[j, h], sems, lower)

    def hop(j, h):
        if j == 0:
            head_block(h)
        else:

            @pl.when(place < context - 1)
            def _():
                hop_copy(j - 1, h).wait_recv()
                both = terms[reach - j, h].astype(f32) + hop_recv[j - 1, h].astype(f32)
                terms[reach - j, h] = both.astype(bf16)

        if j < reach:

            @pl.when(place > 0)
            def _():
                hop_copy(j, h).start()

    def held_copy(b):
        slot = lax.rem(b, 2)
        row = pl.multiple_of(b * width, width)
        return pltpu.make_async_copy(
            weights.at[pl.ds(row, width), pl.ds(0, 3 * local_width)],
            held.at[slot],
            held_sems.at[slot],
        )

    def part_copy(b):
        sems = (part_sems.at[0, b], part_sems.at[1, b])
        return remote(part_send.at[b], part_recv.at[b], sems, other)

    def normed_hat(b):
        columns = pl.ds(pl.multiple_of(b * width, width), width)
        return (tokens[:, columns].astype(f32) - average[...]) * inverse[...]

    def input_block(b):
        slot = lax.rem(b, 2)
        held_copy(b).wait()
        value = contract(query[...], held[slot, :, :local_width], 1, 1)
        for h in range(heads):
            first = local_width + 2 * h * HEAD
            value = value + contract(terms[0, h], held[slot, :, first : first + 2 * HEAD], 1, 1)
        rounded = value.astype(bf16)
        part_send[b] = rounded
        part_copy(b).start()

        @pl.when(b + 2 < blocks)
        def _():
            held_copy(b + 2).start()

        rounded = rounded.astype(f32)
        vec_one[pl.ds(pl.multiple_of(b * width, width), width), :] = column_sums(
            rounded * normed_hat(b), rounded, 0, width
        )

    def scaled_block(b):
        columns = pl.ds(pl.multiple_of(b * width, width), width)
        value = part_send[b].astype(f32) + part_recv[b].astype(f32)
        return value * gain[:, columns]

    def norm_means():
        def add(b, sums):
            part_copy(b).wait_recv()
            scaled = scaled_block(b)
            first = jnp.sum(scaled, axis=1, keepdims=True)
            second = jnp.sum(scaled * normed_hat(b), axis=1, keepdims=True)
            return (sums[0] + first, sums[1] + second)

        zero = jnp.zeros((count, 1), f32)
        first, second = lax.fori_loop(0, blocks, add, (zero, zero))
        means[0] = first * (1.0 / depth)
        means[1] = second * (1.0 / depth)

    def norm_result():
        def write(b, c):
            columns = pl.ds(pl.multiple_of(b * width, width), width)
            back = scaled_block(b) - means[0] - normed_hat(b) * means[1]
            tokens_grad[:, columns] = (
                grad_resid[:, columns] + inverse[...] * back
            ).astype(bf16)
            return c

        lax.fori_loop(0, blocks, write, 0)

    def extra(s):
        @pl.when(s == 0)
        def _():
            for h in range(min(2, heads)):
                for copy in head_copies(h):
                    copy.start()

        for j in range(reach + 1):
            first = 1 + j * gap

            @pl.when((s >= first) & (s < first + heads))
            def _(j=j, first=first):
                hop(j, s - first)

        @pl.when(s == begin - 2)
        def _():
            held_copy(0).start()
            held_copy(1).start()

        @pl.when((s >= begin) & (s < begin + blocks))
        def _():
            input_block(s - begin)

        @pl.when(s == total + 1)
        def _():
            norm_means()

        @pl.when(s == total + 2)
        def _():
            norm_result()

    assert begin + blocks < total and width == 2 * HEAD and gap > 0
    reduce_loop(sizes, width, depth, pairs, outs, scratch, (other, lower, upper), extra)

    @pl.when(place > 0)
    def _():
        for j in range(reach):
            for h in range(heads):
                hop_copy(j, h).wait_send()

    for b in range(blocks):
        part_copy(b).wait_send()


def backward_tail(
    lefts, grad_pre, attn, norm, grad_resid, vec_two, masks, weights, pieces, sizes, width, number
):
    depth, count = lefts[0].shape
    local_width = attn.shape[1]
    heads = local_width // HEAD
    hidden = grad_pre.shape[1]
    reach = len(pieces) - 2
    piece = depth // (sizes["fsdp"] * sizes["context"])
    blocks = depth // width
    vmem = pl.BlockSpec(memory_space=pltpu.VMEM)
    dma = pltpu.SemaphoreType.DMA
    columns = (hidden, local_width, local_width, local_width, local_width, width)
    near = [*lefts, grad_pre, attn, *norm, grad_resid, vec_two, *masks]
    far = [weights, *pieces]
    return pl.pallas_call(
        functools.partial(tail_kernel, sizes, width, reach),
        out_shape=tuple(jax.ShapeDtypeStruct((piece, n), f32) for n in columns)
        + (jax.ShapeDtypeStruct((count, depth), bf16),),
        in_specs=[vmem] * len(near) + [pl.BlockSpec(memory_space=pl.ANY)] * len(far),
        out_specs=(vmem,) * 7,
        scratch_shapes=[
            pltpu.VMEM((count, local_width), bf16),
            pltpu.VMEM((reach + 1, heads, count, 2 * HEAD), bf16),
            pltpu.VMEM((reach, heads, count, 2 * HEAD), bf16),
            pltpu.VMEM((2, count, HEAD), bf16),
            pltpu.VMEM((2, count, HEAD), bf16),
            pltpu.VMEM((2, reach + 1, count, 2 * HEAD), bf16),
            pltpu.VMEM((2, width, 3 * local_width), bf16),
            pltpu.VMEM((blocks, count, width), bf16),
            pltpu.VMEM((blocks, count, width), bf16),
            pltpu.VMEM((depth, 128), f32),
            pltpu.VMEM((2, count, 1), f32),
            dma((2, reach, heads)),
            dma((2, reach + 3)),
            dma((2,)),
            dma((2, blocks)),
        ]
        + reduce_scratch(sizes, width, depth),
        compiler_params=pltpu.CompilerParams(
            collective_id=number, has_side_effects=True, vmem_limit_bytes=63 * 1024 * 1024
        ),
        cost_estimate=pl.CostEstimate(
            flops=8 * depth * count * (hidden + 4 * local_width),
            transcendentals=0,
            bytes_accessed=16 * depth * count,
        ),
        name="backward_tail",
    )(*near, *far)


def per_device(
    sizes,
    tokens,
    segments,
    query_weight,
    key_weight,
    value_weight,
    out_weight,
    up_weight,
    down_weight,
    attn_gain,
    attn_bias,
    mlp_gain,
    mlp_bias,
    cotangent,
):
    seq_dev, group_len, model_width = tokens.shape
    assert seq_dev == 1
    shard_rows, local_width = query_weight.shape
    hidden_local = up_weight.shape[1]
    heads = local_width // HEAD
    seq_len = segments.shape[1]
    context, tensor = sizes["context"], sizes["tensor"]
    place = lax.axis_index("context")
    weight_axes = ("fsdp", "context")

    vectors = jnp.stack([attn_gain, attn_bias, mlp_gain, mlp_bias], axis=1)
    vectors = jnp.pad(vectors, ((0, 0), (0, HEAD - 4)))
    pair_weight = jnp.stack(
        [w.reshape(shard_rows, heads, HEAD) for w in (key_weight, value_weight)], axis=2
    ).reshape(shard_rows, 2 * local_width)
    attn_full = lax.all_gather(
        jnp.concatenate([query_weight, pair_weight, out_weight, vectors], axis=1),
        weight_axes,
        axis=0,
        tiled=True,
    )
    mlp_full = lax.all_gather(
        jnp.concatenate([up_weight, down_weight], axis=1), weight_axes, axis=0, tiled=True
    )
    full_qkv = attn_full[:, : 3 * local_width]
    full_out = attn_full[:, 3 * local_width : 4 * local_width]
    vecs = attn_full[:, 4 * local_width : 4 * local_width + 4].T.astype(f32)
    gain_one, bias_one, gain_two, bias_two = vecs[0], vecs[1], vecs[2], vecs[3]
    full_up = mlp_full[:, :hidden_local]
    full_down = mlp_full[:, hidden_local:]

    rows_in = tokens.reshape(group_len, model_width).astype(f32)
    hat_one, inv_one = norm_stats(rows_in)
    mean_one = jnp.mean(rows_in, axis=-1, keepdims=True)
    normed_one = (hat_one * gain_one + bias_one).astype(bf16)
    qkv = jnp.dot(normed_one, full_qkv, preferred_element_type=f32).astype(bf16)

    reach = min(context - 1, -(-(seq_len // 2 - 1) // group_len))
    far = []
    piece = qkv[:, local_width:]
    for _ in range(reach):
        piece = line_move(piece, "context", context, 1)
        far.append(piece)
    first = place * group_len
    seg_row = lax.dynamic_slice_in_dim(segments, first, group_len, 1)
    seg_cols = [seg_row]
    for back in range(1, reach + 1):
        start = jnp.maximum(first - back * group_len, 0)
        block = lax.dynamic_slice_in_dim(segments, start, group_len, 1)
        seg_cols.append(jnp.where(place >= back, block, -1))
    flags = jnp.stack([(cols[0, -1] == seg_row[0, 0]).astype(jnp.int32) for cols in seg_cols[1:]])
    seg_cols = jnp.concatenate(seg_cols, axis=0)[:, :, None]

    attn, log_sum = attention_forward(flags, seg_row, seg_cols, qkv, far, heads)
    branch = contract(attn, full_out, 1, 1).astype(bf16)
    residual = rows_in + (branch.astype(f32) + tensor_other(branch, tensor).astype(f32))

    hat_two, inv_two = norm_stats(residual)
    normed_two = (hat_two * gain_two + bias_two).astype(bf16)
    row_left, up_left, one_left = lax.optimization_barrier(
        (cotangent.reshape(group_len, model_width).T, normed_two.T, normed_one.T)
    )
    pre_act = jnp.dot(
        after(normed_two, row_left, up_left, one_left), full_up, preferred_element_type=f32
    )
    normal_cdf = 0.5 * (1.0 + lax.erf(pre_act * half_root))
    activated = (pre_act * normal_cdf).astype(bf16)
    slope = normal_cdf + pre_act * density * jnp.exp(-0.5 * pre_act * pre_act)
    grad_rows = cotangent.reshape(group_len, model_width)
    grad_act = jnp.dot(grad_rows, full_down, preferred_element_type=f32)
    grad_pre = (grad_act * slope).astype(bf16)
    mean_two = jnp.mean(residual, axis=-1, keepdims=True)
    down_grad, output, grad_resid, out_left, vec_two, grad_attn = backward_middle(
        row_left,
        activated,
        grad_pre,
        residual,
        grad_rows,
        (mean_two, inv_two, gain_two[None]),
        mlp_full,
        attn_full,
        sizes,
        WIDTH,
        1,
    )
    output = output.reshape(tokens.shape)
    up_grad, out_grad, query_grad, key_grad, value_grad, vector_part, tokens_grad = backward_tail(
        (up_left, out_left, one_left),
        grad_pre,
        attn,
        (tokens.reshape(group_len, model_width), mean_one, inv_one, gain_one[None]),
        grad_resid,
        vec_two,
        (seg_row, seg_cols, log_sum),
        attn_full,
        (grad_attn, qkv, *far),
        sizes,
        WIDTH,
        2,
    )
    tokens_grad = tokens_grad.reshape(tokens.shape)
    vector_part = vector_part[:, :8]
    vector_grads = (vector_part + tensor_other(vector_part, tensor)).T
    return (
        output,
        tokens_grad,
        query_grad,
        key_grad,
        value_grad,
        out_grad,
        up_grad,
        down_grad,
        vector_grads[0],
        vector_grads[1],
        vector_grads[2],
        vector_grads[3],
    )


def solution(mesh):
    weight = P(("fsdp", "context"), "tensor")
    vector = P(("fsdp", "context"))
    rows = P("fsdp", "context", None)
    return jax.shard_map(
        functools.partial(per_device, dict(mesh.shape)),
        mesh=mesh,
        in_specs=(rows, P("fsdp", None)) + (weight,) * 6 + (vector,) * 4 + (rows,),
        out_specs=(rows, rows) + (weight,) * 6 + (vector,) * 4,
        check_vma=False,
    )
```

```python
import functools

import jax
import jax.numpy as jnp
from jax import lax
from jax.experimental import pallas as pl
from jax.experimental.pallas import tpu as pltpu
from jax.sharding import PartitionSpec as P

HEAD = 128

epsilon = 1e-05
big_negative = -1e30
density = 0.3989422804014327
half_root = 0.7071067811865476
bf16 = jnp.bfloat16
f32 = jnp.float32
MESH = pl.DeviceIdType.MESH
WIDTH = 256


def contract(left, right, left_dim, right_dim):
    return lax.dot_general(
        left, right, (((left_dim,), (right_dim,)), ((), ())), preferred_element_type=f32
    )


def norm_stats(row_vals):
    average = jnp.mean(row_vals, axis=-1, keepdims=True)
    centered = row_vals - average
    variance = jnp.mean(centered * centered, axis=-1, keepdims=True)
    inv_std = lax.rsqrt(variance + epsilon)
    return (centered * inv_std, inv_std)


def norm_back(grad_out, normed_hat, inv_std, gain_vals):
    scaled = grad_out * gain_vals
    first_mean = jnp.mean(scaled, axis=-1, keepdims=True)
    second_mean = jnp.mean(scaled * normed_hat, axis=-1, keepdims=True)
    return inv_std * (scaled - first_mean - normed_hat * second_mean)


def attn_forward_kernel(reach, factor, flags, *refs):
    seg_row, seg_cols, query, own_key, own_value = refs[:5]
    far = refs[5 : 5 + 2 * reach]
    out, log_sum, run_max, run_sum, run_acc = refs[5 + 2 * reach :]
    rows = query.shape[0]

    def block(key_ref, value_ref, index, first):
        scores = contract(key_ref[...], query[...], 1, 1) * factor
        allowed = seg_cols[index] == seg_row[...]
        if first:
            key_pos = lax.broadcasted_iota(jnp.int32, (rows, rows), 0)
            query_pos = lax.broadcasted_iota(jnp.int32, (rows, rows), 1)
            allowed = allowed & (key_pos <= query_pos)
        scores = jnp.where(allowed, scores, big_negative)
        peak = jnp.max(scores, axis=0, keepdims=True)
        if not first:
            peak = jnp.maximum(peak, run_max[...])
        terms = jnp.where(allowed, jnp.exp(scores - peak), 0.0)
        total = jnp.sum(terms, axis=0, keepdims=True)
        value_sum = contract(value_ref[...], terms.astype(bf16), 0, 0)
        if first:
            run_sum[...] = total
            run_acc[...] = value_sum
        else:
            shrink = jnp.exp(run_max[...] - peak)
            run_sum[...] = run_sum[...] * shrink + total
            run_acc[...] = run_acc[...] * shrink + value_sum
        run_max[...] = peak

    block(own_key, own_value, 0, True)
    for step in range(reach):

        @pl.when(flags[step] > 0)
        def _(step=step):
            block(far[2 * step], far[2 * step + 1], step + 1, False)

    out[...] = (run_acc[...] / run_sum[...]).T.astype(bf16)
    log_sum[0] = run_max[...] + jnp.log(run_sum[...])


def head_spec(rows, first, stride=1):
    return pl.BlockSpec((rows, HEAD), lambda h, flags: (0, first + stride * h))


def attention_forward(flags, seg_row, seg_cols, qkv, far, heads):
    rows = qkv.shape[0]
    reach = len(far)
    in_specs = [
        pl.BlockSpec((1, rows), lambda h, flags: (0, 0)),
        pl.BlockSpec(seg_cols.shape, lambda h, flags: (0, 0, 0)),
        head_spec(rows, 0),
        head_spec(rows, heads, 2),
        head_spec(rows, heads + 1, 2),
    ]
    operands = [seg_row, seg_cols, qkv, qkv, qkv]
    for piece in far:
        in_specs += [head_spec(rows, 0, 2), head_spec(rows, 1, 2)]
        operands += [piece, piece]
    pairs = heads * rows * rows * (reach + 1)
    return pl.pallas_call(
        functools.partial(attn_forward_kernel, reach, HEAD ** (-0.5)),
        out_shape=(
            jax.ShapeDtypeStruct((rows, heads * HEAD), bf16),
            jax.ShapeDtypeStruct((heads, 1, rows), f32),
        ),
        grid_spec=pltpu.PrefetchScalarGridSpec(
            num_scalar_prefetch=1,
            grid=(heads,),
            in_specs=in_specs,
            out_specs=(
                head_spec(rows, 0),
                pl.BlockSpec((1, 1, rows), lambda h, flags: (h, 0, 0)),
            ),
            scratch_shapes=[
                pltpu.VMEM((1, rows), f32),
                pltpu.VMEM((1, rows), f32),
                pltpu.VMEM((HEAD, rows), f32),
            ],
        ),
        cost_estimate=pl.CostEstimate(
            flops=4 * HEAD * pairs, transcendentals=pairs, bytes_accessed=16 * rows * heads * HEAD
        ),
        name="attention_forward",
    )(flags, *operands)


def swap(array, axis, size):
    return lax.ppermute(array, axis, [(i, i ^ 1) for i in range(size)])


def line_move(array, axis, size, step):
    moves = [(i, i + step) for i in range(size) if 0 <= i + step < size]
    return lax.ppermute(array, axis, moves)


def tensor_other(part, size):
    if size == 2:
        return swap(part, "tensor", 2)
    return lax.psum(part, "tensor") - part


def after(value, *others):
    return lax.optimization_barrier((value,) + others)[0]


def remote(source, target, sems, peer):
    return pltpu.make_async_remote_copy(
        src_ref=source,
        dst_ref=target,
        send_sem=sems[0],
        recv_sem=sems[1],
        device_id=peer,
        device_id_type=MESH,
    )


def give(sem, peer):
    pl.semaphore_signal(sem, inc=1, device_id=peer, device_id_type=MESH)


def reduce_loop(sizes, width, depth, pairs, outs, scratch, others=(), extra=None):
    fsdp, context = sizes["fsdp"], sizes["context"]
    levels = context.bit_length() - 1
    (core_send, core_recv, chip_send, chip_recv, own) = scratch[:5]
    (core_sems, chip_sems, line_sems, core_free, chip_free, line_free) = scratch[5:11]
    line_send = scratch[11 : 11 + levels]
    line_recv = scratch[11 + levels : 11 + 2 * levels]
    line_keep = scratch[11 + 2 * levels : 11 + 3 * levels]
    chips = fsdp // 2
    mine, place = lax.axis_index("fsdp"), lax.axis_index("context")
    core, chip = lax.rem(mine, 2), lax.div(mine, 2)
    rows = depth // fsdp
    piece = rows // context
    starts, total = [], 0
    for pair in pairs:
        starts.append(total)
        total += pair[1]

    sibling = {"fsdp": mine + 1 - 2 * core}
    chip_to = [{"fsdp": lax.rem(mine + 2 * k, fsdp)} for k in range(chips)]
    chip_from = [{"fsdp": lax.rem(mine + fsdp - 2 * k, fsdp)} for k in range(chips)]
    bits = [lax.rem(lax.div(place, 1 << level), 2) for level in range(levels)]
    partners = [
        {"context": place + (1 - 2 * bits[level]) * (1 << level)} for level in range(levels)
    ]

    barrier = pltpu.get_barrier_semaphore()
    peers = [sibling] + chip_to[1:] + partners + list(others)
    for peer in peers:
        pl.semaphore_signal(barrier, inc=1, device_id=peer, device_id_type=MESH)
    pl.semaphore_wait(barrier, len(peers))

    def core_copy(t):
        slot = lax.rem(t, 2)
        sems = (core_sems.at[0, slot], core_sems.at[1, slot])
        return remote(core_send.at[slot], core_recv.at[slot], sems, sibling)

    def chip_copy(t, k):
        slot = lax.rem(t, 2)
        sems = (chip_sems.at[0, slot, k - 1], chip_sems.at[1, slot, k - 1])
        return remote(chip_send.at[slot, k - 1], chip_recv.at[slot, k - 1], sems, chip_to[k])

    def line_copy(t, level):
        slot = lax.rem(t, 3)
        sems = (line_sems.at[0, slot, level], line_sems.at[1, slot, level])
        source = line_send[level].at[slot, 1 - bits[level]]
        return remote(source, line_recv[level].at[slot], sems, partners[level])

    def line_out(t, level, value):
        slot = lax.rem(t, 3)

        @pl.when(t >= 3)
        def _():
            line_copy(t - 3, level).wait_send()

        for i in range(context >> level):
            line_send[level][slot, i % 2, i // 2] = value(i).astype(bf16)

            @pl.when(bits[level] == i % 2)
            def _(i=i):
                line_keep[level][slot, i // 2] = value(i)

        @pl.when(t >= 3)
        def _():
            pl.semaphore_wait(line_free.at[level], 1)

        line_copy(t, level).start()

    def each_pair(t, body):
        for start, (part, count, _) in zip(starts, pairs):

            @pl.when((t >= start) & (t < start + count))
            def _(start=start, part=part):
                body(lambda block: part(t - start, pl.multiple_of(block * rows, rows), rows))

    def first_stage(t):
        slot = lax.rem(t, 2)

        @pl.when(t >= 2)
        def _():
            core_copy(t - 2).wait_send()

        def body(part):
            for j in range(chips):
                core_send[slot, j] = part(2 * j + 1 - core).astype(bf16)

        each_pair(t, body)

        @pl.when(t >= 2)
        def _():
            pl.semaphore_wait(core_free, 1)

        core_copy(t).start()

    def second_stage(t):
        slot = lax.rem(t, 2)
        core_copy(t).wait_recv()

        @pl.when(t >= 2)
        def _():
            for k in range(1, chips):
                chip_copy(t - 2, k).wait_send()

        def body(part):
            for k in list(range(1, chips)) + [0]:
                target = lax.rem(chip + k, chips)
                both = part(2 * target + core) + core_recv[slot, target].astype(f32)
                if k:
                    chip_send[slot, k - 1] = both.astype(bf16)
                else:
                    own[slot] = both

        each_pair(t, body)

        @pl.when(t <= total - 3)
        def _():
            give(core_free, sibling)

        for k in range(1, chips):

            @pl.when(t >= 2)
            def _(k=k):
                pl.semaphore_wait(chip_free.at[k - 1], 1)

            chip_copy(t, k).start()

    def third_stage(t):
        slot = lax.rem(t, 2)
        value = own[slot]
        for k in range(1, chips):
            chip_copy(t, k).wait_recv()
            value = value + chip_recv[slot, k - 1].astype(f32)
        line_out(t, 0, lambda i: value[i * piece : (i + 1) * piece])

        @pl.when(t <= total - 3)
        def _():
            for k in range(1, chips):
                give(chip_free.at[k - 1], chip_from[k])

    def line_stage(t, level):
        slot = lax.rem(t, 3)
        line_copy(t, level).wait_recv()

        def value(i):
            return line_keep[level][slot, i] + line_recv[level][slot, i].astype(f32)

        if level + 1 < levels:
            line_out(t, level + 1, value)
        else:
            result = value(0)
            for start, (_, count, numbers) in zip(starts, pairs):

                @pl.when((t >= start) & (t < start + count))
                def _(start=start, numbers=numbers):
                    span = width // len(numbers)
                    column = pl.multiple_of((t - start) * span, span)
                    for index, number in enumerate(numbers):
                        outs[number][:, pl.ds(column, span)] = result[
                            :, index * span : (index + 1) * span
                        ]

        @pl.when(t <= total - 4)
        def _():
            give(line_free.at[level], partners[level])

    stages = [(0, first_stage), (1, second_stage), (2, third_stage)] + [
        (4 + 2 * level, functools.partial(line_stage, level=level)) for level in range(levels)
    ]

    def step(s, carry):
        for lag, stage in stages:

            @pl.when((s >= lag) & (s < total + lag))
            def _(lag=lag, stage=stage):
                stage(s - lag)

        if extra is not None:
            extra(s)
        return carry

    lax.fori_loop(0, total + 2 + 2 * levels, step, 0)
    for t in range(total - 2, total):
        core_copy(t).wait_send()
        for k in range(1, chips):
            chip_copy(t, k).wait_send()
    for t in range(total - 3, total):
        for level in range(levels):
            line_copy(t, level).wait_send()


def reduce_scratch(sizes, width, depth):
    fsdp, context = sizes["fsdp"], sizes["context"]
    chips = fsdp // 2
    rows = depth // fsdp
    piece = rows // context
    levels = context.bit_length() - 1
    assert context == 1 << levels
    dma, regular = pltpu.SemaphoreType.DMA, pltpu.SemaphoreType.REGULAR
    halves = [context >> (level + 1) for level in range(levels)]
    return (
        [
            pltpu.VMEM((2, chips, rows, width), bf16),
            pltpu.VMEM((2, chips, rows, width), bf16),
            pltpu.VMEM((2, chips - 1, rows, width), bf16),
            pltpu.VMEM((2, chips - 1, rows, width), bf16),
            pltpu.VMEM((2, rows, width), f32),
            dma((2, 2)),
            dma((2, 2, chips - 1)),
            dma((2, 3, levels)),
            regular,
            regular((chips - 1,)),
            regular((levels,)),
        ]
        + [pltpu.VMEM((3, 2, n, piece, width), bf16) for n in halves]
        + [pltpu.VMEM((3, n, piece, width), bf16) for n in halves]
        + [pltpu.VMEM((3, n, piece, width), f32) for n in halves]
    )


def product_part(left, right, first, width):
    def part(chunk, row, rows):
        column = pl.multiple_of((first + chunk) * width, width)
        return jnp.dot(
            left[pl.ds(row, rows), :], right[:, pl.ds(column, width)], preferred_element_type=f32
        )

    return part


def column_sums(first, second, row, width):
    first = jnp.sum(first, axis=0, keepdims=True)
    second = jnp.sum(second, axis=0, keepdims=True)
    line = lax.broadcasted_iota(jnp.int32, (128, width), 0)
    return jnp.where(line == row, first, jnp.where(line == row + 1, second, 0.0)).T


def middle_kernel(sizes, width, *refs):
    row_left, act, grad_pre, resid, rows, average, inverse, gain, weights, attn_full = refs[:10]
    down_grad, output, grad_resid, out_left, vec_two, grad_attn = refs[10:16]
    held, held_out, part_send, part_recv, means, acc = refs[16:22]
    held_sems, out_sem, part_sems = refs[22:25]
    scratch = refs[25:]
    depth, count = row_left.shape
    hidden = act.shape[1]
    local_width = grad_attn.shape[1]
    blocks = depth // width
    other = {"tensor": 1 - lax.axis_index("tensor")}
    pairs = [(product_part(row_left, act, 0, width), hidden // width, (0,))]
    total = hidden // width

    def held_copy(b):
        row = pl.multiple_of(lax.rem(b, blocks) * width, width)
        column = pl.multiple_of(lax.div(b, blocks) * hidden, hidden)
        slot = lax.rem(b, 2)
        return pltpu.make_async_copy(
            weights.at[pl.ds(row, width), pl.ds(column, hidden)], held.at[slot], held_sems.at[slot]
        )

    def out_copy():
        source = attn_full.at[:, pl.ds(3 * local_width, local_width)]
        return pltpu.make_async_copy(source, held_out, out_sem)

    def part_copy(b):
        sems = (part_sems.at[0, b], part_sems.at[1, b])
        return remote(part_send.at[b], part_recv.at[b], sems, other)

    def at(b):
        return pl.ds(pl.multiple_of(b * width, width), width)

    def normed_hat(b):
        return (resid[:, at(b)] - average[...]) * inverse[...]

    def send_block(b, left):
        held_copy(b).wait()
        rounded = contract(left[...], held[lax.rem(b, 2)], 1, 1).astype(bf16)
        part_send[b] = rounded
        part_copy(b).start()

        @pl.when(b + 2 < 2 * blocks)
        def _():
            held_copy(b + 2).start()

        return rounded.astype(f32)

    def norm_block(b):
        rounded = send_block(b, grad_pre)
        vec_two[at(b), :] = column_sums(rounded * normed_hat(b), rounded, 2, width)

    def both(b):
        return part_send[b].astype(f32) + part_recv[b].astype(f32)

    def norm_means():
        def add(b, sums):
            part_copy(b).wait_recv()
            scaled = both(b) * gain[:, at(b)]
            first = jnp.sum(scaled, axis=1, keepdims=True)
            second = jnp.sum(scaled * normed_hat(b), axis=1, keepdims=True)
            return (sums[0] + first, sums[1] + second)

        zero = jnp.zeros((count, 1), f32)
        first, second = lax.fori_loop(0, blocks, add, (zero, zero))
        means[0] = first * (1.0 / depth)
        means[1] = second * (1.0 / depth)

    def norm_result(b):
        back = both(b) * gain[:, at(b)] - means[0] - normed_hat(b) * means[1]
        result = rows[:, at(b)].astype(f32) + inverse[...] * back
        grad_resid[:, at(b)] = result
        out_left[at(b), :] = result.T.astype(bf16)
        update = jnp.dot(result.astype(bf16), held_out[at(b), :], preferred_element_type=f32)

        @pl.when(b == 0)
        def _():
            acc[...] = update

        @pl.when(b > 0)
        def _():
            acc[...] += update

        @pl.when(b == blocks - 1)
        def _():
            grad_attn[...] = acc[...].astype(bf16)

    def output_block(b):
        part_copy(blocks + b).wait_recv()
        output[:, at(b)] = (resid[:, at(b)] + both(blocks + b)).astype(bf16)

    def during(s, first, body):
        @pl.when((s >= first) & (s < first + blocks))
        def _():
            body(s - first)

    def extra(s):
        @pl.when(s == 0)
        def _():
            held_copy(0).start()
            held_copy(1).start()
            out_copy().start()

        during(s, 1, norm_block)
        during(s, 1 + blocks, lambda b: send_block(blocks + b, act))

        @pl.when(s == blocks + 3)
        def _():
            norm_means()
            out_copy().wait()

        during(s, blocks + 4, norm_result)
        during(s, blocks + 5, output_block)

    assert 2 * blocks <= total
    reduce_loop(sizes, width, depth, pairs, [down_grad], scratch, (other,), extra)
    for b in range(2 * blocks):
        part_copy(b).wait_send()


def backward_middle(left, act, grad_pre, resid, rows, norm, weights, attn_full, sizes, width, number):
    depth, count = left.shape
    hidden = act.shape[1]
    local_width = attn_full.shape[1] // HEAD // 4 * HEAD
    piece = depth // (sizes["fsdp"] * sizes["context"])
    blocks = depth // width
    vmem = pl.BlockSpec(memory_space=pltpu.VMEM)
    far = pl.BlockSpec(memory_space=pl.ANY)
    dma = pltpu.SemaphoreType.DMA
    return pl.pallas_call(
        functools.partial(middle_kernel, sizes, width),
        out_shape=(
            jax.ShapeDtypeStruct((piece, hidden), f32),
            jax.ShapeDtypeStruct((count, depth), bf16),
            jax.ShapeDtypeStruct((count, depth), f32),
            jax.ShapeDtypeStruct((depth, count), bf16),
            jax.ShapeDtypeStruct((depth, 128), f32),
            jax.ShapeDtypeStruct((count, local_width), bf16),
        ),
        in_specs=[vmem] * 8 + [far] * 2,
        out_specs=(vmem,) * 6,
        scratch_shapes=[
            pltpu.VMEM((2, width, hidden), bf16),
            pltpu.VMEM((depth, local_width), bf16),
            pltpu.VMEM((2 * blocks, count, width), bf16),
            pltpu.VMEM((2 * blocks, count, width), bf16),
            pltpu.VMEM((2, count, 1), f32),
            pltpu.VMEM((count, local_width), f32),
            dma((2,)),
            dma,
            dma((2, 2 * blocks)),
        ]
        + reduce_scratch(sizes, width, depth),
        compiler_params=pltpu.CompilerParams(
            collective_id=number, has_side_effects=True, vmem_limit_bytes=62 * 1024 * 1024
        ),
        cost_estimate=pl.CostEstimate(
            flops=12 * depth * count * hidden,
            transcendentals=0,
            bytes_accessed=4 * depth * hidden,
        ),
        name="backward_middle",
    )(left, act, grad_pre, resid, rows, *norm, weights, attn_full)


def tail_kernel(sizes, width, reach, *refs):
    up_left, out_left, one_left, grad_pre, attn = refs[:5]
    tokens, average, inverse, gain, grad_resid, vec_two = refs[5:11]
    seg_row, seg_cols, log_sum, weights, grad_attn, qkv = refs[11:17]
    far = refs[17 : 17 + reach]
    refs = refs[17 + reach :]
    outs, tokens_grad = refs[:6], refs[6]
    query, terms, hop_recv, queries, grads, kept, held, part_send, part_recv = refs[7:16]
    vec_one, means, hop_sems, head_sems, held_sems, part_sems = refs[16:22]
    scratch = refs[22:]
    context = sizes["context"]
    place = lax.axis_index("context")
    depth, count = up_left.shape
    local_width = query.shape[1]
    heads = local_width // HEAD
    factor = HEAD ** (-0.5)
    blocks = depth // width
    lower = {"context": lax.rem(place + context - 1, context)}
    upper = {"context": lax.rem(place + 1, context)}
    other = {"tensor": 1 - lax.axis_index("tensor")}

    def vec_part(chunk, row, rows):
        both = vec_one[pl.ds(row, rows), :] + vec_two[pl.ds(row, rows), :]
        return jnp.concatenate([both] * (width // both.shape[1]), axis=1)

    def pair_part(chunk, row, rows):
        return jnp.dot(one_left[pl.ds(row, rows), :], terms[0, chunk], preferred_element_type=f32)

    pairs = [
        (product_part(up_left, grad_pre, 0, width), grad_pre.shape[1] // width, (0,)),
        (product_part(out_left, attn, 0, width), local_width // width, (1,)),
        (product_part(one_left, query, 0, width), local_width // width, (2,)),
        (pair_part, heads, (3, 4)),
        (vec_part, 1, (5,)),
    ]
    total = sum(p[1] for p in pairs)
    begin = sum(p[1] for p in pairs[:3])
    stride = 2
    gap = (begin - 2 - stride * (heads - 1)) // reach

    def head_copies(h):
        slot = lax.rem(h, 2)
        one = pl.ds(pl.multiple_of(h * HEAD, HEAD), HEAD)
        near = pl.ds(pl.multiple_of(local_width + 2 * h * HEAD, HEAD), 2 * HEAD)
        two = pl.ds(pl.multiple_of(2 * h * HEAD, HEAD), 2 * HEAD)
        sources = [(qkv.at[:, one], queries.at[slot]), (grad_attn.at[:, one], grads.at[slot])]
        sources.append((qkv.at[:, near], kept.at[slot, 0]))
        sources += [(far[i].at[:, two], kept.at[slot, i + 1]) for i in range(reach)]
        return [
            pltpu.make_async_copy(source, target, head_sems.at[slot, i])
            for i, (source, target) in enumerate(sources)
        ]

    def head_block(h):
        slot = lax.rem(h, 2)
        one = pl.ds(pl.multiple_of(h * HEAD, HEAD), HEAD)
        for copy in head_copies(h):
            copy.wait()
        own_query, own_grad = queries[slot], grads[slot]
        delta = own_grad.astype(f32) * attn[:, one].astype(f32)
        delta = jnp.sum(delta.T, axis=0, keepdims=True)
        update = None
        for index in range(reach + 1):
            key, value = kept[slot, index, :, :HEAD], kept[slot, index, :, HEAD:]
            scores = contract(key, own_query, 1, 1) * factor
            allowed = seg_cols[index] == seg_row[...]
            if index == 0:
                key_pos = lax.broadcasted_iota(jnp.int32, (count, count), 0)
                query_pos = lax.broadcasted_iota(jnp.int32, (count, count), 1)
                allowed = allowed & (key_pos <= query_pos)
            scores = jnp.where(allowed, scores, big_negative)
            probs = jnp.where(allowed, jnp.exp(scores - log_sum[h]), 0.0)
            grad_probs = contract(value, own_grad, 1, 1)
            grad_scores = (probs * (grad_probs - delta)).astype(bf16)
            key_grad = jnp.dot(grad_scores, own_query, preferred_element_type=f32) * factor
            value_grad = jnp.dot(probs.astype(bf16), own_grad, preferred_element_type=f32)
            terms[index, h, :, :HEAD] = key_grad.astype(bf16)
            terms[index, h, :, HEAD:] = value_grad.astype(bf16)
            change = contract(key, grad_scores, 0, 0)
            update = change if update is None else update + change
        query[:, one] = (update * factor).T.astype(bf16)

        @pl.when(h + 2 < heads)
        def _():
            for copy in head_copies(h + 2):
                copy.start()

    def hop_copy(j, h):
        sems = (hop_sems.at[0, j, h], hop_sems.at[1, j, h])
        return remote(terms.at[reach - j, h], hop_recv.at[j, h], sems, lower)

    def hop(j, h):
        if j == 0:
            head_block(h)
        else:

            @pl.when(place < context - 1)
            def _():
                hop_copy(j - 1, h).wait_recv()
                both = terms[reach - j, h].astype(f32) + hop_recv[j - 1, h].astype(f32)
                terms[reach - j, h] = both.astype(bf16)

        if j < reach:

            @pl.when(place > 0)
            def _():
                hop_copy(j, h).start()

    def held_copy(b):
        slot = lax.rem(b, 2)
        row = pl.multiple_of(b * width, width)
        return pltpu.make_async_copy(
            weights.at[pl.ds(row, width), pl.ds(0, 3 * local_width)],
            held.at[slot],
            held_sems.at[slot],
        )

    def part_copy(b):
        sems = (part_sems.at[0, b], part_sems.at[1, b])
        return remote(part_send.at[b], part_recv.at[b], sems, other)

    def normed_hat(b):
        columns = pl.ds(pl.multiple_of(b * width, width), width)
        return (tokens[:, columns].astype(f32) - average[...]) * inverse[...]

    def input_block(b):
        slot = lax.rem(b, 2)
        held_copy(b).wait()
        value = contract(query[...], held[slot, :, :local_width], 1, 1)
        for h in range(heads):
            first = local_width + 2 * h * HEAD
            value = value + contract(terms[0, h], held[slot, :, first : first + 2 * HEAD], 1, 1)
        rounded = value.astype(bf16)
        part_send[b] = rounded
        part_copy(b).start()

        @pl.when(b + 2 < blocks)
        def _():
            held_copy(b + 2).start()

        rounded = rounded.astype(f32)
        vec_one[pl.ds(pl.multiple_of(b * width, width), width), :] = column_sums(
            rounded * normed_hat(b), rounded, 0, width
        )

    def scaled_block(b):
        columns = pl.ds(pl.multiple_of(b * width, width), width)
        value = part_send[b].astype(f32) + part_recv[b].astype(f32)
        return value * gain[:, columns]

    def norm_means():
        def add(b, sums):
            part_copy(b).wait_recv()
            scaled = scaled_block(b)
            first = jnp.sum(scaled, axis=1, keepdims=True)
            second = jnp.sum(scaled * normed_hat(b), axis=1, keepdims=True)
            return (sums[0] + first, sums[1] + second)

        zero = jnp.zeros((count, 1), f32)
        first, second = lax.fori_loop(0, blocks, add, (zero, zero))
        means[0] = first * (1.0 / depth)
        means[1] = second * (1.0 / depth)

    def norm_result():
        def write(b, c):
            columns = pl.ds(pl.multiple_of(b * width, width), width)
            back = scaled_block(b) - means[0] - normed_hat(b) * means[1]
            tokens_grad[:, columns] = (
                grad_resid[:, columns] + inverse[...] * back
            ).astype(bf16)
            return c

        lax.fori_loop(0, blocks, write, 0)

    def extra(s):
        @pl.when(s == 0)
        def _():
            for h in range(min(2, heads)):
                for copy in head_copies(h):
                    copy.start()

        for j in range(reach + 1):
            first = 1 + j * gap

            @pl.when(
                (s >= first)
                & (s < first + stride * heads)
                & (lax.rem(s + stride - first % stride, stride) == 0)
            )
            def _(j=j, first=first):
                hop(j, lax.div(s - first, stride))

        @pl.when(s == begin - 2)
        def _():
            held_copy(0).start()
            held_copy(1).start()

        @pl.when((s >= begin) & (s < begin + blocks))
        def _():
            input_block(s - begin)

        @pl.when(s == total + 1)
        def _():
            norm_means()

        @pl.when(s == total + 2)
        def _():
            norm_result()

    assert begin + blocks < total and width == 2 * HEAD and gap > 0
    reduce_loop(sizes, width, depth, pairs, outs, scratch, (other, lower, upper), extra)

    @pl.when(place > 0)
    def _():
        for j in range(reach):
            for h in range(heads):
                hop_copy(j, h).wait_send()

    for b in range(blocks):
        part_copy(b).wait_send()


def backward_tail(
    lefts, grad_pre, attn, norm, grad_resid, vec_two, masks, weights, pieces, sizes, width, number
):
    depth, count = lefts[0].shape
    local_width = attn.shape[1]
    heads = local_width // HEAD
    hidden = grad_pre.shape[1]
    reach = len(pieces) - 2
    piece = depth // (sizes["fsdp"] * sizes["context"])
    blocks = depth // width
    vmem = pl.BlockSpec(memory_space=pltpu.VMEM)
    dma = pltpu.SemaphoreType.DMA
    columns = (hidden, local_width, local_width, local_width, local_width, width)
    near = [*lefts, grad_pre, attn, *norm, grad_resid, vec_two, *masks]
    far = [weights, *pieces]
    return pl.pallas_call(
        functools.partial(tail_kernel, sizes, width, reach),
        out_shape=tuple(jax.ShapeDtypeStruct((piece, n), f32) for n in columns)
        + (jax.ShapeDtypeStruct((count, depth), bf16),),
        in_specs=[vmem] * len(near) + [pl.BlockSpec(memory_space=pl.ANY)] * len(far),
        out_specs=(vmem,) * 7,
        scratch_shapes=[
            pltpu.VMEM((count, local_width), bf16),
            pltpu.VMEM((reach + 1, heads, count, 2 * HEAD), bf16),
            pltpu.VMEM((reach, heads, count, 2 * HEAD), bf16),
            pltpu.VMEM((2, count, HEAD), bf16),
            pltpu.VMEM((2, count, HEAD), bf16),
            pltpu.VMEM((2, reach + 1, count, 2 * HEAD), bf16),
            pltpu.VMEM((2, width, 3 * local_width), bf16),
            pltpu.VMEM((blocks, count, width), bf16),
            pltpu.VMEM((blocks, count, width), bf16),
            pltpu.VMEM((depth, 128), f32),
            pltpu.VMEM((2, count, 1), f32),
            dma((2, reach, heads)),
            dma((2, reach + 3)),
            dma((2,)),
            dma((2, blocks)),
        ]
        + reduce_scratch(sizes, width, depth),
        compiler_params=pltpu.CompilerParams(
            collective_id=number, has_side_effects=True, vmem_limit_bytes=63 * 1024 * 1024
        ),
        cost_estimate=pl.CostEstimate(
            flops=8 * depth * count * (hidden + 4 * local_width),
            transcendentals=0,
            bytes_accessed=16 * depth * count,
        ),
        name="backward_tail",
    )(*near, *far)


def per_device(
    sizes,
    tokens,
    segments,
    query_weight,
    key_weight,
    value_weight,
    out_weight,
    up_weight,
    down_weight,
    attn_gain,
    attn_bias,
    mlp_gain,
    mlp_bias,
    cotangent,
):
    seq_dev, group_len, model_width = tokens.shape
    assert seq_dev == 1
    shard_rows, local_width = query_weight.shape
    hidden_local = up_weight.shape[1]
    heads = local_width // HEAD
    seq_len = segments.shape[1]
    context, tensor = sizes["context"], sizes["tensor"]
    place = lax.axis_index("context")
    weight_axes = ("fsdp", "context")

    assert tensor == 2
    reach = min(context - 1, -(-(seq_len // 2 - 1) // group_len))
    half_len = group_len // 2
    side = lax.axis_index("tensor")
    piece = lax.dynamic_slice_in_dim(
        tokens.reshape(group_len, model_width), side * half_len, half_len, 0
    )
    far_tokens = []
    for _ in range(reach):
        piece = line_move(piece, "context", context, 1)
        other = swap(piece, "tensor", tensor)
        far_tokens.append(
            jnp.where(side == 0, jnp.stack([piece, other]), jnp.stack([other, piece])).reshape(
                group_len, model_width
            )
        )

    vectors = jnp.stack([attn_gain, attn_bias, mlp_gain, mlp_bias], axis=1)
    vectors = jnp.pad(vectors, ((0, 0), (0, HEAD - 4)))
    pair_weight = jnp.stack(
        [w.reshape(shard_rows, heads, HEAD) for w in (key_weight, value_weight)], axis=2
    ).reshape(shard_rows, 2 * local_width)
    attn_full = lax.all_gather(
        jnp.concatenate([query_weight, pair_weight, out_weight, vectors], axis=1),
        weight_axes,
        axis=0,
        tiled=True,
    )
    mlp_full = lax.all_gather(
        jnp.concatenate([up_weight, down_weight], axis=1), weight_axes, axis=0, tiled=True
    )
    full_qkv = attn_full[:, : 3 * local_width]
    full_out = attn_full[:, 3 * local_width : 4 * local_width]
    vecs = attn_full[:, 4 * local_width : 4 * local_width + 4].T.astype(f32)
    gain_one, bias_one, gain_two, bias_two = vecs[0], vecs[1], vecs[2], vecs[3]
    full_up = mlp_full[:, :hidden_local]
    full_down = mlp_full[:, hidden_local:]

    rows_in = tokens.reshape(group_len, model_width).astype(f32)
    hat_one, inv_one = norm_stats(rows_in)
    mean_one = jnp.mean(rows_in, axis=-1, keepdims=True)
    normed_one = (hat_one * gain_one + bias_one).astype(bf16)
    qkv = jnp.dot(normed_one, full_qkv, preferred_element_type=f32).astype(bf16)

    far = []
    for block in far_tokens:
        far_hat, _ = norm_stats(block.astype(f32))
        far_normed = (far_hat * gain_one + bias_one).astype(bf16)
        far.append(
            jnp.dot(
                far_normed, full_qkv[:, local_width:], preferred_element_type=f32
            ).astype(bf16)
        )
    first = place * group_len
    seg_row = lax.dynamic_slice_in_dim(segments, first, group_len, 1)
    seg_cols = [seg_row]
    for back in range(1, reach + 1):
        start = jnp.maximum(first - back * group_len, 0)
        block = lax.dynamic_slice_in_dim(segments, start, group_len, 1)
        seg_cols.append(jnp.where(place >= back, block, -1))
    flags = jnp.stack([(cols[0, -1] == seg_row[0, 0]).astype(jnp.int32) for cols in seg_cols[1:]])
    seg_cols = jnp.concatenate(seg_cols, axis=0)[:, :, None]

    attn, log_sum = attention_forward(flags, seg_row, seg_cols, qkv, far, heads)
    branch = contract(attn, full_out, 1, 1).astype(bf16)
    residual = rows_in + (branch.astype(f32) + tensor_other(branch, tensor).astype(f32))

    hat_two, inv_two = norm_stats(residual)
    normed_two = (hat_two * gain_two + bias_two).astype(bf16)
    row_left, up_left, one_left = lax.optimization_barrier(
        (cotangent.reshape(group_len, model_width).T, normed_two.T, normed_one.T)
    )
    pre_act = jnp.dot(
        after(normed_two, row_left, up_left, one_left), full_up, preferred_element_type=f32
    )
    normal_cdf = 0.5 * (1.0 + lax.erf(pre_act * half_root))
    activated = (pre_act * normal_cdf).astype(bf16)
    slope = normal_cdf + pre_act * density * jnp.exp(-0.5 * pre_act * pre_act)
    grad_rows = cotangent.reshape(group_len, model_width)
    grad_act = jnp.dot(grad_rows, full_down, preferred_element_type=f32)
    grad_pre = (grad_act * slope).astype(bf16)
    mean_two = jnp.mean(residual, axis=-1, keepdims=True)
    down_grad, output, grad_resid, out_left, vec_two, grad_attn = backward_middle(
        row_left,
        activated,
        grad_pre,
        residual,
        grad_rows,
        (mean_two, inv_two, gain_two[None]),
        mlp_full,
        attn_full,
        sizes,
        WIDTH,
        1,
    )
    output = output.reshape(tokens.shape)
    up_grad, out_grad, query_grad, key_grad, value_grad, vector_part, tokens_grad = backward_tail(
        (up_left, out_left, one_left),
        grad_pre,
        attn,
        (tokens.reshape(group_len, model_width), mean_one, inv_one, gain_one[None]),
        grad_resid,
        vec_two,
        (seg_row, seg_cols, log_sum),
        attn_full,
        (grad_attn, qkv, *far),
        sizes,
        WIDTH,
        2,
    )
    tokens_grad = tokens_grad.reshape(tokens.shape)
    vector_part = vector_part[:, :8]
    vector_grads = (vector_part + tensor_other(vector_part, tensor)).T
    return (
        output,
        tokens_grad,
        query_grad,
        key_grad,
        value_grad,
        out_grad,
        up_grad,
        down_grad,
        vector_grads[0],
        vector_grads[1],
        vector_grads[2],
        vector_grads[3],
    )


def solution(mesh):
    weight = P(("fsdp", "context"), "tensor")
    vector = P(("fsdp", "context"))
    rows = P("fsdp", "context", None)
    return jax.shard_map(
        functools.partial(per_device, dict(mesh.shape)),
        mesh=mesh,
        in_specs=(rows, P("fsdp", None)) + (weight,) * 6 + (vector,) * 4 + (rows,),
        out_specs=(rows, rows) + (weight,) * 6 + (vector,) * 4,
        check_vma=False,
    )
```

```python
import functools

import jax
import jax.numpy as jnp
from jax import lax
from jax.experimental import pallas as pl
from jax.experimental.pallas import tpu as pltpu
from jax.sharding import PartitionSpec as P

HEAD = 128

epsilon = 1e-05
big_negative = -1e30
density = 0.3989422804014327
half_root = 0.7071067811865476
bf16 = jnp.bfloat16
f32 = jnp.float32
MESH = pl.DeviceIdType.MESH
WIDTH = 256


def contract(left, right, left_dim, right_dim):
    return lax.dot_general(
        left, right, (((left_dim,), (right_dim,)), ((), ())), preferred_element_type=f32
    )


def norm_stats(row_vals):
    average = jnp.mean(row_vals, axis=-1, keepdims=True)
    centered = row_vals - average
    variance = jnp.mean(centered * centered, axis=-1, keepdims=True)
    inv_std = lax.rsqrt(variance + epsilon)
    return (centered * inv_std, inv_std)


def norm_back(grad_out, normed_hat, inv_std, gain_vals):
    scaled = grad_out * gain_vals
    first_mean = jnp.mean(scaled, axis=-1, keepdims=True)
    second_mean = jnp.mean(scaled * normed_hat, axis=-1, keepdims=True)
    return inv_std * (scaled - first_mean - normed_hat * second_mean)


def attn_forward_kernel(reach, factor, flags, *refs):
    seg_row, seg_cols, query, own_key, own_value = refs[:5]
    far = refs[5 : 5 + 2 * reach]
    out, log_sum, run_max, run_sum, run_acc = refs[5 + 2 * reach :]
    rows = query.shape[0]

    def block(key_ref, value_ref, index, first):
        scores = contract(key_ref[...], query[...], 1, 1) * factor
        allowed = seg_cols[index] == seg_row[...]
        if first:
            key_pos = lax.broadcasted_iota(jnp.int32, (rows, rows), 0)
            query_pos = lax.broadcasted_iota(jnp.int32, (rows, rows), 1)
            allowed = allowed & (key_pos <= query_pos)
        scores = jnp.where(allowed, scores, big_negative)
        peak = jnp.max(scores, axis=0, keepdims=True)
        if not first:
            peak = jnp.maximum(peak, run_max[...])
        terms = jnp.where(allowed, jnp.exp(scores - peak), 0.0)
        total = jnp.sum(terms, axis=0, keepdims=True)
        value_sum = contract(value_ref[...], terms.astype(bf16), 0, 0)
        if first:
            run_sum[...] = total
            run_acc[...] = value_sum
        else:
            shrink = jnp.exp(run_max[...] - peak)
            run_sum[...] = run_sum[...] * shrink + total
            run_acc[...] = run_acc[...] * shrink + value_sum
        run_max[...] = peak

    block(own_key, own_value, 0, True)
    for step in range(reach):

        @pl.when(flags[step] > 0)
        def _(step=step):
            block(far[2 * step], far[2 * step + 1], step + 1, False)

    out[...] = (run_acc[...] / run_sum[...]).T.astype(bf16)
    log_sum[0] = run_max[...] + jnp.log(run_sum[...])


def head_spec(rows, first, stride=1):
    return pl.BlockSpec((rows, HEAD), lambda h, flags: (0, first + stride * h))


def attention_forward(flags, seg_row, seg_cols, qkv, far, heads):
    rows = qkv.shape[0]
    reach = len(far)
    in_specs = [
        pl.BlockSpec((1, rows), lambda h, flags: (0, 0)),
        pl.BlockSpec(seg_cols.shape, lambda h, flags: (0, 0, 0)),
        head_spec(rows, 0),
        head_spec(rows, heads, 2),
        head_spec(rows, heads + 1, 2),
    ]
    operands = [seg_row, seg_cols, qkv, qkv, qkv]
    for piece in far:
        in_specs += [head_spec(rows, 0, 2), head_spec(rows, 1, 2)]
        operands += [piece, piece]
    pairs = heads * rows * rows * (reach + 1)
    return pl.pallas_call(
        functools.partial(attn_forward_kernel, reach, HEAD ** (-0.5)),
        out_shape=(
            jax.ShapeDtypeStruct((rows, heads * HEAD), bf16),
            jax.ShapeDtypeStruct((heads, 1, rows), f32),
        ),
        grid_spec=pltpu.PrefetchScalarGridSpec(
            num_scalar_prefetch=1,
            grid=(heads,),
            in_specs=in_specs,
            out_specs=(
                head_spec(rows, 0),
                pl.BlockSpec((1, 1, rows), lambda h, flags: (h, 0, 0)),
            ),
            scratch_shapes=[
                pltpu.VMEM((1, rows), f32),
                pltpu.VMEM((1, rows), f32),
                pltpu.VMEM((HEAD, rows), f32),
            ],
        ),
        cost_estimate=pl.CostEstimate(
            flops=4 * HEAD * pairs, transcendentals=pairs, bytes_accessed=16 * rows * heads * HEAD
        ),
        name="attention_forward",
    )(flags, *operands)


def swap(array, axis, size):
    return lax.ppermute(array, axis, [(i, i ^ 1) for i in range(size)])


def line_move(array, axis, size, step):
    moves = [(i, i + step) for i in range(size) if 0 <= i + step < size]
    return lax.ppermute(array, axis, moves)


def tensor_other(part, size):
    if size == 2:
        return swap(part, "tensor", 2)
    return lax.psum(part, "tensor") - part


def after(value, *others):
    return lax.optimization_barrier((value,) + others)[0]


def remote(source, target, sems, peer):
    return pltpu.make_async_remote_copy(
        src_ref=source,
        dst_ref=target,
        send_sem=sems[0],
        recv_sem=sems[1],
        device_id=peer,
        device_id_type=MESH,
    )


def give(sem, peer):
    pl.semaphore_signal(sem, inc=1, device_id=peer, device_id_type=MESH)


def reduce_loop(sizes, width, depth, pairs, outs, scratch, others=(), extra=None):
    fsdp, context = sizes["fsdp"], sizes["context"]
    levels = context.bit_length() - 1
    (core_send, core_recv, chip_send, chip_recv, own) = scratch[:5]
    (core_sems, chip_sems, line_sems, core_free, chip_free, line_free) = scratch[5:11]
    line_send = scratch[11 : 11 + levels]
    line_recv = scratch[11 + levels : 11 + 2 * levels]
    line_keep = scratch[11 + 2 * levels : 11 + 3 * levels]
    chips = fsdp // 2
    mine, place = lax.axis_index("fsdp"), lax.axis_index("context")
    core, chip = lax.rem(mine, 2), lax.div(mine, 2)
    rows = depth // fsdp
    piece = rows // context
    starts, total = [], 0
    for pair in pairs:
        starts.append(total)
        total += pair[1]

    sibling = {"fsdp": mine + 1 - 2 * core}
    chip_to = [{"fsdp": lax.rem(mine + 2 * k, fsdp)} for k in range(chips)]
    chip_from = [{"fsdp": lax.rem(mine + fsdp - 2 * k, fsdp)} for k in range(chips)]
    bits = [lax.rem(lax.div(place, 1 << level), 2) for level in range(levels)]
    partners = [
        {"context": place + (1 - 2 * bits[level]) * (1 << level)} for level in range(levels)
    ]

    barrier = pltpu.get_barrier_semaphore()
    peers = [sibling] + chip_to[1:] + partners + list(others)
    for peer in peers:
        pl.semaphore_signal(barrier, inc=1, device_id=peer, device_id_type=MESH)
    pl.semaphore_wait(barrier, len(peers))

    def core_copy(t):
        slot = lax.rem(t, 2)
        sems = (core_sems.at[0, slot], core_sems.at[1, slot])
        return remote(core_send.at[slot], core_recv.at[slot], sems, sibling)

    def chip_copy(t, k):
        slot = lax.rem(t, 2)
        sems = (chip_sems.at[0, slot, k - 1], chip_sems.at[1, slot, k - 1])
        return remote(chip_send.at[slot, k - 1], chip_recv.at[slot, k - 1], sems, chip_to[k])

    def line_copy(t, level):
        slot = lax.rem(t, 3)
        sems = (line_sems.at[0, slot, level], line_sems.at[1, slot, level])
        source = line_send[level].at[slot, 1 - bits[level]]
        return remote(source, line_recv[level].at[slot], sems, partners[level])

    def line_out(t, level, value):
        slot = lax.rem(t, 3)

        @pl.when(t >= 3)
        def _():
            line_copy(t - 3, level).wait_send()

        for i in range(context >> level):
            line_send[level][slot, i % 2, i // 2] = value(i).astype(bf16)

            @pl.when(bits[level] == i % 2)
            def _(i=i):
                line_keep[level][slot, i // 2] = value(i)

        @pl.when(t >= 3)
        def _():
            pl.semaphore_wait(line_free.at[level], 1)

        line_copy(t, level).start()

    def each_pair(t, body):
        for start, (part, count, _) in zip(starts, pairs):

            @pl.when((t >= start) & (t < start + count))
            def _(start=start, part=part):
                body(lambda block: part(t - start, pl.multiple_of(block * rows, rows), rows))

    def first_stage(t):
        slot = lax.rem(t, 2)

        @pl.when(t >= 2)
        def _():
            core_copy(t - 2).wait_send()

        def body(part):
            for j in range(chips):
                core_send[slot, j] = part(2 * j + 1 - core).astype(bf16)

        each_pair(t, body)

        @pl.when(t >= 2)
        def _():
            pl.semaphore_wait(core_free, 1)

        core_copy(t).start()

    def second_stage(t):
        slot = lax.rem(t, 2)
        core_copy(t).wait_recv()

        @pl.when(t >= 2)
        def _():
            for k in range(1, chips):
                chip_copy(t - 2, k).wait_send()

        def body(part):
            for k in list(range(1, chips)) + [0]:
                target = lax.rem(chip + k, chips)
                both = part(2 * target + core) + core_recv[slot, target].astype(f32)
                if k:
                    chip_send[slot, k - 1] = both.astype(bf16)
                else:
                    own[slot] = both

        each_pair(t, body)

        @pl.when(t <= total - 3)
        def _():
            give(core_free, sibling)

        for k in range(1, chips):

            @pl.when(t >= 2)
            def _(k=k):
                pl.semaphore_wait(chip_free.at[k - 1], 1)

            chip_copy(t, k).start()

    def third_stage(t):
        slot = lax.rem(t, 2)
        value = own[slot]
        for k in range(1, chips):
            chip_copy(t, k).wait_recv()
            value = value + chip_recv[slot, k - 1].astype(f32)
        line_out(t, 0, lambda i: value[i * piece : (i + 1) * piece])

        @pl.when(t <= total - 3)
        def _():
            for k in range(1, chips):
                give(chip_free.at[k - 1], chip_from[k])

    def line_stage(t, level):
        slot = lax.rem(t, 3)
        line_copy(t, level).wait_recv()

        def value(i):
            return line_keep[level][slot, i] + line_recv[level][slot, i].astype(f32)

        if level + 1 < levels:
            line_out(t, level + 1, value)
        else:
            result = value(0)
            for start, (_, count, numbers) in zip(starts, pairs):

                @pl.when((t >= start) & (t < start + count))
                def _(start=start, numbers=numbers):
                    span = width // len(numbers)
                    column = pl.multiple_of((t - start) * span, span)
                    for index, number in enumerate(numbers):
                        outs[number][:, pl.ds(column, span)] = result[
                            :, index * span : (index + 1) * span
                        ]

        @pl.when(t <= total - 4)
        def _():
            give(line_free.at[level], partners[level])

    stages = [(0, first_stage), (1, second_stage), (2, third_stage)] + [
        (4 + 2 * level, functools.partial(line_stage, level=level)) for level in range(levels)
    ]

    def step(s, carry):
        for lag, stage in stages:

            @pl.when((s >= lag) & (s < total + lag))
            def _(lag=lag, stage=stage):
                stage(s - lag)

        if extra is not None:
            extra(s)
        return carry

    lax.fori_loop(0, total + 2 + 2 * levels, step, 0)
    for t in range(total - 2, total):
        core_copy(t).wait_send()
        for k in range(1, chips):
            chip_copy(t, k).wait_send()
    for t in range(total - 3, total):
        for level in range(levels):
            line_copy(t, level).wait_send()


def reduce_scratch(sizes, width, depth):
    fsdp, context = sizes["fsdp"], sizes["context"]
    chips = fsdp // 2
    rows = depth // fsdp
    piece = rows // context
    levels = context.bit_length() - 1
    assert context == 1 << levels
    dma, regular = pltpu.SemaphoreType.DMA, pltpu.SemaphoreType.REGULAR
    halves = [context >> (level + 1) for level in range(levels)]
    return (
        [
            pltpu.VMEM((2, chips, rows, width), bf16),
            pltpu.VMEM((2, chips, rows, width), bf16),
            pltpu.VMEM((2, chips - 1, rows, width), bf16),
            pltpu.VMEM((2, chips - 1, rows, width), bf16),
            pltpu.VMEM((2, rows, width), f32),
            dma((2, 2)),
            dma((2, 2, chips - 1)),
            dma((2, 3, levels)),
            regular,
            regular((chips - 1,)),
            regular((levels,)),
        ]
        + [pltpu.VMEM((3, 2, n, piece, width), bf16) for n in halves]
        + [pltpu.VMEM((3, n, piece, width), bf16) for n in halves]
        + [pltpu.VMEM((3, n, piece, width), f32) for n in halves]
    )


def product_part(left, right, first, width):
    def part(chunk, row, rows):
        column = pl.multiple_of((first + chunk) * width, width)
        return jnp.dot(
            left[pl.ds(row, rows), :], right[:, pl.ds(column, width)], preferred_element_type=f32
        )

    return part


def column_sums(first, second, row, width):
    first = jnp.sum(first, axis=0, keepdims=True)
    second = jnp.sum(second, axis=0, keepdims=True)
    line = lax.broadcasted_iota(jnp.int32, (128, width), 0)
    return jnp.where(line == row, first, jnp.where(line == row + 1, second, 0.0)).T


def middle_kernel(sizes, width, *refs):
    row_left, act, grad_pre, resid, rows, average, inverse, gain, weights, attn_full = refs[:10]
    down_grad, output, grad_resid, out_left, vec_two, grad_attn = refs[10:16]
    held, held_out, part_send, part_recv, means, acc = refs[16:22]
    held_sems, out_sem, part_sems = refs[22:25]
    scratch = refs[25:]
    depth, count = row_left.shape
    hidden = act.shape[1]
    local_width = grad_attn.shape[1]
    blocks = depth // width
    other = {"tensor": 1 - lax.axis_index("tensor")}
    pairs = [(product_part(row_left, act, 0, width), hidden // width, (0,))]
    total = hidden // width

    def held_copy(b):
        row = pl.multiple_of(lax.rem(b, blocks) * width, width)
        column = pl.multiple_of(lax.div(b, blocks) * hidden, hidden)
        slot = lax.rem(b, 2)
        return pltpu.make_async_copy(
            weights.at[pl.ds(row, width), pl.ds(column, hidden)], held.at[slot], held_sems.at[slot]
        )

    def out_copy():
        source = attn_full.at[:, pl.ds(3 * local_width, local_width)]
        return pltpu.make_async_copy(source, held_out, out_sem)

    def part_copy(b):
        sems = (part_sems.at[0, b], part_sems.at[1, b])
        return remote(part_send.at[b], part_recv.at[b], sems, other)

    def at(b):
        return pl.ds(pl.multiple_of(b * width, width), width)

    def normed_hat(b):
        return (resid[:, at(b)] - average[...]) * inverse[...]

    def send_block(b, left):
        held_copy(b).wait()
        rounded = contract(left[...], held[lax.rem(b, 2)], 1, 1).astype(bf16)
        part_send[b] = rounded
        part_copy(b).start()

        @pl.when(b + 2 < 2 * blocks)
        def _():
            held_copy(b + 2).start()

        return rounded.astype(f32)

    def norm_block(b):
        rounded = send_block(b, grad_pre)
        vec_two[at(b), :] = column_sums(rounded * normed_hat(b), rounded, 2, width)

    def both(b):
        return part_send[b].astype(f32) + part_recv[b].astype(f32)

    def norm_means():
        def add(b, sums):
            part_copy(b).wait_recv()
            scaled = both(b) * gain[:, at(b)]
            first = jnp.sum(scaled, axis=1, keepdims=True)
            second = jnp.sum(scaled * normed_hat(b), axis=1, keepdims=True)
            return (sums[0] + first, sums[1] + second)

        zero = jnp.zeros((count, 1), f32)
        first, second = lax.fori_loop(0, blocks, add, (zero, zero))
        means[0] = first * (1.0 / depth)
        means[1] = second * (1.0 / depth)

    def norm_result(b):
        back = both(b) * gain[:, at(b)] - means[0] - normed_hat(b) * means[1]
        result = rows[:, at(b)].astype(f32) + inverse[...] * back
        grad_resid[:, at(b)] = result
        out_left[at(b), :] = result.T.astype(bf16)
        update = jnp.dot(result.astype(bf16), held_out[at(b), :], preferred_element_type=f32)

        @pl.when(b == 0)
        def _():
            acc[...] = update

        @pl.when(b > 0)
        def _():
            acc[...] += update

        @pl.when(b == blocks - 1)
        def _():
            grad_attn[...] = acc[...].astype(bf16)

    def output_block(b):
        part_copy(blocks + b).wait_recv()
        output[:, at(b)] = (resid[:, at(b)] + both(blocks + b)).astype(bf16)

    def during(s, first, body):
        @pl.when((s >= first) & (s < first + blocks))
        def _():
            body(s - first)

    def extra(s):
        @pl.when(s == 0)
        def _():
            held_copy(0).start()
            held_copy(1).start()
            out_copy().start()

        during(s, 1, norm_block)
        during(s, 1 + blocks, lambda b: send_block(blocks + b, act))

        @pl.when(s == blocks + 4)
        def _():
            norm_means()
            out_copy().wait()

        during(s, blocks + 6, norm_result)
        during(s, blocks + 5, output_block)

    assert 2 * blocks <= total
    reduce_loop(sizes, width, depth, pairs, [down_grad], scratch, (other,), extra)
    for b in range(2 * blocks):
        part_copy(b).wait_send()


def backward_middle(left, act, grad_pre, resid, rows, norm, weights, attn_full, sizes, width, number):
    depth, count = left.shape
    hidden = act.shape[1]
    local_width = attn_full.shape[1] // HEAD // 4 * HEAD
    piece = depth // (sizes["fsdp"] * sizes["context"])
    blocks = depth // width
    vmem = pl.BlockSpec(memory_space=pltpu.VMEM)
    far = pl.BlockSpec(memory_space=pl.ANY)
    dma = pltpu.SemaphoreType.DMA
    return pl.pallas_call(
        functools.partial(middle_kernel, sizes, width),
        out_shape=(
            jax.ShapeDtypeStruct((piece, hidden), f32),
            jax.ShapeDtypeStruct((count, depth), bf16),
            jax.ShapeDtypeStruct((count, depth), f32),
            jax.ShapeDtypeStruct((depth, count), bf16),
            jax.ShapeDtypeStruct((depth, 128), f32),
            jax.ShapeDtypeStruct((count, local_width), bf16),
        ),
        in_specs=[vmem] * 8 + [far] * 2,
        out_specs=(vmem,) * 6,
        scratch_shapes=[
            pltpu.VMEM((2, width, hidden), bf16),
            pltpu.VMEM((depth, local_width), bf16),
            pltpu.VMEM((2 * blocks, count, width), bf16),
            pltpu.VMEM((2 * blocks, count, width), bf16),
            pltpu.VMEM((2, count, 1), f32),
            pltpu.VMEM((count, local_width), f32),
            dma((2,)),
            dma,
            dma((2, 2 * blocks)),
        ]
        + reduce_scratch(sizes, width, depth),
        compiler_params=pltpu.CompilerParams(
            collective_id=number, has_side_effects=True, vmem_limit_bytes=62 * 1024 * 1024
        ),
        cost_estimate=pl.CostEstimate(
            flops=12 * depth * count * hidden,
            transcendentals=0,
            bytes_accessed=4 * depth * hidden,
        ),
        name="backward_middle",
    )(left, act, grad_pre, resid, rows, *norm, weights, attn_full)


def tail_kernel(sizes, width, reach, *refs):
    up_left, out_left, one_left, grad_pre, attn = refs[:5]
    tokens, average, inverse, gain, grad_resid, vec_two = refs[5:11]
    seg_row, seg_cols, log_sum, weights, grad_attn, qkv = refs[11:17]
    far = refs[17 : 17 + reach]
    refs = refs[17 + reach :]
    outs, tokens_grad = refs[:6], refs[6]
    query, terms, hop_recv, queries, grads, kept, held, part_send, part_recv = refs[7:16]
    vec_one, means, hop_sems, head_sems, held_sems, part_sems = refs[16:22]
    scratch = refs[22:]
    context = sizes["context"]
    place = lax.axis_index("context")
    depth, count = up_left.shape
    local_width = query.shape[1]
    heads = local_width // HEAD
    factor = HEAD ** (-0.5)
    blocks = depth // width
    lower = {"context": lax.rem(place + context - 1, context)}
    upper = {"context": lax.rem(place + 1, context)}
    other = {"tensor": 1 - lax.axis_index("tensor")}

    def vec_part(chunk, row, rows):
        both = vec_one[pl.ds(row, rows), :] + vec_two[pl.ds(row, rows), :]
        return jnp.concatenate([both] * (width // both.shape[1]), axis=1)

    def pair_part(chunk, row, rows):
        return jnp.dot(one_left[pl.ds(row, rows), :], terms[0, chunk], preferred_element_type=f32)

    pairs = [
        (product_part(up_left, grad_pre, 0, width), grad_pre.shape[1] // width, (0,)),
        (product_part(out_left, attn, 0, width), local_width // width, (1,)),
        (product_part(one_left, query, 0, width), local_width // width, (2,)),
        (pair_part, heads, (3, 4)),
        (vec_part, 1, (5,)),
    ]
    total = sum(p[1] for p in pairs)
    begin = sum(p[1] for p in pairs[:3])
    stride = 2
    gap = (begin - 2 - stride * (heads - 1)) // reach

    def head_copies(h):
        slot = lax.rem(h, 2)
        one = pl.ds(pl.multiple_of(h * HEAD, HEAD), HEAD)
        near = pl.ds(pl.multiple_of(local_width + 2 * h * HEAD, HEAD), 2 * HEAD)
        two = pl.ds(pl.multiple_of(2 * h * HEAD, HEAD), 2 * HEAD)
        sources = [(qkv.at[:, one], queries.at[slot]), (grad_attn.at[:, one], grads.at[slot])]
        sources.append((qkv.at[:, near], kept.at[slot, 0]))
        sources += [(far[i].at[:, two], kept.at[slot, i + 1]) for i in range(reach)]
        return [
            pltpu.make_async_copy(source, target, head_sems.at[slot, i])
            for i, (source, target) in enumerate(sources)
        ]

    def head_block(h):
        slot = lax.rem(h, 2)
        one = pl.ds(pl.multiple_of(h * HEAD, HEAD), HEAD)
        for copy in head_copies(h):
            copy.wait()
        own_query, own_grad = queries[slot], grads[slot]
        delta = own_grad.astype(f32) * attn[:, one].astype(f32)
        delta = jnp.sum(delta.T, axis=0, keepdims=True)
        update = None
        for index in range(reach + 1):
            key, value = kept[slot, index, :, :HEAD], kept[slot, index, :, HEAD:]
            scores = contract(key, own_query, 1, 1) * factor
            allowed = seg_cols[index] == seg_row[...]
            if index == 0:
                key_pos = lax.broadcasted_iota(jnp.int32, (count, count), 0)
                query_pos = lax.broadcasted_iota(jnp.int32, (count, count), 1)
                allowed = allowed & (key_pos <= query_pos)
            scores = jnp.where(allowed, scores, big_negative)
            probs = jnp.where(allowed, jnp.exp(scores - log_sum[h]), 0.0)
            grad_probs = contract(value, own_grad, 1, 1)
            grad_scores = (probs * (grad_probs - delta)).astype(bf16)
            key_grad = jnp.dot(grad_scores, own_query, preferred_element_type=f32) * factor
            value_grad = jnp.dot(probs.astype(bf16), own_grad, preferred_element_type=f32)
            terms[index, h, :, :HEAD] = key_grad.astype(bf16)
            terms[index, h, :, HEAD:] = value_grad.astype(bf16)
            change = contract(key, grad_scores, 0, 0)
            update = change if update is None else update + change
        query[:, one] = (update * factor).T.astype(bf16)

        @pl.when(h + 2 < heads)
        def _():
            for copy in head_copies(h + 2):
                copy.start()

    def hop_copy(j, h):
        sems = (hop_sems.at[0, j, h], hop_sems.at[1, j, h])
        return remote(terms.at[reach - j, h], hop_recv.at[j, h], sems, lower)

    def hop(j, h):
        if j == 0:
            head_block(h)
        else:

            @pl.when(place < context - 1)
            def _():
                hop_copy(j - 1, h).wait_recv()
                both = terms[reach - j, h].astype(f32) + hop_recv[j - 1, h].astype(f32)
                terms[reach - j, h] = both.astype(bf16)

        if j < reach:

            @pl.when(place > 0)
            def _():
                hop_copy(j, h).start()

    def held_copy(b):
        slot = lax.rem(b, 2)
        row = pl.multiple_of(b * width, width)
        return pltpu.make_async_copy(
            weights.at[pl.ds(row, width), pl.ds(0, 3 * local_width)],
            held.at[slot],
            held_sems.at[slot],
        )

    def part_copy(b):
        sems = (part_sems.at[0, b], part_sems.at[1, b])
        return remote(part_send.at[b], part_recv.at[b], sems, other)

    def normed_hat(b):
        columns = pl.ds(pl.multiple_of(b * width, width), width)
        return (tokens[:, columns].astype(f32) - average[...]) * inverse[...]

    def input_block(b):
        slot = lax.rem(b, 2)
        held_copy(b).wait()
        value = contract(query[...], held[slot, :, :local_width], 1, 1)
        for h in range(heads):
            first = local_width + 2 * h * HEAD
            value = value + contract(terms[0, h], held[slot, :, first : first + 2 * HEAD], 1, 1)
        rounded = value.astype(bf16)
        part_send[b] = rounded
        part_copy(b).start()

        @pl.when(b + 2 < blocks)
        def _():
            held_copy(b + 2).start()

        rounded = rounded.astype(f32)
        vec_one[pl.ds(pl.multiple_of(b * width, width), width), :] = column_sums(
            rounded * normed_hat(b), rounded, 0, width
        )

    def scaled_block(b):
        columns = pl.ds(pl.multiple_of(b * width, width), width)
        value = part_send[b].astype(f32) + part_recv[b].astype(f32)
        return value * gain[:, columns]

    def norm_means():
        def add(b, sums):
            part_copy(b).wait_recv()
            scaled = scaled_block(b)
            first = jnp.sum(scaled, axis=1, keepdims=True)
            second = jnp.sum(scaled * normed_hat(b), axis=1, keepdims=True)
            return (sums[0] + first, sums[1] + second)

        zero = jnp.zeros((count, 1), f32)
        first, second = lax.fori_loop(0, blocks, add, (zero, zero))
        means[0] = first * (1.0 / depth)
        means[1] = second * (1.0 / depth)

    def norm_result():
        def write(b, c):
            columns = pl.ds(pl.multiple_of(b * width, width), width)
            back = scaled_block(b) - means[0] - normed_hat(b) * means[1]
            tokens_grad[:, columns] = (
                grad_resid[:, columns] + inverse[...] * back
            ).astype(bf16)
            return c

        lax.fori_loop(0, blocks, write, 0)

    def extra(s):
        @pl.when(s == 0)
        def _():
            for h in range(min(2, heads)):
                for copy in head_copies(h):
                    copy.start()

        for j in range(reach + 1):
            first = 1 + j * gap

            @pl.when(
                (s >= first)
                & (s < first + stride * heads)
                & (lax.rem(s + stride - first % stride, stride) == 0)
            )
            def _(j=j, first=first):
                hop(j, lax.div(s - first, stride))

        @pl.when(s == begin - 2)
        def _():
            held_copy(0).start()
            held_copy(1).start()

        @pl.when((s >= begin) & (s < begin + blocks))
        def _():
            input_block(s - begin)

        @pl.when(s == total + 1)
        def _():
            norm_means()

        @pl.when(s == total + 2)
        def _():
            norm_result()

    assert begin + blocks < total and width == 2 * HEAD and gap > 0
    reduce_loop(sizes, width, depth, pairs, outs, scratch, (other, lower, upper), extra)

    @pl.when(place > 0)
    def _():
        for j in range(reach):
            for h in range(heads):
                hop_copy(j, h).wait_send()

    for b in range(blocks):
        part_copy(b).wait_send()


def backward_tail(
    lefts, grad_pre, attn, norm, grad_resid, vec_two, masks, weights, pieces, sizes, width, number
):
    depth, count = lefts[0].shape
    local_width = attn.shape[1]
    heads = local_width // HEAD
    hidden = grad_pre.shape[1]
    reach = len(pieces) - 2
    piece = depth // (sizes["fsdp"] * sizes["context"])
    blocks = depth // width
    vmem = pl.BlockSpec(memory_space=pltpu.VMEM)
    dma = pltpu.SemaphoreType.DMA
    columns = (hidden, local_width, local_width, local_width, local_width, width)
    near = [*lefts, grad_pre, attn, *norm, grad_resid, vec_two, *masks]
    far = [weights, *pieces]
    return pl.pallas_call(
        functools.partial(tail_kernel, sizes, width, reach),
        out_shape=tuple(jax.ShapeDtypeStruct((piece, n), f32) for n in columns)
        + (jax.ShapeDtypeStruct((count, depth), bf16),),
        in_specs=[vmem] * len(near) + [pl.BlockSpec(memory_space=pl.ANY)] * len(far),
        out_specs=(vmem,) * 7,
        scratch_shapes=[
            pltpu.VMEM((count, local_width), bf16),
            pltpu.VMEM((reach + 1, heads, count, 2 * HEAD), bf16),
            pltpu.VMEM((reach, heads, count, 2 * HEAD), bf16),
            pltpu.VMEM((2, count, HEAD), bf16),
            pltpu.VMEM((2, count, HEAD), bf16),
            pltpu.VMEM((2, reach + 1, count, 2 * HEAD), bf16),
            pltpu.VMEM((2, width, 3 * local_width), bf16),
            pltpu.VMEM((blocks, count, width), bf16),
            pltpu.VMEM((blocks, count, width), bf16),
            pltpu.VMEM((depth, 128), f32),
            pltpu.VMEM((2, count, 1), f32),
            dma((2, reach, heads)),
            dma((2, reach + 3)),
            dma((2,)),
            dma((2, blocks)),
        ]
        + reduce_scratch(sizes, width, depth),
        compiler_params=pltpu.CompilerParams(
            collective_id=number, has_side_effects=True, vmem_limit_bytes=63 * 1024 * 1024
        ),
        cost_estimate=pl.CostEstimate(
            flops=8 * depth * count * (hidden + 4 * local_width),
            transcendentals=0,
            bytes_accessed=16 * depth * count,
        ),
        name="backward_tail",
    )(*near, *far)


def per_device(
    sizes,
    tokens,
    segments,
    query_weight,
    key_weight,
    value_weight,
    out_weight,
    up_weight,
    down_weight,
    attn_gain,
    attn_bias,
    mlp_gain,
    mlp_bias,
    cotangent,
):
    seq_dev, group_len, model_width = tokens.shape
    assert seq_dev == 1
    shard_rows, local_width = query_weight.shape
    hidden_local = up_weight.shape[1]
    heads = local_width // HEAD
    seq_len = segments.shape[1]
    context, tensor = sizes["context"], sizes["tensor"]
    place = lax.axis_index("context")
    weight_axes = ("fsdp", "context")

    assert tensor == 2
    reach = min(context - 1, -(-(seq_len // 2 - 1) // group_len))
    half_len = group_len // 2
    side = lax.axis_index("tensor")
    piece = lax.dynamic_slice_in_dim(
        tokens.reshape(group_len, model_width), side * half_len, half_len, 0
    )
    far_tokens = []
    for _ in range(reach):
        piece = line_move(piece, "context", context, 1)
        other = swap(piece, "tensor", tensor)
        far_tokens.append(
            jnp.where(side == 0, jnp.stack([piece, other]), jnp.stack([other, piece])).reshape(
                group_len, model_width
            )
        )

    vectors = jnp.stack([attn_gain, attn_bias, mlp_gain, mlp_bias], axis=1)
    vectors = jnp.pad(vectors, ((0, 0), (0, HEAD - 4)))
    pair_weight = jnp.stack(
        [w.reshape(shard_rows, heads, HEAD) for w in (key_weight, value_weight)], axis=2
    ).reshape(shard_rows, 2 * local_width)
    attn_full = lax.all_gather(
        jnp.concatenate([query_weight, pair_weight, out_weight, vectors], axis=1),
        weight_axes,
        axis=0,
        tiled=True,
    )
    mlp_full = lax.all_gather(
        jnp.concatenate([up_weight, down_weight], axis=1), weight_axes, axis=0, tiled=True
    )
    full_qkv = attn_full[:, : 3 * local_width]
    full_out = attn_full[:, 3 * local_width : 4 * local_width]
    vecs = attn_full[:, 4 * local_width : 4 * local_width + 4].T.astype(f32)
    gain_one, bias_one, gain_two, bias_two = vecs[0], vecs[1], vecs[2], vecs[3]
    full_up = mlp_full[:, :hidden_local]
    full_down = mlp_full[:, hidden_local:]

    rows_in = tokens.reshape(group_len, model_width).astype(f32)
    hat_one, inv_one = norm_stats(rows_in)
    mean_one = jnp.mean(rows_in, axis=-1, keepdims=True)
    normed_one = (hat_one * gain_one + bias_one).astype(bf16)
    qkv = jnp.dot(normed_one, full_qkv, preferred_element_type=f32).astype(bf16)

    far = []
    for block in far_tokens:
        far_hat, _ = norm_stats(block.astype(f32))
        far_normed = (far_hat * gain_one + bias_one).astype(bf16)
        far.append(
            jnp.dot(
                far_normed, full_qkv[:, local_width:], preferred_element_type=f32
            ).astype(bf16)
        )
    first = place * group_len
    seg_row = lax.dynamic_slice_in_dim(segments, first, group_len, 1)
    seg_cols = [seg_row]
    for back in range(1, reach + 1):
        start = jnp.maximum(first - back * group_len, 0)
        block = lax.dynamic_slice_in_dim(segments, start, group_len, 1)
        seg_cols.append(jnp.where(place >= back, block, -1))
    flags = jnp.stack([(cols[0, -1] == seg_row[0, 0]).astype(jnp.int32) for cols in seg_cols[1:]])
    seg_cols = jnp.concatenate(seg_cols, axis=0)[:, :, None]

    attn, log_sum = attention_forward(flags, seg_row, seg_cols, qkv, far, heads)
    branch = contract(attn, full_out, 1, 1).astype(bf16)
    residual = rows_in + (branch.astype(f32) + tensor_other(branch, tensor).astype(f32))

    hat_two, inv_two = norm_stats(residual)
    normed_two = (hat_two * gain_two + bias_two).astype(bf16)
    row_left, up_left, one_left = lax.optimization_barrier(
        (cotangent.reshape(group_len, model_width).T, normed_two.T, normed_one.T)
    )
    pre_act = jnp.dot(
        after(normed_two, row_left, up_left, one_left), full_up, preferred_element_type=f32
    )
    normal_cdf = 0.5 * (1.0 + lax.erf(pre_act * half_root))
    activated = (pre_act * normal_cdf).astype(bf16)
    slope = normal_cdf + pre_act * density * jnp.exp(-0.5 * pre_act * pre_act)
    grad_rows = cotangent.reshape(group_len, model_width)
    grad_act = jnp.dot(grad_rows, full_down, preferred_element_type=f32)
    grad_pre = (grad_act * slope).astype(bf16)
    mean_two = jnp.mean(residual, axis=-1, keepdims=True)
    down_grad, output, grad_resid, out_left, vec_two, grad_attn = backward_middle(
        row_left,
        activated,
        grad_pre,
        residual,
        grad_rows,
        (mean_two, inv_two, gain_two[None]),
        mlp_full,
        attn_full,
        sizes,
        WIDTH,
        1,
    )
    output = output.reshape(tokens.shape)
    up_grad, out_grad, query_grad, key_grad, value_grad, vector_part, tokens_grad = backward_tail(
        (up_left, out_left, one_left),
        grad_pre,
        attn,
        (tokens.reshape(group_len, model_width), mean_one, inv_one, gain_one[None]),
        grad_resid,
        vec_two,
        (seg_row, seg_cols, log_sum),
        attn_full,
        (grad_attn, qkv, *far),
        sizes,
        WIDTH,
        2,
    )
    tokens_grad = tokens_grad.reshape(tokens.shape)
    vector_part = vector_part[:, :8]
    vector_grads = (vector_part + tensor_other(vector_part, tensor)).T
    return (
        output,
        tokens_grad,
        query_grad,
        key_grad,
        value_grad,
        out_grad,
        up_grad,
        down_grad,
        vector_grads[0],
        vector_grads[1],
        vector_grads[2],
        vector_grads[3],
    )


def solution(mesh):
    weight = P(("fsdp", "context"), "tensor")
    vector = P(("fsdp", "context"))
    rows = P("fsdp", "context", None)
    return jax.shard_map(
        functools.partial(per_device, dict(mesh.shape)),
        mesh=mesh,
        in_specs=(rows, P("fsdp", None)) + (weight,) * 6 + (vector,) * 4 + (rows,),
        out_specs=(rows, rows) + (weight,) * 6 + (vector,) * 4,
        check_vma=False,
    )
```
